32 devices in a mesh: gx: 4 (over z), gy: 8 (over y, x, core).
Axes of the slice: x: 2, y: 2, z: 4, core: 2. Of those that a mesh axis runs over, the one named last changes fastest.
Arguments:
- flow: float32 [19, 32, 64, 512], P(None, 'gx', 'gy'), may hold values from 0.0116 to 0.467, as said below
- field: float32 [7, 32, 64, 512], P(None, 'gx', 'gy'), may hold values from -0.45 to 0.45, as said below
- adj_flow_in: float32 [19, 32, 64, 512], P(None, 'gx', 'gy'), may hold values from -6 to 6
- adj_field_in: float32 [7, 32, 64, 512], P(None, 'gx', 'gy'), may hold values from -6 to 6
- profile: float32 [32, 64, 512], P('gx', 'gy'), may hold values from 0.5 to 1.5
- strengths: float32 [32], replicated, may hold values from 0.5 to 2
- wall: int32 [32, 64, 512], P('gx', 'gy'), may hold values 0 or 1
- magnet: int32 [32, 64, 512], P('gx', 'gy'), may hold values from 0 to 31
Outputs:
- new_flow: float32 [19, 32, 64, 512], P(None, 'gx', 'gy')
- new_field: float32 [7, 32, 64, 512], P(None, 'gx', 'gy')
- adj_flow: float32 [19, 32, 64, 512], P(None, 'gx', 'gy')
- adj_field: float32 [7, 32, 64, 512], P(None, 'gx', 'gy')
- magnet_grad: float32 [32], replicated
The draws below stay inside these ranges and needn't reach their ends.
Inputs may be any that keep to these rules, and one draw needn't show every extreme that they name: flow populations are positive, near w_i times a density of order one. field populations are v_k times a local field value plus noise.
All inputs are finite; a program needn't handle non-finite values. No bound on the sum of `wall` on one device may be relied on, other than what follows from the above.
Results may differ from the reference program's by a relative error of at most 0.00023.
Values sent between devices are 32-bit elements; how exact they have to be, the bound alone decides.
No kernel may reach another device: no remote copies, remote signals or barrier semaphores. Data moves between devices by JAX's collectives and lax.ppermute only.
A program may use at most 64 MiB of HBM per device.

```python
import math
import jax
import jax.numpy as jnp
import numpy as np
from jax import lax

NZ = 512
NMAG = 32
NX = 32
NY = 64


def draw_flow(key, part):
    weights = jnp.asarray(np.array([1.0 / 3.0] + [1.0 / 18.0] * 6 + [1.0 / 36.0] * 12), jnp.float32).reshape(19, 1, 1, 1)
    velx = jnp.asarray(np.array([0, 1, -1, 0, 0, 0, 0, 1, -1, 1, -1, 1, -1, 1, -1, 0, 0, 0, 0]), jnp.float32).reshape(19, 1, 1, 1)
    noise = jax.random.uniform(key, (19, NX, NY, NZ), jnp.float32, 0.6, 1.4)
    return weights * (1.0 + 0.3 * velx) * noise


def draw_field(key, part):
    weights = jnp.asarray(np.array([0.25] + [0.125] * 6), jnp.float32).reshape(7, 1, 1, 1)
    first = jax.random.fold_in(key, 11)
    second = jax.random.fold_in(key, 12)
    level = jax.random.uniform(first, (1, NX, NY, NZ), jnp.float32, -1.5, 1.5)
    noise = jax.random.uniform(second, (7, NX, NY, NZ), jnp.float32, -0.3, 0.3)
    return weights * (level + noise)


def set_ends(drawn, rng, least, high):
    shape = drawn.shape
    spot = [jax.random.randint(jax.random.fold_in(rng, axis), (), 0, shape[axis]) for axis in range(len(shape))]
    drawn = drawn.at[tuple(spot)].set(least)
    longest = shape.index(max(shape))
    spot[longest] = (spot[longest] + 1) % shape[longest]
    return drawn.at[tuple(spot)].set(high)


def level_of(key, extent, split, smallest, high):
    factor_of, own = 1.0, jax.random.fold_in(key, 6)
    for axis_at, shards_of in split:
        steps = jnp.exp(jax.random.uniform(jax.random.fold_in(own, axis_at), (shards_of,), jnp.float32, smallest / len(split), high / len(split)))
        factor_of = factor_of * jnp.repeat(steps, extent[axis_at] // shards_of).reshape([-1 if axis == axis_at else 1 for axis in range(len(extent))])
    return factor_of


def scatter_about(stream_key, extent, width, most, split=(), kind=jnp.bfloat16):
    result = jax.random.normal(stream_key, extent, jnp.float32) * width
    if len(split) > 0:
        result = level_of(stream_key, extent, split, -0.22, 0.18) * result
    return jnp.clip(result, min=-most, max=most).astype(kind)


def setup_inputs(seed: int = 0) -> dict:
    keys = jax.random.split(jax.random.key(seed), 9)
    return {
        "flow": draw_flow(jax.random.fold_in(keys[8], 71), 0),
        "field": draw_field(jax.random.fold_in(keys[8], 71), 0),
        "adj_flow_in": scatter_about(keys[2], (19, NX, NY, NZ), 1.0, 6.0, ((1, 4), (2, 8)), jnp.float32),
        "adj_field_in": scatter_about(keys[3], (7, NX, NY, NZ), 1.0, 6.0, ((1, 4), (2, 8)), jnp.float32),
        "profile": jnp.clip(0.5 + 1.0 * jax.random.uniform(keys[4], (NX, NY, NZ), jnp.float32) ** level_of(keys[4], (NX, NY, NZ), ((0, 4), (1, 8)), -0.2, 0.2), 0.5, 1.5),
        "strengths": jnp.clip(jnp.exp(jax.random.uniform(keys[5], (NMAG,), jnp.float32, math.log(0.5), math.log(2.0))), 0.5, 2.0),
        "wall": set_ends((jax.random.randint(keys[6], (NX, NY, NZ), 0, 8) < 1).astype(jnp.int32), jax.random.fold_in(keys[6], 1), 0, 1),
        "magnet": set_ends(jax.random.randint(keys[7], (NX, NY, NZ), 0, NMAG), jax.random.fold_in(keys[7], 1), 0, NMAG - 1).astype(jnp.int32),
    }


LATTICE = np.array([[0, 0, 0], [1, 0, 0], [-1, 0, 0], [0, 1, 0], [0, -1, 0], [0, 0, 1], [0, 0, -1], [1, 1, 0], [-1, -1, 0], [1, -1, 0], [-1, 1, 0], [1, 0, 1], [-1, 0, -1], [1, 0, -1], [-1, 0, 1], [0, 1, 1], [0, -1, -1], [0, 1, -1], [0, -1, 1]])
OPPOSITE = [0, 2, 1, 4, 3, 6, 5, 8, 7, 10, 9, 12, 11, 14, 13, 16, 15, 18, 17]
WEIGHTS_FLOW = [1.0 / 3.0] + [1.0 / 18.0] * 6 + [1.0 / 36.0] * 12
WEIGHTS_FIELD = [0.25] + [0.125] * 6
OMEGA_PLUS = 1.25
OMEGA_MINUS = 1.0 / 1.125
TAU_PLUS = 0.8
COUPLE = 2.0
SOURCE = 2.0

def column(values, ndim):
    return jnp.array([float(v) for v in values], jnp.float32).reshape((len(values),) + (1,) * (ndim - 1))

def collide(flow, field, bfield, fluid):
    ndim = flow.ndim
    velx = column(LATTICE[:, 0], ndim)
    vely = column(LATTICE[:, 1], ndim)
    velz = column(LATTICE[:, 2], ndim)
    weight = column(WEIGHTS_FLOW, ndim)
    weight_b = column(WEIGHTS_FIELD, ndim)
    rho = lax.optimization_barrier(jnp.sum(flow, 0)) + (1.0 - fluid)
    momx = lax.optimization_barrier(jnp.sum(velx * flow, 0))
    momy = lax.optimization_barrier(jnp.sum(vely * flow, 0))
    momz = lax.optimization_barrier(jnp.sum(velz * flow, 0))
    speed_x = momx / rho
    speed_y = momy / rho
    speed_z = momz / rho
    bvalue = lax.optimization_barrier(jnp.sum(field, 0))
    current = lax.optimization_barrier(jnp.sum(vely[:7] * field, 0)) - bvalue * speed_y
    shear = lax.optimization_barrier(jnp.sum(velx * vely * flow, 0)) - momx * speed_y
    force = COUPLE * bfield * current
    shifted = speed_x + TAU_PLUS * force / rho
    along = velx * shifted + vely * speed_y + velz * speed_z
    square = shifted * shifted + speed_y * speed_y + speed_z * speed_z
    equil = weight * rho * (1.0 + 3.0 * along + 4.5 * along * along - 1.5 * square)
    offset = flow - equil
    flipped = jnp.stack([offset[k] for k in OPPOSITE], 0)
    post_flow = flow - 0.5 * OMEGA_PLUS * (offset + flipped) - 0.5 * OMEGA_MINUS * (offset - flipped)
    along_b = velx[:7] * speed_x + vely[:7] * speed_y + velz[:7] * speed_z
    post_field = weight_b * bvalue * (1.0 + 4.0 * along_b) + weight_b * SOURCE * bfield * shear
    return (post_flow, post_field)

def pull_stream(pad_pops, pad_fluid, post, fluid, count):
    size_x, size_y, size_z = fluid.shape
    parts = []
    for i in range(count):
        cx, cy, cz = (int(v) for v in LATTICE[i])
        near = pad_fluid[1 - cx:1 - cx + size_x, 1 - cy:1 - cy + size_y, 1 - cz:1 - cz + size_z]
        moved = pad_pops[i, 1 - cx:1 - cx + size_x, 1 - cy:1 - cy + size_y, 1 - cz:1 - cz + size_z]
        parts.append(fluid * (near * moved + (1.0 - near) * post[OPPOSITE[i]]))
    return jnp.stack(parts, 0)

def push_adjoint(pad_pops, pad_fluid, local, fluid, count):
    size_x, size_y, size_z = fluid.shape
    parts = []
    for i in range(count):
        cx, cy, cz = (int(v) for v in LATTICE[i])
        near = pad_fluid[1 + cx:1 + cx + size_x, 1 + cy:1 + cy + size_y, 1 + cz:1 + cz + size_z]
        moved = pad_pops[i, 1 + cx:1 + cx + size_x, 1 + cy:1 + cy + size_y, 1 + cz:1 + cz + size_z]
        parts.append(fluid * (near * moved + (1.0 - near) * local[OPPOSITE[i]]))
    return jnp.stack(parts, 0)

def pad_grid(stack):
    wrapped = jnp.concatenate([stack[:, -1:], stack, stack[:, :1]], 1)
    return jnp.pad(wrapped, ((0, 0), (0, 0), (1, 1), (1, 1)))

def reference(flow, field, adj_flow_in, adj_field_in, profile, strengths, wall, magnet):
    fluid = (1 - wall).astype(jnp.float32)
    bcell = strengths[magnet] * profile

    def plane_collide(items):
        return collide(items[0], items[1], items[2], items[3])
    post_flow, post_field = lax.map(plane_collide, (jnp.moveaxis(flow, 1, 0), jnp.moveaxis(field, 1, 0), bcell, fluid))
    post_flow = jnp.moveaxis(post_flow, 0, 1)
    post_field = jnp.moveaxis(post_field, 0, 1)
    padded = pad_grid(jnp.concatenate([post_flow, post_field, fluid[None]], 0))
    pad_fluid = padded[26]
    new_flow = pull_stream(padded[:19], pad_fluid, post_flow, fluid, 19)
    new_field = pull_stream(padded[19:26], pad_fluid, post_field, fluid, 7)
    pad_adj = pad_grid(jnp.concatenate([adj_flow_in, adj_field_in], 0))
    ast_flow = push_adjoint(pad_adj[:19], pad_fluid, adj_flow_in, fluid, 19)
    ast_field = push_adjoint(pad_adj[19:], pad_fluid, adj_field_in, fluid, 7)

    def plane_adjoint(items):
        mask = items[3]
        _, pullback = jax.vjp(lambda a, b, c: collide(a, b, c, mask), items[0], items[1], items[2])
        return pullback((items[4], items[5]))
    adj_flow, adj_field, dcell = lax.map(plane_adjoint, (jnp.moveaxis(new_flow, 1, 0), jnp.moveaxis(new_field, 1, 0), bcell, fluid, jnp.moveaxis(ast_flow, 1, 0), jnp.moveaxis(ast_field, 1, 0)))
    adj_flow = jnp.moveaxis(adj_flow, 0, 1)
    adj_field = jnp.moveaxis(adj_field, 0, 1)
    sums = jax.ops.segment_sum((dcell * profile).reshape(-1), magnet.reshape(-1).astype(jnp.int32), NMAG)
    magnet_grad = sums / math.sqrt(NX * NY * NZ / NMAG)
    return (new_flow, new_field, adj_flow, adj_field, magnet_grad)
```

```python
import functools
import math

import jax
import jax.numpy as jnp
from jax import lax
from jax.experimental import pallas as pl
from jax.experimental.pallas import tpu as pltpu
from jax.sharding import PartitionSpec as P

LATTICE = [
    (0, 0, 0),
    (1, 0, 0),
    (-1, 0, 0),
    (0, 1, 0),
    (0, -1, 0),
    (0, 0, 1),
    (0, 0, -1),
    (1, 1, 0),
    (-1, -1, 0),
    (1, -1, 0),
    (-1, 1, 0),
    (1, 0, 1),
    (-1, 0, -1),
    (1, 0, -1),
    (-1, 0, 1),
    (0, 1, 1),
    (0, -1, -1),
    (0, 1, -1),
    (0, -1, 1),
]
NF, NG = 19, 7
NP = NF + NG
FIRST = [1, 3, 5, 7, 9, 11, 13, 15, 17]
W0, W1, W2 = 1.0 / 3.0, 1.0 / 18.0, 1.0 / 36.0
V0, V1 = 0.25, 0.125
PLUS = 0.625
MINUS = 0.5 / 1.125
TAU_PLUS = 0.8
COUPLE = 2.0
SOURCE = 2.0

UP = [3, 7, 10, 15, 17, NF + 3]
DOWN = [4, 8, 9, 16, 18, NF + 4]
RIGHT = [1, 7, 9, 11, 13, NF + 1]
LEFT = [2, 8, 10, 12, 14, NF + 2]
SLOTS = 13
MASK = 12


def weight(i):
    return W1 if i <= 6 else W2


def gather_strength(table, magnet):
    parts = [
        jnp.take_along_axis(table, magnet[:, z : z + 128], axis=1, mode="promise_in_bounds")
        for z in range(0, magnet.shape[1], 128)
    ]
    return jnp.concatenate(parts, axis=1)


def lane_table(strengths_ref):
    row = strengths_ref[...]
    rest = 128 - row.shape[1]
    if rest:
        row = jnp.concatenate([row, jnp.zeros((1, rest), jnp.float32)], axis=1)
    return jnp.broadcast_to(row, (8, 128))


def vector_sums(pair):
    x = pair[1] + pair[7] + pair[9] + pair[11] + pair[13]
    y = pair[3] + pair[7] - pair[9] + pair[15] + pair[17]
    z = pair[5] + pair[11] - pair[13] + pair[15] - pair[17]
    return x, y, z


def along(i, vx, vy, vz):
    out = None
    for c, v in zip(LATTICE[i], (vx, vy, vz)):
        if c:
            if out is None:
                out = v if c > 0 else -v
            else:
                out = out + v if c > 0 else out - v
    return out


def collide_kernel(
    planes,
    flow_ref,
    field_ref,
    adjf_ref,
    adjg_ref,
    profile_ref,
    strengths_ref,
    wall_ref,
    magnet_ref,
    post_ref,
    first_ref,
    second_ref,
    right_ref,
    left_ref,
):
    step = pl.program_id(0)
    steps = pl.num_programs(0)
    odd = lax.rem(lax.axis_index("gy"), 2)
    table = lane_table(strengths_ref)
    last = flow_ref.shape[2] - 1

    for p in range(planes):
        fluid = 1.0 - wall_ref[p].astype(jnp.float32)
        bcell = gather_strength(table, magnet_ref[p]) * profile_ref[p]
        f = [flow_ref[i, p] for i in range(NF)]
        g = [field_ref[k, p] for k in range(NG)]
        even = {i: f[i] + f[i + 1] for i in FIRST}
        diff = {i: f[i] - f[i + 1] for i in FIRST}
        rho = f[0] + (1.0 - fluid)
        for i in FIRST:
            rho = rho + even[i]
        momx, momy, momz = vector_sums(diff)
        inv = 1.0 / rho
        ux, uy, uz = momx * inv, momy * inv, momz * inv
        bval = g[0] + g[1] + g[2] + g[3] + g[4] + g[5] + g[6]
        current = (g[3] - g[4]) - bval * uy
        shear = (even[7] - even[9]) - momx * uy
        force = (COUPLE * bcell) * current
        vx = ux + TAU_PLUS * force * inv
        base = 1.0 - 1.5 * (vx * vx + uy * uy + uz * uz)
        post_ref[0, p] = f[0] - 2.0 * PLUS * (f[0] - (W0 * rho) * base)
        rho1, rho2 = W1 * rho, W2 * rho
        for i in FIRST:
            wr = rho1 if i <= 6 else rho2
            a = along(i, vx, uy, uz)
            ne = even[i] - (2.0 * wr) * (base + 4.5 * a * a)
            no = diff[i] - (6.0 * wr) * a
            ne = PLUS * ne
            no = MINUS * no
            post_ref[i, p] = f[i] - ne - no
            post_ref[i + 1, p] = f[i + 1] - ne + no
        common = bval + (SOURCE * bcell) * shear
        slope = 4.0 * bval
        post_ref[NF, p] = V0 * common
        for k, u in ((1, ux), (3, uy), (5, uz)):
            su = slope * u
            post_ref[NF + k, p] = V1 * (common + su)
            post_ref[NF + k + 1, p] = V1 * (common - su)

        x = step * planes + p
        here = pl.ds(x, 1)

        def adj_row(i, row):
            return adjf_ref[i, p, pl.ds(row, 1), :]

        for out, side in ((first_ref, odd), (second_ref, 1 - odd)):
            row = (1 - side) * last
            for s in range(6):
                up, down = UP[s], DOWN[s]
                out[s, here, :] = post_ref[up + side * (down - up), p, pl.ds(row, 1), :]
                if up < NF:
                    line = adjf_ref[down + side * (up - down), p, pl.ds(row, 1), :]
                else:
                    line = adjg_ref[down - NF + side * (up - down), p, pl.ds(row, 1), :]
                out[6 + s, here, :] = line
            out[MASK, here, :] = 1.0 - wall_ref[p, pl.ds(row, 1), :].astype(jnp.float32)

    def pack_x(out, p, posts, adjs):
        for s in range(6):
            out[s] = post_ref[posts[s], p]
            j = adjs[s]
            out[6 + s] = adjf_ref[j, p] if j < NF else adjg_ref[j - NF, p]
        out[MASK] = 1.0 - wall_ref[p].astype(jnp.float32)

    @pl.when(step == 0)
    def _():
        pack_x(left_ref, 0, LEFT, RIGHT)

    @pl.when(step == steps - 1)
    def _():
        pack_x(right_ref, planes - 1, RIGHT, LEFT)


def collide_call(flow, field, adjf, adjg, profile, strengths, wall, magnet, planes=2):
    sx, sy, sz = profile.shape
    grid = sx // planes

    def stack(n):
        return pl.BlockSpec((n, planes, sy, sz), lambda x: (0, x, 0, 0))

    one = pl.BlockSpec((planes, sy, sz), lambda x: (x, 0, 0))

    def whole(*shape):
        return pl.BlockSpec(shape, lambda x: (0,) * len(shape))

    rows = jax.ShapeDtypeStruct((SLOTS, sx, sz), jnp.float32)
    faces = jax.ShapeDtypeStruct((SLOTS, sy, sz), jnp.float32)
    return pl.pallas_call(
        functools.partial(collide_kernel, planes),
        grid=(grid,),
        in_specs=[
            stack(NF),
            stack(NG),
            stack(NF),
            stack(NG),
            one,
            whole(*strengths.shape),
            one,
            one,
        ],
        out_specs=[
            stack(NP),
            whole(*rows.shape),
            whole(*rows.shape),
            whole(*faces.shape),
            whole(*faces.shape),
        ],
        out_shape=[
            jax.ShapeDtypeStruct((NP, sx, sy, sz), jnp.float32),
            rows,
            rows,
            faces,
            faces,
        ],
        compiler_params=pltpu.CompilerParams(vmem_limit_bytes=40 << 20),
        name="collide",
    )(flow, field, adjf, adjg, profile, strengths, wall, magnet)


CORNER_RIGHT = ((0, 7, 0, 8), (1, 9, 1, 10))
CORNER_LEFT = ((0, 10, 0, 9), (1, 8, 1, 7))


def corner_slots(side, post, adj):
    posts, adjs = (UP, DOWN) if side == 0 else (DOWN, UP)
    return posts.index(post), 6 + adjs.index(adj), MASK


def corner_kernel(first_ref, second_ref, right_ref, left_ref):
    odd = lax.rem(lax.axis_index("gy"), 2) == 1
    sx = first_ref.shape[1]

    def row(side, slot, x):
        a, b = first_ref[slot, x : x + 1, :], second_ref[slot, x : x + 1, :]
        return jnp.where(odd, a, b) if side == 0 else jnp.where(odd, b, a)

    for out, table, x in ((right_ref, CORNER_RIGHT, sx - 1), (left_ref, CORNER_LEFT, 0)):
        out[...] = jnp.zeros_like(out)
        for side, post, _, adj in table:
            for n, slot in enumerate(corner_slots(side, post, adj)):
                out[2 * n + side : 2 * n + side + 1, :] = row(side, slot, x)


def corner_call(first, second):
    sz = first.shape[2]
    out = jax.ShapeDtypeStruct((8, sz), jnp.float32)
    return pl.pallas_call(corner_kernel, out_shape=[out, out], name="corners")(first, second)


def plane_step(
    x_index, post, post_row, adj, adj_row, mask, mask_row, fluid, bcell, profile, magnet,
    near_ref, new_ref, out_ref, sums_ref, count,
):
    sy, sz = fluid.shape
    yi = lax.broadcasted_iota(jnp.int32, (sy, sz), 0)
    zi = lax.broadcasted_iota(jnp.int32, (sy, sz), 1)
    top, bottom = yi == sy - 1, yi == 0
    zlast, zfirst = zi == sz - 1, zi == 0

    def shift(value, row, dy, dz):
        if dy == -1:
            value = jnp.where(bottom, row(), pltpu.roll(value, 1, 0))
        elif dy == 1:
            value = jnp.where(top, row(), pltpu.roll(value, sy - 1, 0))
        if dz == -1:
            value = pltpu.roll(value, 1, 1)
        elif dz == 1:
            value = pltpu.roll(value, sz - 1, 1)
        return value

    def moved(get, get_row, i, sign):
        dx, dy, dz = (sign * c for c in LATTICE[i if i < NF else i - NF])
        return shift(get(i, dx), lambda: get_row(i, dx, dy), dy, dz)

    def near_of(i, sign):
        dx, dy, dz = (sign * c for c in LATTICE[i])
        value = shift(mask(dx), lambda: mask_row(dx, dy), dy, dz)
        if dz == -1:
            value = jnp.where(zfirst, 0.0, value)
        elif dz == 1:
            value = jnp.where(zlast, 0.0, value)
        return value

    for n, i in enumerate(FIRST):
        near_ref[2 * n] = near_of(i, -1)
        near_ref[2 * n + 1] = near_of(i, 1)

    def near(n):
        return near_ref[2 * n] > 0.5, near_ref[2 * n + 1] > 0.5

    def pull(i, n):
        minus, plus = near(n)
        a = fluid * jnp.where(minus, moved(post, post_row, i, -1), post(i + 1, 0))
        b = fluid * jnp.where(plus, moved(post, post_row, i + 1, -1), post(i, 0))
        new_ref[i, x_index] = a
        new_ref[i + 1, x_index] = b
        return a, b

    f0 = fluid * post(0, 0)
    new_ref[0, x_index] = f0
    rho = f0 + (1.0 - fluid)
    momx = momy = momz = shear0 = 0.0
    for n, i in enumerate(FIRST):
        a, b = pull(i, n)
        s, d = a + b, a - b
        rho = rho + s
        cx, cy, cz = LATTICE[i]
        if cx:
            momx = momx + d
        if cy:
            momy = momy + d if cy > 0 else momy - d
        if cz:
            momz = momz + d if cz > 0 else momz - d
        if cx and cy:
            shear0 = shear0 + s if cx * cy > 0 else shear0 - s
    g0 = fluid * post(NF, 0)
    new_ref[NF, x_index] = g0
    bval = g0
    gy = None
    for n, k in enumerate((1, 3, 5)):
        a, b = pull(NF + k, n)
        bval = bval + (a + b)
        if k == 3:
            gy = a - b
    inv = 1.0 / rho
    ux, uy, uz = momx * inv, momy * inv, momz * inv
    current = gy - bval * uy
    shear = shear0 - momx * uy
    force = (COUPLE * bcell) * current
    vx = ux + TAU_PLUS * force * inv

    def push(i, n):
        minus, plus = near(n)
        a = fluid * jnp.where(plus, moved(adj, adj_row, i, 1), adj(i + 1, 0))
        b = fluid * jnp.where(minus, moved(adj, adj_row, i + 1, 1), adj(i, 0))
        return a, b

    l0 = fluid * adj(0, 0)
    out_ref[0, x_index] = (1.0 - 2.0 * PLUS) * l0
    total = (2.0 * PLUS * W0) * l0
    m1 = [0.0, 0.0, 0.0]
    m2 = {}
    for n, i in enumerate(FIRST):
        a, b = push(i, n)
        s, d = a + b, a - b
        de = (0.5 - PLUS) * s
        do = (0.5 - MINUS) * d
        out_ref[i, x_index] = de + do
        out_ref[i + 1, x_index] = de - do
        w = weight(i)
        s = (2.0 * PLUS * w) * s
        d = (2.0 * MINUS * w) * d
        total = total + s
        c = LATTICE[i]
        for axis in range(3):
            if c[axis]:
                m1[axis] = m1[axis] + d if c[axis] > 0 else m1[axis] - d
            for other in range(axis, 3):
                sign = c[axis] * c[other]
                if sign:
                    old = m2.get((axis, other))
                    if old is None:
                        m2[axis, other] = s if sign > 0 else -s
                    else:
                        m2[axis, other] = old + s if sign > 0 else old - s
    h0 = fluid * adj(NF, 0)
    hsum = V0 * h0
    h1 = []
    hs = None
    for n, k in enumerate((1, 3, 5)):
        a, b = push(NF + k, n)
        hs = a + b if hs is None else hs + (a + b)
        h1.append(V1 * (a - b))
    hsum = hsum + V1 * hs

    base = 1.0 - 1.5 * (vx * vx + uy * uy + uz * uz)
    tx = m2[0, 0] * vx + m2[0, 1] * uy + m2[0, 2] * uz
    ty = m2[0, 1] * vx + m2[1, 1] * uy + m2[1, 2] * uz
    tz = m2[0, 2] * vx + m2[1, 2] * uy + m2[2, 2] * uz
    rhobar = (
        total * base
        + 4.5 * (vx * tx + uy * ty + uz * tz)
        + 3.0 * (m1[0] * vx + m1[1] * uy + m1[2] * uz)
    )
    total3 = 3.0 * total
    vxbar = rho * (9.0 * tx + 3.0 * m1[0] - total3 * vx)
    uybar = rho * (9.0 * ty + 3.0 * m1[1] - total3 * uy)
    uzbar = rho * (9.0 * tz + 3.0 * m1[2] - total3 * uz)
    slope = 4.0 * bval
    forcebar = (TAU_PLUS * vxbar) * inv
    rhobar = rhobar - forcebar * force * inv
    currentbar = (COUPLE * bcell) * forcebar
    shearbar = (SOURCE * bcell) * hsum
    dcell = COUPLE * current * forcebar + SOURCE * shear * hsum
    uxbar = vxbar + slope * h1[0]
    uybar = uybar + slope * h1[1] - bval * currentbar - momx * shearbar
    uzbar = uzbar + slope * h1[2]
    bbar = hsum + 4.0 * (h1[0] * ux + h1[1] * uy + h1[2] * uz) - uy * currentbar
    mxbar = uxbar * inv - uy * shearbar
    mybar = uybar * inv
    mzbar = uzbar * inv
    rhobar = rhobar - (ux * uxbar + uy * uybar + uz * uzbar) * inv

    out_ref[0, x_index] = out_ref[0, x_index] + rhobar
    for i in FIRST:
        cm = along(i, mxbar, mybar, mzbar)
        cx, cy, _ = LATTICE[i]
        common = rhobar
        if cx and cy:
            common = rhobar + shearbar if cx * cy > 0 else rhobar - shearbar
        out_ref[i, x_index] = out_ref[i, x_index] + (common + cm)
        out_ref[i + 1, x_index] = out_ref[i + 1, x_index] + (common - cm)
    for k in range(NG):
        value = bbar
        if k == 3:
            value = bbar + currentbar
        elif k == 4:
            value = bbar - currentbar
        out_ref[NF + k, x_index] = value

    share = dcell * profile
    for m in range(count):
        hit = jnp.where(magnet == m, share, 0.0)
        part = hit[:, 0:128]
        for z in range(128, sz, 128):
            part = part + hit[:, z : z + 128]
        sums_ref[m] = sums_ref[m] + part


def edges():
    here = lax.axis_index("gy")
    keep_low = jnp.where(here == 0, 0.0, 1.0)
    keep_high = jnp.where(here == lax.axis_size("gy") - 1, 0.0, 1.0)
    return keep_low, keep_high


def halo_slot(kind, i, dy):
    names = (UP, DOWN) if (dy == -1) == (kind == 0) else (DOWN, UP)
    return names[0].index(i) + 6 * kind


def face_slot(kind, i, dx):
    names = RIGHT if (dx == -1) == (kind == 0) else LEFT
    return names.index(i) + 6 * kind


def start_all(copies):
    for c in copies:
        c.start()


def load_halo(first_ref, second_ref, halo_ref, sem):
    odd = lax.rem(lax.axis_index("gy"), 2)
    return [
        pltpu.make_async_copy(first_ref, halo_ref.at[1 - odd], sem.at[0]),
        pltpu.make_async_copy(second_ref, halo_ref.at[odd], sem.at[1]),
    ]


def mask_halo(halo_ref):
    keep_low, keep_high = edges()
    halo_ref[0, MASK] = halo_ref[0, MASK] * keep_low
    halo_ref[1, MASK] = halo_ref[1, MASK] * keep_high


def inner_kernel(
    post_ref, adjf_ref, adjg_ref, first_ref, second_ref, profile_ref, strengths_ref, wall_ref,
    magnet_ref,
    newf_ref, newg_ref, outf_ref, outg_ref, sums_ref,
    post_v, adj_v, new_v, out_v, halo_v, near_v,
    post_sem, adjf_sem, adjg_sem, halo_sem, newf_sem, newg_sem, outf_sem, outg_sem,
):
    sx = post_v.shape[1]
    count = sums_ref.shape[0]

    def loads(x):
        return [
            pltpu.make_async_copy(post_ref.at[:, x], post_v.at[:, x], post_sem.at[x]),
            pltpu.make_async_copy(adjf_ref.at[:, x], adj_v.at[pl.ds(0, NF), x], adjf_sem.at[x]),
            pltpu.make_async_copy(adjg_ref.at[:, x], adj_v.at[pl.ds(NF, NG), x], adjg_sem.at[x]),
        ]

    def stores(x):
        return [
            pltpu.make_async_copy(new_v.at[pl.ds(0, NF), x], newf_ref.at[:, x], newf_sem.at[x]),
            pltpu.make_async_copy(new_v.at[pl.ds(NF, NG), x], newg_ref.at[:, x], newg_sem.at[x]),
            pltpu.make_async_copy(out_v.at[pl.ds(0, NF), x], outf_ref.at[:, x], outf_sem.at[x]),
            pltpu.make_async_copy(out_v.at[pl.ds(NF, NG), x], outg_ref.at[:, x], outg_sem.at[x]),
        ]

    def finish(copies):
        for c in copies:
            c.wait()

    halo = load_halo(first_ref, second_ref, halo_v, halo_sem)
    start_all(halo)
    for x in range(sx):
        start_all(loads(x))
    sums_ref[...] = jnp.zeros_like(sums_ref)
    table = lane_table(strengths_ref)
    finish(halo)
    mask_halo(halo_v)
    finish(loads(0))
    finish(loads(1))

    def body(x, carry):
        finish(loads(x + 1))

        def side(dy):
            return 0 if dy == -1 else 1

        def row_of(slot, dx, dy):
            return halo_v[side(dy), slot, pl.ds(x + dx, 1), :]

        def mask(dx):
            return 1.0 - wall_ref[x + dx].astype(jnp.float32)

        magnet = magnet_ref[x]
        profile = profile_ref[x]
        plane_step(
            x,
            lambda i, dx: post_v[i, x + dx],
            lambda i, dx, dy: row_of(halo_slot(0, i, dy), dx, dy),
            lambda i, dx: adj_v[i, x + dx],
            lambda i, dx, dy: row_of(halo_slot(1, i, dy), dx, dy),
            mask,
            lambda dx, dy: row_of(MASK, dx, dy),
            mask(0),
            gather_strength(table, magnet) * profile,
            profile,
            magnet,
            near_v,
            new_v,
            out_v,
            sums_ref,
            count,
        )
        start_all(stores(x))
        return carry

    lax.fori_loop(1, sx - 1, body, 0)
    for x in range(1, sx - 1):
        finish(stores(x))


ANY = pl.BlockSpec(memory_space=pl.ANY)
VMEM = pl.BlockSpec(memory_space=pltpu.VMEM)


def inner_call(post, adjf, adjg, first, second, profile, strengths, wall, magnet):
    sx, sy, sz = profile.shape
    count = strengths.shape[1]
    full = pltpu.VMEM((NP, sx, sy, sz), jnp.float32)
    dma = pltpu.SemaphoreType.DMA
    return pl.pallas_call(
        inner_kernel,
        in_specs=[ANY, ANY, ANY, ANY, ANY, VMEM, VMEM, VMEM, VMEM],
        out_specs=[ANY, ANY, ANY, ANY, VMEM],
        out_shape=[
            jax.ShapeDtypeStruct(adjf.shape, jnp.float32),
            jax.ShapeDtypeStruct(adjg.shape, jnp.float32),
            jax.ShapeDtypeStruct(adjf.shape, jnp.float32),
            jax.ShapeDtypeStruct(adjg.shape, jnp.float32),
            jax.ShapeDtypeStruct((count, 8, 128), jnp.float32),
        ],
        scratch_shapes=[
            full,
            full,
            full,
            full,
            pltpu.VMEM((2, SLOTS, sx, sz), jnp.float32),
            pltpu.VMEM((18, sy, sz), jnp.float32),
            dma((sx,)),
            dma((sx,)),
            dma((sx,)),
            dma((2,)),
            dma((sx,)),
            dma((sx,)),
            dma((sx,)),
            dma((sx,)),
        ],
        compiler_params=pltpu.CompilerParams(vmem_limit_bytes=40 << 20),
        cost_estimate=pl.CostEstimate(
            flops=700 * sx * sy * sz, bytes_accessed=16 * NP * sx * sy * sz, transcendentals=0
        ),
        name="inner",
    )(post, adjf, adjg, first, second, profile, strengths, wall, magnet)


def outer_kernel(
    post_ref, adjf_ref, adjg_ref, first_ref, second_ref, fromleft_ref, fromright_ref,
    cornerleft_ref, cornerright_ref, profile_ref, strengths_ref, wall_ref, magnet_ref,
    partial_ref, newf_in, newg_in, outf_in, outg_in,
    newf_ref, newg_ref, outf_ref, outg_ref, share_ref,
    post_v, adj_v, new_v, out_v, halo_v, near_v, sums_v,
    post_sem, adjf_sem, adjg_sem, halo_sem, store_sem,
):
    del newf_in, newg_in, outf_in, outg_in
    sx = wall_ref.shape[0]
    count = sums_v.shape[0]
    from_planes = (0, 1, sx - 2, sx - 1)
    loads = []
    for n, x in enumerate(from_planes):
        loads += [
            pltpu.make_async_copy(post_ref.at[:, x], post_v.at[:, n], post_sem.at[n]),
            pltpu.make_async_copy(adjf_ref.at[:, x], adj_v.at[pl.ds(0, NF), n], adjf_sem.at[n]),
            pltpu.make_async_copy(adjg_ref.at[:, x], adj_v.at[pl.ds(NF, NG), n], adjg_sem.at[n]),
        ]
    halo = load_halo(first_ref, second_ref, halo_v, halo_sem)
    start_all(halo)
    start_all(loads)
    sums_v[...] = partial_ref[...]
    table = lane_table(strengths_ref)
    keep_low, keep_high = edges()
    for c in halo:
        c.wait()
    mask_halo(halo_v)
    stores = []
    for n, (x, away, here, near_plane) in enumerate(((0, -1, 0, 1), (sx - 1, 1, 3, 2))):
        for c in loads[6 * n : 6 * n + 6]:
            c.wait()
        face_ref, corner_ref = (
            (fromleft_ref, cornerleft_ref) if away == -1 else (fromright_ref, cornerright_ref)
        )

        def get(kind, i, dx, held, here=here, near_plane=near_plane, away=away, face_ref=face_ref):
            if dx == 0:
                return held[i, here]
            if dx == away:
                return face_ref[face_slot(kind, i, dx)]
            return held[i, near_plane]

        def row(kind, i, dx, dy, x=x, away=away, corner_ref=corner_ref):
            side = 0 if dy == -1 else 1
            if dx == away:
                line = corner_ref[2 * kind + side : 2 * kind + side + 1, :]
                if kind == 2:
                    line = line * (keep_low if side == 0 else keep_high)
                return line
            slot = MASK if kind == 2 else halo_slot(kind, i, dy)
            return halo_v[side, slot, x + dx : x + dx + 1, :]

        def mask(dx, x=x, away=away, face_ref=face_ref):
            if dx == away:
                return face_ref[MASK]
            return 1.0 - wall_ref[x + dx].astype(jnp.float32)

        magnet = magnet_ref[x]
        profile = profile_ref[x]
        plane_step(
            n,
            lambda i, dx, get=get: get(0, i, dx, post_v),
            lambda i, dx, dy, row=row: row(0, i, dx, dy),
            lambda i, dx, get=get: get(1, i, dx, adj_v),
            lambda i, dx, dy, row=row: row(1, i, dx, dy),
            mask,
            lambda dx, dy, row=row: row(2, 0, dx, dy),
            mask(0),
            gather_strength(table, magnet) * profile,
            profile,
            magnet,
            near_v,
            new_v,
            out_v,
            sums_v,
            count,
        )
        these = [
            pltpu.make_async_copy(new_v.at[pl.ds(0, NF), n], newf_ref.at[:, x], store_sem.at[n, 0]),
            pltpu.make_async_copy(new_v.at[pl.ds(NF, NG), n], newg_ref.at[:, x], store_sem.at[n, 1]),
            pltpu.make_async_copy(out_v.at[pl.ds(0, NF), n], outf_ref.at[:, x], store_sem.at[n, 2]),
            pltpu.make_async_copy(out_v.at[pl.ds(NF, NG), n], outg_ref.at[:, x], store_sem.at[n, 3]),
        ]
        start_all(these)
        stores += these
    rows = jnp.concatenate(
        [jnp.sum(sums_v[m], axis=0, keepdims=True) for m in range(count)], axis=0
    )
    share_ref[...] = lax.dot_general(
        jnp.ones((8, 128), jnp.float32),
        rows,
        (((1,), (1,)), ((), ())),
        precision=lax.Precision.HIGHEST,
        preferred_element_type=jnp.float32,
    )
    for c in stores:
        c.wait()


def outer_call(
    post, adjf, adjg, first, second, fromleft, fromright, cornerleft, cornerright, profile,
    strengths, wall, magnet, partial, newf, newg, outf, outg,
):
    sx, sy, sz = profile.shape
    count = strengths.shape[1]
    dma = pltpu.SemaphoreType.DMA
    return pl.pallas_call(
        outer_kernel,
        in_specs=[ANY] * 5 + [VMEM] * 9 + [ANY] * 4,
        out_specs=[ANY] * 4 + [VMEM],
        out_shape=[
            jax.ShapeDtypeStruct(adjf.shape, jnp.float32),
            jax.ShapeDtypeStruct(adjg.shape, jnp.float32),
            jax.ShapeDtypeStruct(adjf.shape, jnp.float32),
            jax.ShapeDtypeStruct(adjg.shape, jnp.float32),
            jax.ShapeDtypeStruct((8, count), jnp.float32),
        ],
        input_output_aliases={14: 0, 15: 1, 16: 2, 17: 3},
        scratch_shapes=[
            pltpu.VMEM((NP, 4, sy, sz), jnp.float32),
            pltpu.VMEM((NP, 4, sy, sz), jnp.float32),
            pltpu.VMEM((NP, 2, sy, sz), jnp.float32),
            pltpu.VMEM((NP, 2, sy, sz), jnp.float32),
            pltpu.VMEM((2, SLOTS, sx, sz), jnp.float32),
            pltpu.VMEM((18, sy, sz), jnp.float32),
            pltpu.VMEM((count, 8, 128), jnp.float32),
            dma((4,)),
            dma((4,)),
            dma((4,)),
            dma((2,)),
            dma((2, 4)),
        ],
        compiler_params=pltpu.CompilerParams(vmem_limit_bytes=40 << 20),
        name="outer",
    )(
        post, adjf, adjg, first, second, fromleft, fromright, cornerleft, cornerright, profile,
        strengths, wall, magnet, partial, newf, newg, outf, outg,
    )


def ring(count, step):
    return [(i, (i + step) % count) for i in range(count)]


def butterfly(value):
    for axis in ("gy", "gx"):
        count = lax.axis_size(axis)
        step = 1
        while step < count:
            value = value + lax.ppermute(value, axis, [(i, i ^ step) for i in range(count)])
            step *= 2
    return value


def on_device(flow, field, adj_flow_in, adj_field_in, profile, strengths, wall, magnet):
    across, around = lax.axis_size("gy"), lax.axis_size("gx")
    count = strengths.shape[0]
    table = strengths.reshape(1, count)
    post, mine1, mine2, right, left = collide_call(
        flow, field, adj_flow_in, adj_field_in, profile, table, wall, magnet
    )
    inside = [(i, i ^ 1) for i in range(across)]
    between = [(i, (((i + 1) ^ 1) - 1) % across) for i in range(across)]
    second = lax.ppermute(mine2, "gy", between)
    first = lax.ppermute(mine1, "gy", inside)
    fromleft = lax.ppermute(right, "gx", ring(around, 1))
    fromright = lax.ppermute(left, "gx", ring(around, -1))
    corner_r, corner_l = corner_call(first, second)
    cornerleft = lax.ppermute(corner_r, "gx", ring(around, 1))
    cornerright = lax.ppermute(corner_l, "gx", ring(around, -1))
    newf, newg, outf, outg, partial = inner_call(
        post, adj_flow_in, adj_field_in, first, second, profile, table, wall, magnet
    )
    newf, newg, outf, outg, share = outer_call(
        post, adj_flow_in, adj_field_in, first, second, fromleft, fromright, cornerleft,
        cornerright, profile, table, wall, magnet, partial, newf, newg, outf, outg,
    )
    cells = flow.shape[1] * around * flow.shape[2] * across * flow.shape[3]
    totals = butterfly(share[0])
    return (newf, newg, outf, outg, totals / math.sqrt(cells / count))


def solution(mesh):
    stack = P(None, "gx", "gy", None)
    cell = P("gx", "gy", None)
    return jax.shard_map(
        on_device,
        mesh=mesh,
        in_specs=(stack, stack, stack, stack, cell, P(), cell, cell),
        out_specs=(stack, stack, stack, stack, P()),
        check_vma=False,
    )
```

```python
import functools
import math

import jax
import jax.numpy as jnp
from jax import lax
from jax.experimental import pallas as pl
from jax.experimental.pallas import tpu as pltpu
from jax.sharding import PartitionSpec as P

LATTICE = [
    (0, 0, 0),
    (1, 0, 0),
    (-1, 0, 0),
    (0, 1, 0),
    (0, -1, 0),
    (0, 0, 1),
    (0, 0, -1),
    (1, 1, 0),
    (-1, -1, 0),
    (1, -1, 0),
    (-1, 1, 0),
    (1, 0, 1),
    (-1, 0, -1),
    (1, 0, -1),
    (-1, 0, 1),
    (0, 1, 1),
    (0, -1, -1),
    (0, 1, -1),
    (0, -1, 1),
]
NF, NG = 19, 7
NP = NF + NG
FIRST = [1, 3, 5, 7, 9, 11, 13, 15, 17]
W0, W1, W2 = 1.0 / 3.0, 1.0 / 18.0, 1.0 / 36.0
V0, V1 = 0.25, 0.125
PLUS = 0.625
MINUS = 0.5 / 1.125
TAU_PLUS = 0.8
COUPLE = 2.0
SOURCE = 2.0

UP = [3, 7, 10, 15, 17, NF + 3]
DOWN = [4, 8, 9, 16, 18, NF + 4]
RIGHT = [1, 7, 9, 11, 13, NF + 1]
LEFT = [2, 8, 10, 12, 14, NF + 2]
SLOTS = 13
MASK = 12


def weight(i):
    return W1 if i <= 6 else W2


def gather_strength(table, magnet):
    parts = [
        jnp.take_along_axis(table, magnet[:, z : z + 128], axis=1, mode="promise_in_bounds")
        for z in range(0, magnet.shape[1], 128)
    ]
    return jnp.concatenate(parts, axis=1)


def lane_table(strengths_ref):
    row = strengths_ref[...]
    rest = 128 - row.shape[1]
    if rest:
        row = jnp.concatenate([row, jnp.zeros((1, rest), jnp.float32)], axis=1)
    return jnp.broadcast_to(row, (8, 128))


def vector_sums(pair):
    x = pair[1] + pair[7] + pair[9] + pair[11] + pair[13]
    y = pair[3] + pair[7] - pair[9] + pair[15] + pair[17]
    z = pair[5] + pair[11] - pair[13] + pair[15] - pair[17]
    return x, y, z


def along(i, vx, vy, vz):
    out = None
    for c, v in zip(LATTICE[i], (vx, vy, vz)):
        if c:
            if out is None:
                out = v if c > 0 else -v
            else:
                out = out + v if c > 0 else out - v
    return out


def collide_kernel(
    planes,
    flow_ref,
    field_ref,
    adjf_ref,
    adjg_ref,
    profile_ref,
    strengths_ref,
    wall_ref,
    magnet_ref,
    post_ref,
    first_ref,
    second_ref,
    right_ref,
    left_ref,
):
    step = pl.program_id(0)
    steps = pl.num_programs(0)
    odd = lax.rem(lax.axis_index("gy"), 2)
    table = lane_table(strengths_ref)
    last = flow_ref.shape[2] - 1

    for p in range(planes):
        fluid = 1.0 - wall_ref[p].astype(jnp.float32)
        bcell = gather_strength(table, magnet_ref[p]) * profile_ref[p]
        f = [flow_ref[i, p] for i in range(NF)]
        g = [field_ref[k, p] for k in range(NG)]
        even = {i: f[i] + f[i + 1] for i in FIRST}
        diff = {i: f[i] - f[i + 1] for i in FIRST}
        rho = f[0] + (1.0 - fluid)
        for i in FIRST:
            rho = rho + even[i]
        momx, momy, momz = vector_sums(diff)
        inv = 1.0 / rho
        ux, uy, uz = momx * inv, momy * inv, momz * inv
        bval = g[0] + g[1] + g[2] + g[3] + g[4] + g[5] + g[6]
        current = (g[3] - g[4]) - bval * uy
        shear = (even[7] - even[9]) - momx * uy
        force = (COUPLE * bcell) * current
        vx = ux + TAU_PLUS * force * inv
        base = 1.0 - 1.5 * (vx * vx + uy * uy + uz * uz)
        post_ref[0, p] = f[0] - 2.0 * PLUS * (f[0] - (W0 * rho) * base)
        rho1, rho2 = W1 * rho, W2 * rho
        for i in FIRST:
            wr = rho1 if i <= 6 else rho2
            a = along(i, vx, uy, uz)
            ne = even[i] - (2.0 * wr) * (base + 4.5 * a * a)
            no = diff[i] - (6.0 * wr) * a
            ne = PLUS * ne
            no = MINUS * no
            post_ref[i, p] = f[i] - ne - no
            post_ref[i + 1, p] = f[i + 1] - ne + no
        common = bval + (SOURCE * bcell) * shear
        slope = 4.0 * bval
        post_ref[NF, p] = V0 * common
        for k, u in ((1, ux), (3, uy), (5, uz)):
            su = slope * u
            post_ref[NF + k, p] = V1 * (common + su)
            post_ref[NF + k + 1, p] = V1 * (common - su)

        x = step * planes + p
        here = pl.ds(x, 1)

        def adj_row(i, row):
            return adjf_ref[i, p, pl.ds(row, 1), :]

        for out, side in ((first_ref, odd), (second_ref, 1 - odd)):
            row = (1 - side) * last
            for s in range(6):
                up, down = UP[s], DOWN[s]
                out[s, here, :] = post_ref[up + side * (down - up), p, pl.ds(row, 1), :]
                if up < NF:
                    line = adjf_ref[down + side * (up - down), p, pl.ds(row, 1), :]
                else:
                    line = adjg_ref[down - NF + side * (up - down), p, pl.ds(row, 1), :]
                out[6 + s, here, :] = line
            out[MASK, here, :] = 1.0 - wall_ref[p, pl.ds(row, 1), :].astype(jnp.float32)

    def pack_x(out, p, posts, adjs):
        for s in range(6):
            out[s] = post_ref[posts[s], p]
            j = adjs[s]
            out[6 + s] = adjf_ref[j, p] if j < NF else adjg_ref[j - NF, p]
        out[MASK] = 1.0 - wall_ref[p].astype(jnp.float32)

    @pl.when(step == 0)
    def _():
        pack_x(left_ref, 0, LEFT, RIGHT)

    @pl.when(step == steps - 1)
    def _():
        pack_x(right_ref, planes - 1, RIGHT, LEFT)


def collide_call(flow, field, adjf, adjg, profile, strengths, wall, magnet, planes=2):
    sx, sy, sz = profile.shape
    grid = sx // planes

    def stack(n):
        return pl.BlockSpec((n, planes, sy, sz), lambda x: (0, x, 0, 0))

    one = pl.BlockSpec((planes, sy, sz), lambda x: (x, 0, 0))

    def whole(*shape):
        return pl.BlockSpec(shape, lambda x: (0,) * len(shape))

    rows = jax.ShapeDtypeStruct((SLOTS, sx, sz), jnp.float32)
    faces = jax.ShapeDtypeStruct((SLOTS, sy, sz), jnp.float32)
    return pl.pallas_call(
        functools.partial(collide_kernel, planes),
        grid=(grid,),
        in_specs=[
            stack(NF),
            stack(NG),
            stack(NF),
            stack(NG),
            one,
            whole(*strengths.shape),
            one,
            one,
        ],
        out_specs=[
            stack(NP),
            whole(*rows.shape),
            whole(*rows.shape),
            whole(*faces.shape),
            whole(*faces.shape),
        ],
        out_shape=[
            jax.ShapeDtypeStruct((NP, sx, sy, sz), jnp.float32),
            rows,
            rows,
            faces,
            faces,
        ],
        compiler_params=pltpu.CompilerParams(vmem_limit_bytes=62 << 20),
        name="collide",
    )(flow, field, adjf, adjg, profile, strengths, wall, magnet)


CORNER_RIGHT = ((0, 7, 0, 8), (1, 9, 1, 10))
CORNER_LEFT = ((0, 10, 0, 9), (1, 8, 1, 7))


def corner_slots(side, post, adj):
    posts, adjs = (UP, DOWN) if side == 0 else (DOWN, UP)
    return posts.index(post), 6 + adjs.index(adj), MASK


def corner_kernel(first_ref, second_ref, right_ref, left_ref):
    odd = lax.rem(lax.axis_index("gy"), 2) == 1
    sx = first_ref.shape[1]

    def row(side, slot, x):
        a, b = first_ref[slot, x : x + 1, :], second_ref[slot, x : x + 1, :]
        return jnp.where(odd, a, b) if side == 0 else jnp.where(odd, b, a)

    for out, table, x in ((right_ref, CORNER_RIGHT, sx - 1), (left_ref, CORNER_LEFT, 0)):
        out[...] = jnp.zeros_like(out)
        for side, post, _, adj in table:
            for n, slot in enumerate(corner_slots(side, post, adj)):
                out[2 * n + side : 2 * n + side + 1, :] = row(side, slot, x)


def corner_call(first, second):
    sz = first.shape[2]
    out = jax.ShapeDtypeStruct((8, sz), jnp.float32)
    return pl.pallas_call(corner_kernel, out_shape=[out, out], compiler_params=pltpu.CompilerParams(vmem_limit_bytes=2 << 20), name="corners")(first, second)


def plane_step(
    x_index, post, post_row, adj, adj_row, mask, mask_row, fluid, bcell, profile, magnet,
    near_ref, new_ref, out_ref, sums_ref, count,
):
    sy, sz = fluid.shape
    yi = lax.broadcasted_iota(jnp.int32, (sy, sz), 0)
    zi = lax.broadcasted_iota(jnp.int32, (sy, sz), 1)
    top, bottom = yi == sy - 1, yi == 0
    zlast, zfirst = zi == sz - 1, zi == 0

    def shift(value, row, dy, dz):
        if dy == -1:
            value = jnp.where(bottom, row(), pltpu.roll(value, 1, 0))
        elif dy == 1:
            value = jnp.where(top, row(), pltpu.roll(value, sy - 1, 0))
        if dz == -1:
            value = pltpu.roll(value, 1, 1)
        elif dz == 1:
            value = pltpu.roll(value, sz - 1, 1)
        return value

    def moved(get, get_row, i, sign):
        dx, dy, dz = (sign * c for c in LATTICE[i if i < NF else i - NF])
        return shift(get(i, dx), lambda: get_row(i, dx, dy), dy, dz)

    def near_of(i, sign):
        dx, dy, dz = (sign * c for c in LATTICE[i])
        value = shift(mask(dx), lambda: mask_row(dx, dy), dy, dz)
        if dz == -1:
            value = jnp.where(zfirst, 0.0, value)
        elif dz == 1:
            value = jnp.where(zlast, 0.0, value)
        return value

    for n, i in enumerate(FIRST):
        near_ref[2 * n] = near_of(i, -1)
        near_ref[2 * n + 1] = near_of(i, 1)

    def near(n):
        return near_ref[2 * n] > 0.5, near_ref[2 * n + 1] > 0.5

    def pull(i, n):
        minus, plus = near(n)
        a = fluid * jnp.where(minus, moved(post, post_row, i, -1), post(i + 1, 0))
        b = fluid * jnp.where(plus, moved(post, post_row, i + 1, -1), post(i, 0))
        new_ref[i, x_index] = a
        new_ref[i + 1, x_index] = b
        return a, b

    f0 = fluid * post(0, 0)
    new_ref[0, x_index] = f0
    rho = f0 + (1.0 - fluid)
    momx = momy = momz = shear0 = 0.0
    for n, i in enumerate(FIRST):
        a, b = pull(i, n)
        s, d = a + b, a - b
        rho = rho + s
        cx, cy, cz = LATTICE[i]
        if cx:
            momx = momx + d
        if cy:
            momy = momy + d if cy > 0 else momy - d
        if cz:
            momz = momz + d if cz > 0 else momz - d
        if cx and cy:
            shear0 = shear0 + s if cx * cy > 0 else shear0 - s
    g0 = fluid * post(NF, 0)
    new_ref[NF, x_index] = g0
    bval = g0
    gy = None
    for n, k in enumerate((1, 3, 5)):
        a, b = pull(NF + k, n)
        bval = bval + (a + b)
        if k == 3:
            gy = a - b
    inv = 1.0 / rho
    ux, uy, uz = momx * inv, momy * inv, momz * inv
    current = gy - bval * uy
    shear = shear0 - momx * uy
    force = (COUPLE * bcell) * current
    vx = ux + TAU_PLUS * force * inv

    def push(i, n):
        minus, plus = near(n)
        a = fluid * jnp.where(plus, moved(adj, adj_row, i, 1), adj(i + 1, 0))
        b = fluid * jnp.where(minus, moved(adj, adj_row, i + 1, 1), adj(i, 0))
        return a, b

    l0 = fluid * adj(0, 0)
    out_ref[0, x_index] = (1.0 - 2.0 * PLUS) * l0
    total = (2.0 * PLUS * W0) * l0
    m1 = [0.0, 0.0, 0.0]
    m2 = {}
    for n, i in enumerate(FIRST):
        a, b = push(i, n)
        s, d = a + b, a - b
        de = (0.5 - PLUS) * s
        do = (0.5 - MINUS) * d
        out_ref[i, x_index] = de + do
        out_ref[i + 1, x_index] = de - do
        w = weight(i)
        s = (2.0 * PLUS * w) * s
        d = (2.0 * MINUS * w) * d
        total = total + s
        c = LATTICE[i]
        for axis in range(3):
            if c[axis]:
                m1[axis] = m1[axis] + d if c[axis] > 0 else m1[axis] - d
            for other in range(axis, 3):
                sign = c[axis] * c[other]
                if sign:
                    old = m2.get((axis, other))
                    if old is None:
                        m2[axis, other] = s if sign > 0 else -s
                    else:
                        m2[axis, other] = old + s if sign > 0 else old - s
    h0 = fluid * adj(NF, 0)
    hsum = V0 * h0
    h1 = []
    hs = None
    for n, k in enumerate((1, 3, 5)):
        a, b = push(NF + k, n)
        hs = a + b if hs is None else hs + (a + b)
        h1.append(V1 * (a - b))
    hsum = hsum + V1 * hs

    base = 1.0 - 1.5 * (vx * vx + uy * uy + uz * uz)
    tx = m2[0, 0] * vx + m2[0, 1] * uy + m2[0, 2] * uz
    ty = m2[0, 1] * vx + m2[1, 1] * uy + m2[1, 2] * uz
    tz = m2[0, 2] * vx + m2[1, 2] * uy + m2[2, 2] * uz
    rhobar = (
        total * base
        + 4.5 * (vx * tx + uy * ty + uz * tz)
        + 3.0 * (m1[0] * vx + m1[1] * uy + m1[2] * uz)
    )
    total3 = 3.0 * total
    vxbar = rho * (9.0 * tx + 3.0 * m1[0] - total3 * vx)
    uybar = rho * (9.0 * ty + 3.0 * m1[1] - total3 * uy)
    uzbar = rho * (9.0 * tz + 3.0 * m1[2] - total3 * uz)
    slope = 4.0 * bval
    forcebar = (TAU_PLUS * vxbar) * inv
    rhobar = rhobar - forcebar * force * inv
    currentbar = (COUPLE * bcell) * forcebar
    shearbar = (SOURCE * bcell) * hsum
    dcell = COUPLE * current * forcebar + SOURCE * shear * hsum
    uxbar = vxbar + slope * h1[0]
    uybar = uybar + slope * h1[1] - bval * currentbar - momx * shearbar
    uzbar = uzbar + slope * h1[2]
    bbar = hsum + 4.0 * (h1[0] * ux + h1[1] * uy + h1[2] * uz) - uy * currentbar
    mxbar = uxbar * inv - uy * shearbar
    mybar = uybar * inv
    mzbar = uzbar * inv
    rhobar = rhobar - (ux * uxbar + uy * uybar + uz * uzbar) * inv

    out_ref[0, x_index] = out_ref[0, x_index] + rhobar
    for i in FIRST:
        cm = along(i, mxbar, mybar, mzbar)
        cx, cy, _ = LATTICE[i]
        common = rhobar
        if cx and cy:
            common = rhobar + shearbar if cx * cy > 0 else rhobar - shearbar
        out_ref[i, x_index] = out_ref[i, x_index] + (common + cm)
        out_ref[i + 1, x_index] = out_ref[i + 1, x_index] + (common - cm)
    for k in range(NG):
        value = bbar
        if k == 3:
            value = bbar + currentbar
        elif k == 4:
            value = bbar - currentbar
        out_ref[NF + k, x_index] = value

    share = dcell * profile
    for m in range(count):
        hit = jnp.where(magnet == m, share, 0.0)
        part = hit[:, 0:128]
        for z in range(128, sz, 128):
            part = part + hit[:, z : z + 128]
        sums_ref[m] = sums_ref[m] + part


def edges():
    here = lax.axis_index("gy")
    keep_low = jnp.where(here == 0, 0.0, 1.0)
    keep_high = jnp.where(here == lax.axis_size("gy") - 1, 0.0, 1.0)
    return keep_low, keep_high


def halo_slot(kind, i, dy):
    names = (UP, DOWN) if (dy == -1) == (kind == 0) else (DOWN, UP)
    return names[0].index(i) + 6 * kind


def face_slot(kind, i, dx):
    names = RIGHT if (dx == -1) == (kind == 0) else LEFT
    return names.index(i) + 6 * kind


def start_all(copies):
    for c in copies:
        c.start()


def load_halo(first_ref, second_ref, halo_ref, sem):
    odd = lax.rem(lax.axis_index("gy"), 2)
    return [
        pltpu.make_async_copy(first_ref, halo_ref.at[1 - odd], sem.at[0]),
        pltpu.make_async_copy(second_ref, halo_ref.at[odd], sem.at[1]),
    ]


def mask_halo(halo_ref):
    keep_low, keep_high = edges()
    halo_ref[0, MASK] = halo_ref[0, MASK] * keep_low
    halo_ref[1, MASK] = halo_ref[1, MASK] * keep_high


def inner_kernel(
    post_ref, adjf_ref, adjg_ref, first_ref, second_ref, profile_ref, strengths_ref, wall_ref,
    magnet_ref,
    newf_ref, newg_ref, outf_ref, outg_ref, sums_ref,
    post_v, adj_v, new_v, out_v, halo_v, near_v,
    post_sem, adjf_sem, adjg_sem, halo_sem, newf_sem, newg_sem, outf_sem, outg_sem,
):
    sx = post_v.shape[1]
    count = sums_ref.shape[0]

    def loads(x):
        return [
            pltpu.make_async_copy(post_ref.at[:, x], post_v.at[:, x], post_sem.at[x]),
            pltpu.make_async_copy(adjf_ref.at[:, x], adj_v.at[pl.ds(0, NF), x], adjf_sem.at[x]),
            pltpu.make_async_copy(adjg_ref.at[:, x], adj_v.at[pl.ds(NF, NG), x], adjg_sem.at[x]),
        ]

    def stores(x):
        return [
            pltpu.make_async_copy(new_v.at[pl.ds(0, NF), x], newf_ref.at[:, x], newf_sem.at[x]),
            pltpu.make_async_copy(new_v.at[pl.ds(NF, NG), x], newg_ref.at[:, x], newg_sem.at[x]),
            pltpu.make_async_copy(out_v.at[pl.ds(0, NF), x], outf_ref.at[:, x], outf_sem.at[x]),
            pltpu.make_async_copy(out_v.at[pl.ds(NF, NG), x], outg_ref.at[:, x], outg_sem.at[x]),
        ]

    def finish(copies):
        for c in copies:
            c.wait()

    halo = load_halo(first_ref, second_ref, halo_v, halo_sem)
    start_all(halo)
    for x in range(sx):
        start_all(loads(x))
    sums_ref[...] = jnp.zeros_like(sums_ref)
    table = lane_table(strengths_ref)
    finish(halo)
    mask_halo(halo_v)
    finish(loads(0))
    finish(loads(1))

    def body(x, carry):
        finish(loads(x + 1))

        def side(dy):
            return 0 if dy == -1 else 1

        def row_of(slot, dx, dy):
            return halo_v[side(dy), slot, pl.ds(x + dx, 1), :]

        def mask(dx):
            return 1.0 - wall_ref[x + dx].astype(jnp.float32)

        magnet = magnet_ref[x]
        profile = profile_ref[x]
        plane_step(
            x,
            lambda i, dx: post_v[i, x + dx],
            lambda i, dx, dy: row_of(halo_slot(0, i, dy), dx, dy),
            lambda i, dx: adj_v[i, x + dx],
            lambda i, dx, dy: row_of(halo_slot(1, i, dy), dx, dy),
            mask,
            lambda dx, dy: row_of(MASK, dx, dy),
            mask(0),
            gather_strength(table, magnet) * profile,
            profile,
            magnet,
            near_v,
            new_v,
            out_v,
            sums_ref,
            count,
        )
        start_all(stores(x))
        return carry

    lax.fori_loop(1, sx - 1, body, 0)
    for x in range(1, sx - 1):
        finish(stores(x))


ANY = pl.BlockSpec(memory_space=pl.ANY)
VMEM = pl.BlockSpec(memory_space=pltpu.VMEM)


def inner_call(post, adjf, adjg, first, second, profile, strengths, wall, magnet):
    sx, sy, sz = profile.shape
    count = strengths.shape[1]
    full = pltpu.VMEM((NP, sx, sy, sz), jnp.float32)
    dma = pltpu.SemaphoreType.DMA
    return pl.pallas_call(
        inner_kernel,
        in_specs=[ANY, ANY, ANY, ANY, ANY, VMEM, VMEM, VMEM, VMEM],
        out_specs=[ANY, ANY, ANY, ANY, VMEM],
        out_shape=[
            jax.ShapeDtypeStruct(adjf.shape, jnp.float32),
            jax.ShapeDtypeStruct(adjg.shape, jnp.float32),
            jax.ShapeDtypeStruct(adjf.shape, jnp.float32),
            jax.ShapeDtypeStruct(adjg.shape, jnp.float32),
            jax.ShapeDtypeStruct((count, 8, 128), jnp.float32),
        ],
        scratch_shapes=[
            full,
            full,
            full,
            full,
            pltpu.VMEM((2, SLOTS, sx, sz), jnp.float32),
            pltpu.VMEM((18, sy, sz), jnp.float32),
            dma((sx,)),
            dma((sx,)),
            dma((sx,)),
            dma((2,)),
            dma((sx,)),
            dma((sx,)),
            dma((sx,)),
            dma((sx,)),
        ],
        compiler_params=pltpu.CompilerParams(vmem_limit_bytes=51 << 20),
        cost_estimate=pl.CostEstimate(
            flops=700 * sx * sy * sz, bytes_accessed=16 * NP * sx * sy * sz, transcendentals=0
        ),
        name="inner",
    )(post, adjf, adjg, first, second, profile, strengths, wall, magnet)


def outer_kernel(
    post_ref, adjf_ref, adjg_ref, first_ref, second_ref, fromleft_ref, fromright_ref,
    cornerleft_ref, cornerright_ref, profile_ref, strengths_ref, wall_ref, magnet_ref,
    partial_ref, newf_in, newg_in, outf_in, outg_in,
    newf_ref, newg_ref, outf_ref, outg_ref, share_ref,
    post_v, adj_v, new_v, out_v, halo_v, near_v, sums_v,
    post_sem, adjf_sem, adjg_sem, halo_sem, store_sem,
):
    del newf_in, newg_in, outf_in, outg_in
    sx = wall_ref.shape[0]
    count = sums_v.shape[0]
    from_planes = (0, 1, sx - 2, sx - 1)
    loads = []
    for n, x in enumerate(from_planes):
        loads += [
            pltpu.make_async_copy(post_ref.at[:, x], post_v.at[:, n], post_sem.at[n]),
            pltpu.make_async_copy(adjf_ref.at[:, x], adj_v.at[pl.ds(0, NF), n], adjf_sem.at[n]),
            pltpu.make_async_copy(adjg_ref.at[:, x], adj_v.at[pl.ds(NF, NG), n], adjg_sem.at[n]),
        ]
    halo = load_halo(first_ref, second_ref, halo_v, halo_sem)
    start_all(halo)
    start_all(loads)
    sums_v[...] = partial_ref[...]
    table = lane_table(strengths_ref)
    keep_low, keep_high = edges()
    for c in halo:
        c.wait()
    mask_halo(halo_v)
    stores = []
    for n, (x, away, here, near_plane) in enumerate(((0, -1, 0, 1), (sx - 1, 1, 3, 2))):
        for c in loads[6 * n : 6 * n + 6]:
            c.wait()
        face_ref, corner_ref = (
            (fromleft_ref, cornerleft_ref) if away == -1 else (fromright_ref, cornerright_ref)
        )

        def get(kind, i, dx, held, here=here, near_plane=near_plane, away=away, face_ref=face_ref):
            if dx == 0:
                return held[i, here]
            if dx == away:
                return face_ref[face_slot(kind, i, dx)]
            return held[i, near_plane]

        def row(kind, i, dx, dy, x=x, away=away, corner_ref=corner_ref):
            side = 0 if dy == -1 else 1
            if dx == away:
                line = corner_ref[2 * kind + side : 2 * kind + side + 1, :]
                if kind == 2:
                    line = line * (keep_low if side == 0 else keep_high)
                return line
            slot = MASK if kind == 2 else halo_slot(kind, i, dy)
            return halo_v[side, slot, x + dx : x + dx + 1, :]

        def mask(dx, x=x, away=away, face_ref=face_ref):
            if dx == away:
                return face_ref[MASK]
            return 1.0 - wall_ref[x + dx].astype(jnp.float32)

        magnet = magnet_ref[x]
        profile = profile_ref[x]
        plane_step(
            n,
            lambda i, dx, get=get: get(0, i, dx, post_v),
            lambda i, dx, dy, row=row: row(0, i, dx, dy),
            lambda i, dx, get=get: get(1, i, dx, adj_v),
            lambda i, dx, dy, row=row: row(1, i, dx, dy),
            mask,
            lambda dx, dy, row=row: row(2, 0, dx, dy),
            mask(0),
            gather_strength(table, magnet) * profile,
            profile,
            magnet,
            near_v,
            new_v,
            out_v,
            sums_v,
            count,
        )
        these = [
            pltpu.make_async_copy(new_v.at[pl.ds(0, NF), n], newf_ref.at[:, x], store_sem.at[n, 0]),
            pltpu.make_async_copy(new_v.at[pl.ds(NF, NG), n], newg_ref.at[:, x], store_sem.at[n, 1]),
            pltpu.make_async_copy(out_v.at[pl.ds(0, NF), n], outf_ref.at[:, x], store_sem.at[n, 2]),
            pltpu.make_async_copy(out_v.at[pl.ds(NF, NG), n], outg_ref.at[:, x], store_sem.at[n, 3]),
        ]
        start_all(these)
        stores += these
    rows = jnp.concatenate(
        [jnp.sum(sums_v[m], axis=0, keepdims=True) for m in range(count)], axis=0
    )
    share_ref[...] = lax.dot_general(
        jnp.ones((8, 128), jnp.float32),
        rows,
        (((1,), (1,)), ((), ())),
        precision=lax.Precision.HIGHEST,
        preferred_element_type=jnp.float32,
    )
    for c in stores:
        c.wait()


def outer_call(
    post, adjf, adjg, first, second, fromleft, fromright, cornerleft, cornerright, profile,
    strengths, wall, magnet, partial, newf, newg, outf, outg,
):
    sx, sy, sz = profile.shape
    count = strengths.shape[1]
    dma = pltpu.SemaphoreType.DMA
    return pl.pallas_call(
        outer_kernel,
        in_specs=[ANY] * 5 + [VMEM] * 9 + [ANY] * 4,
        out_specs=[ANY] * 4 + [VMEM],
        out_shape=[
            jax.ShapeDtypeStruct(adjf.shape, jnp.float32),
            jax.ShapeDtypeStruct(adjg.shape, jnp.float32),
            jax.ShapeDtypeStruct(adjf.shape, jnp.float32),
            jax.ShapeDtypeStruct(adjg.shape, jnp.float32),
            jax.ShapeDtypeStruct((8, count), jnp.float32),
        ],
        input_output_aliases={14: 0, 15: 1, 16: 2, 17: 3},
        scratch_shapes=[
            pltpu.VMEM((NP, 4, sy, sz), jnp.float32),
            pltpu.VMEM((NP, 4, sy, sz), jnp.float32),
            pltpu.VMEM((NP, 2, sy, sz), jnp.float32),
            pltpu.VMEM((NP, 2, sy, sz), jnp.float32),
            pltpu.VMEM((2, SLOTS, sx, sz), jnp.float32),
            pltpu.VMEM((18, sy, sz), jnp.float32),
            pltpu.VMEM((count, 8, 128), jnp.float32),
            dma((4,)),
            dma((4,)),
            dma((4,)),
            dma((2,)),
            dma((2, 4)),
        ],
        compiler_params=pltpu.CompilerParams(vmem_limit_bytes=51 << 20),
        name="outer",
    )(
        post, adjf, adjg, first, second, fromleft, fromright, cornerleft, cornerright, profile,
        strengths, wall, magnet, partial, newf, newg, outf, outg,
    )


def ring(count, step):
    return [(i, (i + step) % count) for i in range(count)]


def butterfly(value):
    for axis in ("gy", "gx"):
        count = lax.axis_size(axis)
        step = 1
        while step < count:
            value = value + lax.ppermute(value, axis, [(i, i ^ step) for i in range(count)])
            step *= 2
    return value


def on_device(flow, field, adj_flow_in, adj_field_in, profile, strengths, wall, magnet):
    across, around = lax.axis_size("gy"), lax.axis_size("gx")
    count = strengths.shape[0]
    table = strengths.reshape(1, count)
    post, mine1, mine2, right, left = collide_call(
        flow, field, adj_flow_in, adj_field_in, profile, table, wall, magnet
    )
    inside = [(i, i ^ 1) for i in range(across)]
    between = [(i, (((i + 1) ^ 1) - 1) % across) for i in range(across)]
    second = lax.ppermute(mine2, "gy", between)
    first = lax.ppermute(mine1, "gy", inside)
    fromleft = lax.ppermute(right, "gx", ring(around, 1))
    fromright = lax.ppermute(left, "gx", ring(around, -1))
    corner_r, corner_l = corner_call(first, second)
    cornerleft = lax.ppermute(corner_r, "gx", ring(around, 1))
    cornerright = lax.ppermute(corner_l, "gx", ring(around, -1))
    newf, newg, outf, outg, partial = inner_call(
        post, adj_flow_in, adj_field_in, first, second, profile, table, wall, magnet
    )
    newf, newg, outf, outg, share = outer_call(
        post, adj_flow_in, adj_field_in, first, second, fromleft, fromright, cornerleft,
        cornerright, profile, table, wall, magnet, partial, newf, newg, outf, outg,
    )
    cells = flow.shape[1] * around * flow.shape[2] * across * flow.shape[3]
    totals = butterfly(share[0])
    return (newf, newg, outf, outg, totals / math.sqrt(cells / count))


def solution(mesh):
    stack = P(None, "gx", "gy", None)
    cell = P("gx", "gy", None)
    return jax.shard_map(
        on_device,
        mesh=mesh,
        in_specs=(stack, stack, stack, stack, cell, P(), cell, cell),
        out_specs=(stack, stack, stack, stack, P()),
        check_vma=False,
    )
```

```python
import functools
import math

import jax
import jax.numpy as jnp
from jax import lax
from jax.experimental import pallas as pl
from jax.experimental.pallas import tpu as pltpu
from jax.sharding import PartitionSpec as P

LATTICE = [
    (0, 0, 0),
    (1, 0, 0),
    (-1, 0, 0),
    (0, 1, 0),
    (0, -1, 0),
    (0, 0, 1),
    (0, 0, -1),
    (1, 1, 0),
    (-1, -1, 0),
    (1, -1, 0),
    (-1, 1, 0),
    (1, 0, 1),
    (-1, 0, -1),
    (1, 0, -1),
    (-1, 0, 1),
    (0, 1, 1),
    (0, -1, -1),
    (0, 1, -1),
    (0, -1, 1),
]
NF, NG = 19, 7
NP = NF + NG
FIRST = [1, 3, 5, 7, 9, 11, 13, 15, 17]
W0, W1, W2 = 1.0 / 3.0, 1.0 / 18.0, 1.0 / 36.0
V0, V1 = 0.25, 0.125
PLUS = 0.625
MINUS = 0.5 / 1.125
TAU_PLUS = 0.8
COUPLE = 2.0
SOURCE = 2.0

UP = [3, 7, 10, 15, 17, NF + 3]
DOWN = [4, 8, 9, 16, 18, NF + 4]
RIGHT = [1, 7, 9, 11, 13, NF + 1]
LEFT = [2, 8, 10, 12, 14, NF + 2]
SLOTS = 13
MASK = 12


def weight(i):
    return W1 if i <= 6 else W2


def gather_strength(table, magnet):
    parts = [
        jnp.take_along_axis(table, magnet[:, z : z + 128], axis=1, mode="promise_in_bounds")
        for z in range(0, magnet.shape[1], 128)
    ]
    return jnp.concatenate(parts, axis=1)


def lane_table(strengths_ref):
    row = strengths_ref[...]
    rest = 128 - row.shape[1]
    if rest:
        row = jnp.concatenate([row, jnp.zeros((1, rest), jnp.float32)], axis=1)
    return jnp.broadcast_to(row, (8, 128))


def vector_sums(pair):
    x = pair[1] + pair[7] + pair[9] + pair[11] + pair[13]
    y = pair[3] + pair[7] - pair[9] + pair[15] + pair[17]
    z = pair[5] + pair[11] - pair[13] + pair[15] - pair[17]
    return x, y, z


def along(i, vx, vy, vz):
    out = None
    for c, v in zip(LATTICE[i], (vx, vy, vz)):
        if c:
            if out is None:
                out = v if c > 0 else -v
            else:
                out = out + v if c > 0 else out - v
    return out


def collide_kernel(
    planes,
    flow_ref,
    field_ref,
    adjf_ref,
    adjg_ref,
    profile_ref,
    strengths_ref,
    wall_ref,
    magnet_ref,
    post_ref,
    first_ref,
    second_ref,
    right_ref,
    left_ref,
):
    step = pl.program_id(0)
    steps = pl.num_programs(0)
    odd = lax.rem(lax.axis_index("gy"), 2)
    table = lane_table(strengths_ref)
    last = flow_ref.shape[2] - 1

    for p in range(planes):
        fluid = 1.0 - wall_ref[p].astype(jnp.float32)
        bcell = gather_strength(table, magnet_ref[p]) * profile_ref[p]
        f = [flow_ref[i, p] for i in range(NF)]
        g = [field_ref[k, p] for k in range(NG)]
        even = {i: f[i] + f[i + 1] for i in FIRST}
        diff = {i: f[i] - f[i + 1] for i in FIRST}
        rho = f[0] + (1.0 - fluid)
        for i in FIRST:
            rho = rho + even[i]
        momx, momy, momz = vector_sums(diff)
        inv = 1.0 / rho
        ux, uy, uz = momx * inv, momy * inv, momz * inv
        bval = g[0] + g[1] + g[2] + g[3] + g[4] + g[5] + g[6]
        current = (g[3] - g[4]) - bval * uy
        shear = (even[7] - even[9]) - momx * uy
        force = (COUPLE * bcell) * current
        vx = ux + TAU_PLUS * force * inv
        base = 1.0 - 1.5 * (vx * vx + uy * uy + uz * uz)
        post_ref[0, p] = f[0] - 2.0 * PLUS * (f[0] - (W0 * rho) * base)
        rho1, rho2 = W1 * rho, W2 * rho
        for i in FIRST:
            wr = rho1 if i <= 6 else rho2
            a = along(i, vx, uy, uz)
            ne = even[i] - (2.0 * wr) * (base + 4.5 * a * a)
            no = diff[i] - (6.0 * wr) * a
            ne = PLUS * ne
            no = MINUS * no
            post_ref[i, p] = f[i] - ne - no
            post_ref[i + 1, p] = f[i + 1] - ne + no
        common = bval + (SOURCE * bcell) * shear
        slope = 4.0 * bval
        post_ref[NF, p] = V0 * common
        for k, u in ((1, ux), (3, uy), (5, uz)):
            su = slope * u
            post_ref[NF + k, p] = V1 * (common + su)
            post_ref[NF + k + 1, p] = V1 * (common - su)

        x = step * planes + p
        here = pl.ds(x, 1)

        def adj_row(i, row):
            return adjf_ref[i, p, pl.ds(row, 1), :]

        for out, side in ((first_ref, odd), (second_ref, 1 - odd)):
            row = (1 - side) * last
            for s in range(6):
                up, down = UP[s], DOWN[s]
                out[s, here, :] = post_ref[up + side * (down - up), p, pl.ds(row, 1), :]
                if up < NF:
                    line = adjf_ref[down + side * (up - down), p, pl.ds(row, 1), :]
                else:
                    line = adjg_ref[down - NF + side * (up - down), p, pl.ds(row, 1), :]
                out[6 + s, here, :] = line
            out[MASK, here, :] = 1.0 - wall_ref[p, pl.ds(row, 1), :].astype(jnp.float32)

    def pack_x(out, p, posts, adjs):
        for s in range(6):
            out[s] = post_ref[posts[s], p]
            j = adjs[s]
            out[6 + s] = adjf_ref[j, p] if j < NF else adjg_ref[j - NF, p]
        out[MASK] = 1.0 - wall_ref[p].astype(jnp.float32)

    @pl.when(step == 0)
    def _():
        pack_x(left_ref, 0, LEFT, RIGHT)

    @pl.when(step == steps - 1)
    def _():
        pack_x(right_ref, planes - 1, RIGHT, LEFT)


def collide_call(flow, field, adjf, adjg, profile, strengths, wall, magnet, planes=2):
    sx, sy, sz = profile.shape
    grid = sx // planes

    def stack(n):
        return pl.BlockSpec((n, planes, sy, sz), lambda x: (0, x, 0, 0))

    one = pl.BlockSpec((planes, sy, sz), lambda x: (x, 0, 0))

    def whole(*shape):
        return pl.BlockSpec(shape, lambda x: (0,) * len(shape))

    rows = jax.ShapeDtypeStruct((SLOTS, sx, sz), jnp.float32)
    faces = jax.ShapeDtypeStruct((SLOTS, sy, sz), jnp.float32)
    return pl.pallas_call(
        functools.partial(collide_kernel, planes),
        grid=(grid,),
        in_specs=[
            stack(NF),
            stack(NG),
            stack(NF),
            stack(NG),
            one,
            whole(*strengths.shape),
            one,
            one,
        ],
        out_specs=[
            stack(NP),
            whole(*rows.shape),
            whole(*rows.shape),
            whole(*faces.shape),
            whole(*faces.shape),
        ],
        out_shape=[
            jax.ShapeDtypeStruct((NP, sx, sy, sz), jnp.float32),
            rows,
            rows,
            faces,
            faces,
        ],
        compiler_params=pltpu.CompilerParams(vmem_limit_bytes=62 << 20),
        name="collide",
    )(flow, field, adjf, adjg, profile, strengths, wall, magnet)


CORNER_RIGHT = ((0, 7, 0, 8), (1, 9, 1, 10))
CORNER_LEFT = ((0, 10, 0, 9), (1, 8, 1, 7))


def corner_slots(side, post, adj):
    posts, adjs = (UP, DOWN) if side == 0 else (DOWN, UP)
    return posts.index(post), 6 + adjs.index(adj), MASK


def corner_kernel(first_ref, second_ref, right_ref, left_ref):
    odd = lax.rem(lax.axis_index("gy"), 2) == 1
    sx = first_ref.shape[1]

    def row(side, slot, x):
        a, b = first_ref[slot, x : x + 1, :], second_ref[slot, x : x + 1, :]
        return jnp.where(odd, a, b) if side == 0 else jnp.where(odd, b, a)

    for out, table, x in ((right_ref, CORNER_RIGHT, sx - 1), (left_ref, CORNER_LEFT, 0)):
        out[...] = jnp.zeros_like(out)
        for side, post, _, adj in table:
            for n, slot in enumerate(corner_slots(side, post, adj)):
                out[2 * n + side : 2 * n + side + 1, :] = row(side, slot, x)


def corner_call(first, second):
    sz = first.shape[2]
    out = jax.ShapeDtypeStruct((8, sz), jnp.float32)
    return pl.pallas_call(corner_kernel, out_shape=[out, out], compiler_params=pltpu.CompilerParams(vmem_limit_bytes=2 << 20), name="corners")(first, second)


def plane_step(
    x_index, post, post_row, adj, adj_row, mask, mask_row, fluid, bcell, profile, magnet,
    near_ref, new_ref, out_ref, sums_ref, count,
):
    sy, sz = fluid.shape
    yi = lax.broadcasted_iota(jnp.int32, (sy, sz), 0)
    zi = lax.broadcasted_iota(jnp.int32, (sy, sz), 1)
    top, bottom = yi == sy - 1, yi == 0
    zlast, zfirst = zi == sz - 1, zi == 0

    def shift(value, row, dy, dz):
        if dy == -1:
            value = jnp.where(bottom, row(), pltpu.roll(value, 1, 0))
        elif dy == 1:
            value = jnp.where(top, row(), pltpu.roll(value, sy - 1, 0))
        if dz == -1:
            value = pltpu.roll(value, 1, 1)
        elif dz == 1:
            value = pltpu.roll(value, sz - 1, 1)
        return value

    def moved(get, get_row, i, sign):
        dx, dy, dz = (sign * c for c in LATTICE[i if i < NF else i - NF])
        return shift(get(i, dx), lambda: get_row(i, dx, dy), dy, dz)

    def near_of(i, sign):
        dx, dy, dz = (sign * c for c in LATTICE[i])
        value = shift(mask(dx), lambda: mask_row(dx, dy), dy, dz)
        if dz == -1:
            value = jnp.where(zfirst, 0.0, value)
        elif dz == 1:
            value = jnp.where(zlast, 0.0, value)
        return value

    for n, i in enumerate(FIRST):
        near_ref[2 * n] = near_of(i, -1)
        near_ref[2 * n + 1] = near_of(i, 1)

    def near(n):
        return near_ref[2 * n] > 0.5, near_ref[2 * n + 1] > 0.5

    def pull(i, n):
        minus, plus = near(n)
        a = fluid * jnp.where(minus, moved(post, post_row, i, -1), post(i + 1, 0))
        b = fluid * jnp.where(plus, moved(post, post_row, i + 1, -1), post(i, 0))
        new_ref[i, x_index] = a
        new_ref[i + 1, x_index] = b
        return a, b

    f0 = fluid * post(0, 0)
    new_ref[0, x_index] = f0
    rho = f0 + (1.0 - fluid)
    momx = momy = momz = shear0 = 0.0
    for n, i in enumerate(FIRST):
        a, b = pull(i, n)
        s, d = a + b, a - b
        rho = rho + s
        cx, cy, cz = LATTICE[i]
        if cx:
            momx = momx + d
        if cy:
            momy = momy + d if cy > 0 else momy - d
        if cz:
            momz = momz + d if cz > 0 else momz - d
        if cx and cy:
            shear0 = shear0 + s if cx * cy > 0 else shear0 - s
    g0 = fluid * post(NF, 0)
    new_ref[NF, x_index] = g0
    bval = g0
    gy = None
    for n, k in enumerate((1, 3, 5)):
        a, b = pull(NF + k, n)
        bval = bval + (a + b)
        if k == 3:
            gy = a - b
    inv = 1.0 / rho
    ux, uy, uz = momx * inv, momy * inv, momz * inv
    current = gy - bval * uy
    shear = shear0 - momx * uy
    force = (COUPLE * bcell) * current
    vx = ux + TAU_PLUS * force * inv

    def push(i, n):
        minus, plus = near(n)
        a = fluid * jnp.where(plus, moved(adj, adj_row, i, 1), adj(i + 1, 0))
        b = fluid * jnp.where(minus, moved(adj, adj_row, i + 1, 1), adj(i, 0))
        return a, b

    l0 = fluid * adj(0, 0)
    out_ref[0, x_index] = (1.0 - 2.0 * PLUS) * l0
    total = (2.0 * PLUS * W0) * l0
    m1 = [0.0, 0.0, 0.0]
    m2 = {}
    for n, i in enumerate(FIRST):
        a, b = push(i, n)
        s, d = a + b, a - b
        de = (0.5 - PLUS) * s
        do = (0.5 - MINUS) * d
        out_ref[i, x_index] = de + do
        out_ref[i + 1, x_index] = de - do
        w = weight(i)
        s = (2.0 * PLUS * w) * s
        d = (2.0 * MINUS * w) * d
        total = total + s
        c = LATTICE[i]
        for axis in range(3):
            if c[axis]:
                m1[axis] = m1[axis] + d if c[axis] > 0 else m1[axis] - d
            for other in range(axis, 3):
                sign = c[axis] * c[other]
                if sign:
                    old = m2.get((axis, other))
                    if old is None:
                        m2[axis, other] = s if sign > 0 else -s
                    else:
                        m2[axis, other] = old + s if sign > 0 else old - s
    h0 = fluid * adj(NF, 0)
    hsum = V0 * h0
    h1 = []
    hs = None
    for n, k in enumerate((1, 3, 5)):
        a, b = push(NF + k, n)
        hs = a + b if hs is None else hs + (a + b)
        h1.append(V1 * (a - b))
    hsum = hsum + V1 * hs

    base = 1.0 - 1.5 * (vx * vx + uy * uy + uz * uz)
    tx = m2[0, 0] * vx + m2[0, 1] * uy + m2[0, 2] * uz
    ty = m2[0, 1] * vx + m2[1, 1] * uy + m2[1, 2] * uz
    tz = m2[0, 2] * vx + m2[1, 2] * uy + m2[2, 2] * uz
    rhobar = (
        total * base
        + 4.5 * (vx * tx + uy * ty + uz * tz)
        + 3.0 * (m1[0] * vx + m1[1] * uy + m1[2] * uz)
    )
    total3 = 3.0 * total
    vxbar = rho * (9.0 * tx + 3.0 * m1[0] - total3 * vx)
    uybar = rho * (9.0 * ty + 3.0 * m1[1] - total3 * uy)
    uzbar = rho * (9.0 * tz + 3.0 * m1[2] - total3 * uz)
    slope = 4.0 * bval
    forcebar = (TAU_PLUS * vxbar) * inv
    rhobar = rhobar - forcebar * force * inv
    currentbar = (COUPLE * bcell) * forcebar
    shearbar = (SOURCE * bcell) * hsum
    dcell = COUPLE * current * forcebar + SOURCE * shear * hsum
    uxbar = vxbar + slope * h1[0]
    uybar = uybar + slope * h1[1] - bval * currentbar - momx * shearbar
    uzbar = uzbar + slope * h1[2]
    bbar = hsum + 4.0 * (h1[0] * ux + h1[1] * uy + h1[2] * uz) - uy * currentbar
    mxbar = uxbar * inv - uy * shearbar
    mybar = uybar * inv
    mzbar = uzbar * inv
    rhobar = rhobar - (ux * uxbar + uy * uybar + uz * uzbar) * inv

    out_ref[0, x_index] = out_ref[0, x_index] + rhobar
    for i in FIRST:
        cm = along(i, mxbar, mybar, mzbar)
        cx, cy, _ = LATTICE[i]
        common = rhobar
        if cx and cy:
            common = rhobar + shearbar if cx * cy > 0 else rhobar - shearbar
        out_ref[i, x_index] = out_ref[i, x_index] + (common + cm)
        out_ref[i + 1, x_index] = out_ref[i + 1, x_index] + (common - cm)
    for k in range(NG):
        value = bbar
        if k == 3:
            value = bbar + currentbar
        elif k == 4:
            value = bbar - currentbar
        out_ref[NF + k, x_index] = value

    share = dcell * profile
    for m in range(count):
        hit = jnp.where(magnet == m, share, 0.0)
        part = hit[:, 0:128]
        for z in range(128, sz, 128):
            part = part + hit[:, z : z + 128]
        sums_ref[m] = sums_ref[m] + part


def edges():
    here = lax.axis_index("gy")
    keep_low = jnp.where(here == 0, 0.0, 1.0)
    keep_high = jnp.where(here == lax.axis_size("gy") - 1, 0.0, 1.0)
    return keep_low, keep_high


def halo_slot(kind, i, dy):
    names = (UP, DOWN) if (dy == -1) == (kind == 0) else (DOWN, UP)
    return names[0].index(i) + 6 * kind


def face_slot(kind, i, dx):
    names = RIGHT if (dx == -1) == (kind == 0) else LEFT
    return names.index(i) + 6 * kind


def start_all(copies):
    for c in copies:
        c.start()


def load_halo(first_ref, second_ref, halo_ref, sem):
    odd = lax.rem(lax.axis_index("gy"), 2)
    return [
        pltpu.make_async_copy(first_ref, halo_ref.at[1 - odd], sem.at[0]),
        pltpu.make_async_copy(second_ref, halo_ref.at[odd], sem.at[1]),
    ]


def mask_halo(halo_ref):
    keep_low, keep_high = edges()
    halo_ref[0, MASK] = halo_ref[0, MASK] * keep_low
    halo_ref[1, MASK] = halo_ref[1, MASK] * keep_high


def inner_kernel(
    post_ref, adjf_ref, adjg_ref, first_ref, second_ref, profile_ref, strengths_ref, wall_ref,
    magnet_ref,
    newf_ref, newg_ref, outf_ref, outg_ref, sums_ref,
    post_v, adj_v, new_v, out_v, halo_v, near_v,
    post_sem, adjf_sem, adjg_sem, halo_sem, newf_sem, newg_sem, outf_sem, outg_sem,
):
    sx = post_v.shape[1]
    count = sums_ref.shape[0]

    def loads(x):
        return [
            pltpu.make_async_copy(post_ref.at[:, x], post_v.at[:, x], post_sem.at[x]),
            pltpu.make_async_copy(adjf_ref.at[:, x], adj_v.at[pl.ds(0, NF), x], adjf_sem.at[x]),
            pltpu.make_async_copy(adjg_ref.at[:, x], adj_v.at[pl.ds(NF, NG), x], adjg_sem.at[x]),
        ]

    def stores(x):
        return [
            pltpu.make_async_copy(new_v.at[pl.ds(0, NF), x], newf_ref.at[:, x], newf_sem.at[x]),
            pltpu.make_async_copy(new_v.at[pl.ds(NF, NG), x], newg_ref.at[:, x], newg_sem.at[x]),
            pltpu.make_async_copy(out_v.at[pl.ds(0, NF), x], outf_ref.at[:, x], outf_sem.at[x]),
            pltpu.make_async_copy(out_v.at[pl.ds(NF, NG), x], outg_ref.at[:, x], outg_sem.at[x]),
        ]

    def finish(copies):
        for c in copies:
            c.wait()

    halo = load_halo(first_ref, second_ref, halo_v, halo_sem)
    start_all(halo)
    for x in range(sx):
        start_all(loads(x))
    sums_ref[...] = jnp.zeros_like(sums_ref)
    table = lane_table(strengths_ref)
    finish(halo)
    mask_halo(halo_v)
    finish(loads(0))
    finish(loads(1))

    def body(x, carry):
        finish(loads(x + 1))

        def side(dy):
            return 0 if dy == -1 else 1

        def row_of(slot, dx, dy):
            return halo_v[side(dy), slot, pl.ds(x + dx, 1), :]

        def mask(dx):
            return 1.0 - wall_ref[x + dx].astype(jnp.float32)

        magnet = magnet_ref[x]
        profile = profile_ref[x]
        plane_step(
            x,
            lambda i, dx: post_v[i, x + dx],
            lambda i, dx, dy: row_of(halo_slot(0, i, dy), dx, dy),
            lambda i, dx: adj_v[i, x + dx],
            lambda i, dx, dy: row_of(halo_slot(1, i, dy), dx, dy),
            mask,
            lambda dx, dy: row_of(MASK, dx, dy),
            mask(0),
            gather_strength(table, magnet) * profile,
            profile,
            magnet,
            near_v,
            new_v,
            out_v,
            sums_ref,
            count,
        )
        start_all(stores(x))
        return carry

    lax.fori_loop(1, sx - 1, body, 0)
    for x in range(1, sx - 1):
        finish(stores(x))


ANY = pl.BlockSpec(memory_space=pl.ANY)
VMEM = pl.BlockSpec(memory_space=pltpu.VMEM)


def inner_call(post, adjf, adjg, first, second, profile, strengths, wall, magnet):
    sx, sy, sz = profile.shape
    count = strengths.shape[1]
    full = pltpu.VMEM((NP, sx, sy, sz), jnp.float32)
    dma = pltpu.SemaphoreType.DMA
    return pl.pallas_call(
        inner_kernel,
        in_specs=[ANY, ANY, ANY, ANY, ANY, VMEM, VMEM, VMEM, VMEM],
        out_specs=[ANY, ANY, ANY, ANY, VMEM],
        out_shape=[
            jax.ShapeDtypeStruct(adjf.shape, jnp.float32),
            jax.ShapeDtypeStruct(adjg.shape, jnp.float32),
            jax.ShapeDtypeStruct(adjf.shape, jnp.float32),
            jax.ShapeDtypeStruct(adjg.shape, jnp.float32),
            jax.ShapeDtypeStruct((count, 8, 128), jnp.float32),
        ],
        scratch_shapes=[
            full,
            full,
            full,
            full,
            pltpu.VMEM((2, SLOTS, sx, sz), jnp.float32),
            pltpu.VMEM((18, sy, sz), jnp.float32),
            dma((sx,)),
            dma((sx,)),
            dma((sx,)),
            dma((2,)),
            dma((sx,)),
            dma((sx,)),
            dma((sx,)),
            dma((sx,)),
        ],
        compiler_params=pltpu.CompilerParams(vmem_limit_bytes=51 << 20),
        cost_estimate=pl.CostEstimate(
            flops=700 * sx * sy * sz, bytes_accessed=16 * NP * sx * sy * sz, transcendentals=0
        ),
        name="inner",
    )(post, adjf, adjg, first, second, profile, strengths, wall, magnet)


def outer_kernel(
    post_ref, adjf_ref, adjg_ref, first_ref, second_ref, fromleft_ref, fromright_ref,
    cornerleft_ref, cornerright_ref, profile_ref, strengths_ref, wall_ref, magnet_ref,
    partial_ref, newf_in, newg_in, outf_in, outg_in,
    newf_ref, newg_ref, outf_ref, outg_ref, share_ref,
    post_v, adj_v, new_v, out_v, halo_v, near_v, sums_v,
    post_sem, adjf_sem, adjg_sem, halo_sem, store_sem,
):
    del newf_in, newg_in, outf_in, outg_in
    sx = wall_ref.shape[0]
    count = sums_v.shape[0]
    from_planes = (0, 1, sx - 2, sx - 1)
    loads = []
    for n, x in enumerate(from_planes):
        loads += [
            pltpu.make_async_copy(post_ref.at[:, x], post_v.at[:, n], post_sem.at[n]),
            pltpu.make_async_copy(adjf_ref.at[:, x], adj_v.at[pl.ds(0, NF), n], adjf_sem.at[n]),
            pltpu.make_async_copy(adjg_ref.at[:, x], adj_v.at[pl.ds(NF, NG), n], adjg_sem.at[n]),
        ]
    halo = load_halo(first_ref, second_ref, halo_v, halo_sem)
    start_all(halo)
    start_all(loads)
    sums_v[...] = partial_ref[...]
    table = lane_table(strengths_ref)
    keep_low, keep_high = edges()
    for c in halo:
        c.wait()
    mask_halo(halo_v)
    stores = []
    for n, (x, away, here, near_plane) in enumerate(((0, -1, 0, 1), (sx - 1, 1, 3, 2))):
        for c in loads[6 * n : 6 * n + 6]:
            c.wait()
        face_ref, corner_ref = (
            (fromleft_ref, cornerleft_ref) if away == -1 else (fromright_ref, cornerright_ref)
        )

        def get(kind, i, dx, held, here=here, near_plane=near_plane, away=away, face_ref=face_ref):
            if dx == 0:
                return held[i, here]
            if dx == away:
                return face_ref[face_slot(kind, i, dx)]
            return held[i, near_plane]

        def row(kind, i, dx, dy, x=x, away=away, corner_ref=corner_ref):
            side = 0 if dy == -1 else 1
            if dx == away:
                line = corner_ref[2 * kind + side : 2 * kind + side + 1, :]
                if kind == 2:
                    line = line * (keep_low if side == 0 else keep_high)
                return line
            slot = MASK if kind == 2 else halo_slot(kind, i, dy)
            return halo_v[side, slot, x + dx : x + dx + 1, :]

        def mask(dx, x=x, away=away, face_ref=face_ref):
            if dx == away:
                return face_ref[MASK]
            return 1.0 - wall_ref[x + dx].astype(jnp.float32)

        magnet = magnet_ref[x]
        profile = profile_ref[x]
        plane_step(
            n,
            lambda i, dx, get=get: get(0, i, dx, post_v),
            lambda i, dx, dy, row=row: row(0, i, dx, dy),
            lambda i, dx, get=get: get(1, i, dx, adj_v),
            lambda i, dx, dy, row=row: row(1, i, dx, dy),
            mask,
            lambda dx, dy, row=row: row(2, 0, dx, dy),
            mask(0),
            gather_strength(table, magnet) * profile,
            profile,
            magnet,
            near_v,
            new_v,
            out_v,
            sums_v,
            count,
        )
        these = [
            pltpu.make_async_copy(new_v.at[pl.ds(0, NF), n], newf_ref.at[:, x], store_sem.at[n, 0]),
            pltpu.make_async_copy(new_v.at[pl.ds(NF, NG), n], newg_ref.at[:, x], store_sem.at[n, 1]),
            pltpu.make_async_copy(out_v.at[pl.ds(0, NF), n], outf_ref.at[:, x], store_sem.at[n, 2]),
            pltpu.make_async_copy(out_v.at[pl.ds(NF, NG), n], outg_ref.at[:, x], store_sem.at[n, 3]),
        ]
        start_all(these)
        stores += these
    rows = jnp.concatenate(
        [jnp.sum(sums_v[m], axis=0, keepdims=True) for m in range(count)], axis=0
    )
    share_ref[...] = lax.dot_general(
        jnp.ones((share_ref.shape[0], 128), jnp.float32),
        rows,
        (((1,), (1,)), ((), ())),
        precision=lax.Precision.HIGHEST,
        preferred_element_type=jnp.float32,
    )
    for c in stores:
        c.wait()


def outer_call(
    post, adjf, adjg, first, second, fromleft, fromright, cornerleft, cornerright, profile,
    strengths, wall, magnet, partial, newf, newg, outf, outg,
):
    sx, sy, sz = profile.shape
    count = strengths.shape[1]
    dma = pltpu.SemaphoreType.DMA
    return pl.pallas_call(
        outer_kernel,
        in_specs=[ANY] * 5 + [VMEM] * 9 + [ANY] * 4,
        out_specs=[ANY] * 4 + [VMEM],
        out_shape=[
            jax.ShapeDtypeStruct(adjf.shape, jnp.float32),
            jax.ShapeDtypeStruct(adjg.shape, jnp.float32),
            jax.ShapeDtypeStruct(adjf.shape, jnp.float32),
            jax.ShapeDtypeStruct(adjg.shape, jnp.float32),
            jax.ShapeDtypeStruct((lax.axis_size(("gx", "gy")), count), jnp.float32),
        ],
        input_output_aliases={14: 0, 15: 1, 16: 2, 17: 3},
        scratch_shapes=[
            pltpu.VMEM((NP, 4, sy, sz), jnp.float32),
            pltpu.VMEM((NP, 4, sy, sz), jnp.float32),
            pltpu.VMEM((NP, 2, sy, sz), jnp.float32),
            pltpu.VMEM((NP, 2, sy, sz), jnp.float32),
            pltpu.VMEM((2, SLOTS, sx, sz), jnp.float32),
            pltpu.VMEM((18, sy, sz), jnp.float32),
            pltpu.VMEM((count, 8, 128), jnp.float32),
            dma((4,)),
            dma((4,)),
            dma((4,)),
            dma((2,)),
            dma((2, 4)),
        ],
        compiler_params=pltpu.CompilerParams(vmem_limit_bytes=51 << 20),
        name="outer",
    )(
        post, adjf, adjg, first, second, fromleft, fromright, cornerleft, cornerright, profile,
        strengths, wall, magnet, partial, newf, newg, outf, outg,
    )


def ring(count, step):
    return [(i, (i + step) % count) for i in range(count)]


def on_device(flow, field, adj_flow_in, adj_field_in, profile, strengths, wall, magnet):
    across, around = lax.axis_size("gy"), lax.axis_size("gx")
    count = strengths.shape[0]
    table = strengths.reshape(1, count)
    post, mine1, mine2, right, left = collide_call(
        flow, field, adj_flow_in, adj_field_in, profile, table, wall, magnet
    )
    inside = [(i, i ^ 1) for i in range(across)]
    between = [(i, (((i + 1) ^ 1) - 1) % across) for i in range(across)]
    second = lax.ppermute(mine2, "gy", between)
    first = lax.ppermute(mine1, "gy", inside)
    fromleft = lax.ppermute(right, "gx", ring(around, 1))
    fromright = lax.ppermute(left, "gx", ring(around, -1))
    corner_r, corner_l = corner_call(first, second)
    cornerleft = lax.ppermute(corner_r, "gx", ring(around, 1))
    cornerright = lax.ppermute(corner_l, "gx", ring(around, -1))
    newf, newg, outf, outg, partial = inner_call(
        post, adj_flow_in, adj_field_in, first, second, profile, table, wall, magnet
    )
    newf, newg, outf, outg, share = outer_call(
        post, adj_flow_in, adj_field_in, first, second, fromleft, fromright, cornerleft,
        cornerright, profile, table, wall, magnet, partial, newf, newg, outf, outg,
    )
    cells = flow.shape[1] * around * flow.shape[2] * across * flow.shape[3]
    totals = jnp.sum(lax.all_to_all(share, ("gx", "gy"), 0, 0, tiled=True), axis=0)
    return (newf, newg, outf, outg, totals / math.sqrt(cells / count))


def solution(mesh):
    stack = P(None, "gx", "gy", None)
    cell = P("gx", "gy", None)
    return jax.shard_map(
        on_device,
        mesh=mesh,
        in_specs=(stack, stack, stack, stack, cell, P(), cell, cell),
        out_specs=(stack, stack, stack, stack, P()),
        check_vma=False,
    )
```

```python
import functools
import math

import jax
import jax.numpy as jnp
from jax import lax
from jax.experimental import pallas as pl
from jax.experimental.pallas import tpu as pltpu
from jax.sharding import PartitionSpec as P

LATTICE = [
    (0, 0, 0),
    (1, 0, 0),
    (-1, 0, 0),
    (0, 1, 0),
    (0, -1, 0),
    (0, 0, 1),
    (0, 0, -1),
    (1, 1, 0),
    (-1, -1, 0),
    (1, -1, 0),
    (-1, 1, 0),
    (1, 0, 1),
    (-1, 0, -1),
    (1, 0, -1),
    (-1, 0, 1),
    (0, 1, 1),
    (0, -1, -1),
    (0, 1, -1),
    (0, -1, 1),
]
NF, NG = 19, 7
NP = NF + NG
FIRST = [1, 3, 5, 7, 9, 11, 13, 15, 17]
W0, W1, W2 = 1.0 / 3.0, 1.0 / 18.0, 1.0 / 36.0
V0, V1 = 0.25, 0.125
PLUS = 0.625
MINUS = 0.5 / 1.125
TAU_PLUS = 0.8
COUPLE = 2.0
SOURCE = 2.0

UP = [3, 7, 10, 15, 17, NF + 3]
DOWN = [4, 8, 9, 16, 18, NF + 4]
RIGHT = [1, 7, 9, 11, 13, NF + 1]
LEFT = [2, 8, 10, 12, 14, NF + 2]
SLOTS = 13
MASK = 12

COLLIDE_VMEM = 48 << 20
INNER_VMEM = 42 << 20
OUTER_VMEM = 42 << 20


def weight(i):
    return W1 if i <= 6 else W2


def gather_strength(table, magnet):
    parts = [
        jnp.take_along_axis(table, magnet[:, z : z + 128], axis=1, mode="promise_in_bounds")
        for z in range(0, magnet.shape[1], 128)
    ]
    return jnp.concatenate(parts, axis=1)


def lane_table(strengths_ref):
    row = strengths_ref[...]
    rest = 128 - row.shape[1]
    if rest:
        row = jnp.concatenate([row, jnp.zeros((1, rest), jnp.float32)], axis=1)
    return jnp.broadcast_to(row, (8, 128))


def vector_sums(pair):
    x = pair[1] + pair[7] + pair[9] + pair[11] + pair[13]
    y = pair[3] + pair[7] - pair[9] + pair[15] + pair[17]
    z = pair[5] + pair[11] - pair[13] + pair[15] - pair[17]
    return x, y, z


def along(i, vx, vy, vz):
    out = None
    for c, v in zip(LATTICE[i], (vx, vy, vz)):
        if c:
            if out is None:
                out = v if c > 0 else -v
            else:
                out = out + v if c > 0 else out - v
    return out


def start_all(copies):
    for c in copies:
        c.start()


def wait_all(copies):
    for c in copies:
        c.wait()


def collide_kernel(
    flow_ref, field_ref, adjf_ref, adjg_ref, profile_ref, strengths_ref, wall_ref, magnet_ref,
    post_ref, adj_ref, fluid_ref, bcell_ref, profile_v, magnet_v, first_ref, second_ref, right_ref,
    left_ref,
    flow_v, field_v, wall_v, plane_sem, adj_sem,
):
    sx, sy = fluid_ref.shape[:2]
    odd = lax.rem(lax.axis_index("gy"), 2)

    def loads(x):
        pairs = (
            (wall_ref.at[x], wall_v.at[x]),
            (magnet_ref.at[x], magnet_v.at[x]),
            (profile_ref.at[x], profile_v.at[x]),
            (flow_ref.at[:, x], flow_v.at[:, x]),
            (field_ref.at[:, x], field_v.at[:, x]),
        )
        return [pltpu.make_async_copy(a, b, plane_sem.at[n, x]) for n, (a, b) in enumerate(pairs)]

    for x in range(sx):
        start_all(loads(x))
    adj_loads = [
        pltpu.make_async_copy(adjf_ref, adj_ref.at[pl.ds(0, NF)], adj_sem.at[0]),
        pltpu.make_async_copy(adjg_ref, adj_ref.at[pl.ds(NF, NG)], adj_sem.at[1]),
    ]
    start_all(adj_loads)
    table = lane_table(strengths_ref)

    def body(x, carry):
        wait_all(loads(x))
        fluid = 1.0 - wall_v[x].astype(jnp.float32)
        bcell = gather_strength(table, magnet_v[x]) * profile_v[x]
        fluid_ref[x] = fluid
        bcell_ref[x] = bcell
        f = [flow_v[i, x] for i in range(NF)]
        g = [field_v[k, x] for k in range(NG)]
        even = {i: f[i] + f[i + 1] for i in FIRST}
        diff = {i: f[i] - f[i + 1] for i in FIRST}
        rho = f[0] + (1.0 - fluid)
        for i in FIRST:
            rho = rho + even[i]
        momx, momy, momz = vector_sums(diff)
        inv = 1.0 / rho
        ux, uy, uz = momx * inv, momy * inv, momz * inv
        bval = g[0] + g[1] + g[2] + g[3] + g[4] + g[5] + g[6]
        current = (g[3] - g[4]) - bval * uy
        shear = (even[7] - even[9]) - momx * uy
        force = (COUPLE * bcell) * current
        vx = ux + TAU_PLUS * force * inv
        base = 1.0 - 1.5 * (vx * vx + uy * uy + uz * uz)
        post_ref[0, x] = f[0] - 2.0 * PLUS * (f[0] - (W0 * rho) * base)
        rho1, rho2 = W1 * rho, W2 * rho
        for i in FIRST:
            wr = rho1 if i <= 6 else rho2
            a = along(i, vx, uy, uz)
            ne = even[i] - (2.0 * wr) * (base + 4.5 * a * a)
            no = diff[i] - (6.0 * wr) * a
            ne = PLUS * ne
            no = MINUS * no
            post_ref[i, x] = f[i] - ne - no
            post_ref[i + 1, x] = f[i + 1] - ne + no
        common = bval + (SOURCE * bcell) * shear
        slope = 4.0 * bval
        post_ref[NF, x] = V0 * common
        for k, u in ((1, ux), (3, uy), (5, uz)):
            su = slope * u
            post_ref[NF + k, x] = V1 * (common + su)
            post_ref[NF + k + 1, x] = V1 * (common - su)
        return carry

    lax.fori_loop(0, sx, body, 0)

    wait_all(adj_loads)

    def pack(x, carry):
        here = pl.ds(x, 1)
        for out, side in ((first_ref, odd), (second_ref, 1 - odd)):
            line = pl.ds((1 - side) * (sy - 1), 1)
            for s in range(6):
                up, down = UP[s], DOWN[s]
                out[s, here, :] = post_ref[up + side * (down - up), x, line, :]
                out[6 + s, here, :] = adj_ref[down + side * (up - down), x, line, :]
            out[MASK, here, :] = fluid_ref[x, line, :]
        return carry

    lax.fori_loop(0, sx, pack, 0)
    for out, x, posts, adjs in ((left_ref, 0, LEFT, RIGHT), (right_ref, sx - 1, RIGHT, LEFT)):
        for s in range(6):
            out[s] = post_ref[posts[s], x]
            out[6 + s] = adj_ref[adjs[s], x]
        out[MASK] = fluid_ref[x]


ANY = pl.BlockSpec(memory_space=pl.ANY)
VMEM = pl.BlockSpec(memory_space=pltpu.VMEM)


def collide_call(flow, field, adjf, adjg, profile, strengths, wall, magnet):
    sx, sy, sz = profile.shape
    full = pltpu.VMEM((NP, sx, sy, sz), jnp.float32)
    cells = pltpu.VMEM((sx, sy, sz), jnp.float32)
    names = pltpu.VMEM((sx, sy, sz), jnp.int32)
    rows = pltpu.VMEM((SLOTS, sx, sz), jnp.float32)
    faces = pltpu.VMEM((SLOTS, sy, sz), jnp.float32)
    dma = pltpu.SemaphoreType.DMA
    return pl.pallas_call(
        collide_kernel,
        in_specs=[ANY, ANY, ANY, ANY, ANY, VMEM, ANY, ANY],
        out_specs=[VMEM] * 10,
        out_shape=[full, full, cells, cells, cells, names, rows, rows, faces, faces],
        scratch_shapes=[
            pltpu.VMEM(flow.shape, jnp.float32),
            pltpu.VMEM(field.shape, jnp.float32),
            names,
            dma((5, sx)),
            dma((2,)),
        ],
        compiler_params=pltpu.CompilerParams(vmem_limit_bytes=COLLIDE_VMEM),
        name="collide",
    )(flow, field, adjf, adjg, profile, strengths, wall, magnet)


CORNER_RIGHT = ((0, 7, 0, 8), (1, 9, 1, 10))
CORNER_LEFT = ((0, 10, 0, 9), (1, 8, 1, 7))


def corner_slots(side, post, adj):
    posts, adjs = (UP, DOWN) if side == 0 else (DOWN, UP)
    return posts.index(post), 6 + adjs.index(adj), MASK


def corner_kernel(first_ref, second_ref, right_ref, left_ref):
    odd = lax.rem(lax.axis_index("gy"), 2) == 1
    sx = first_ref.shape[1]

    def row(side, slot, x):
        a, b = first_ref[slot, x : x + 1, :], second_ref[slot, x : x + 1, :]
        return jnp.where(odd, a, b) if side == 0 else jnp.where(odd, b, a)

    for out, table, x in ((right_ref, CORNER_RIGHT, sx - 1), (left_ref, CORNER_LEFT, 0)):
        out[...] = jnp.zeros_like(out)
        for side, post, _, adj in table:
            for n, slot in enumerate(corner_slots(side, post, adj)):
                out[2 * n + side : 2 * n + side + 1, :] = row(side, slot, x)


def corner_call(first, second):
    sz = first.shape[2]
    out = jax.ShapeDtypeStruct((8, sz), jnp.float32)
    return pl.pallas_call(corner_kernel, out_shape=[out, out], compiler_params=pltpu.CompilerParams(vmem_limit_bytes=2 << 20), name="corners")(first, second)


def plane_step(
    x_index, post, post_row, adj, adj_row, mask, mask_row, fluid, bcell, profile, magnet,
    near_ref, new_ref, out_ref, sums_ref, count,
):
    sy, sz = fluid.shape
    yi = lax.broadcasted_iota(jnp.int32, (sy, sz), 0)
    zi = lax.broadcasted_iota(jnp.int32, (sy, sz), 1)
    top, bottom = yi == sy - 1, yi == 0
    zlast, zfirst = zi == sz - 1, zi == 0

    def shift(value, row, dy, dz):
        if dy == -1:
            value = jnp.where(bottom, row(), pltpu.roll(value, 1, 0))
        elif dy == 1:
            value = jnp.where(top, row(), pltpu.roll(value, sy - 1, 0))
        if dz == -1:
            value = pltpu.roll(value, 1, 1)
        elif dz == 1:
            value = pltpu.roll(value, sz - 1, 1)
        return value

    def moved(get, get_row, i, sign):
        dx, dy, dz = (sign * c for c in LATTICE[i if i < NF else i - NF])
        return shift(get(i, dx), lambda: get_row(i, dx, dy), dy, dz)

    def near_of(i, sign):
        dx, dy, dz = (sign * c for c in LATTICE[i])
        value = shift(mask(dx), lambda: mask_row(dx, dy), dy, dz)
        if dz == -1:
            value = jnp.where(zfirst, 0.0, value)
        elif dz == 1:
            value = jnp.where(zlast, 0.0, value)
        return value

    for n, i in enumerate(FIRST):
        near_ref[2 * n] = near_of(i, -1)
        near_ref[2 * n + 1] = near_of(i, 1)

    def near(n):
        return near_ref[2 * n] > 0.5, near_ref[2 * n + 1] > 0.5

    def pull(i, n):
        minus, plus = near(n)
        a = fluid * jnp.where(minus, moved(post, post_row, i, -1), post(i + 1, 0))
        b = fluid * jnp.where(plus, moved(post, post_row, i + 1, -1), post(i, 0))
        new_ref[i, x_index] = a
        new_ref[i + 1, x_index] = b
        return a, b

    f0 = fluid * post(0, 0)
    new_ref[0, x_index] = f0
    rho = f0 + (1.0 - fluid)
    momx = momy = momz = shear0 = 0.0
    for n, i in enumerate(FIRST):
        a, b = pull(i, n)
        s, d = a + b, a - b
        rho = rho + s
        cx, cy, cz = LATTICE[i]
        if cx:
            momx = momx + d
        if cy:
            momy = momy + d if cy > 0 else momy - d
        if cz:
            momz = momz + d if cz > 0 else momz - d
        if cx and cy:
            shear0 = shear0 + s if cx * cy > 0 else shear0 - s
    g0 = fluid * post(NF, 0)
    new_ref[NF, x_index] = g0
    bval = g0
    gy = None
    for n, k in enumerate((1, 3, 5)):
        a, b = pull(NF + k, n)
        bval = bval + (a + b)
        if k == 3:
            gy = a - b
    inv = 1.0 / rho
    ux, uy, uz = momx * inv, momy * inv, momz * inv
    current = gy - bval * uy
    shear = shear0 - momx * uy
    force = (COUPLE * bcell) * current
    vx = ux + TAU_PLUS * force * inv

    def push(i, n):
        minus, plus = near(n)
        a = fluid * jnp.where(plus, moved(adj, adj_row, i, 1), adj(i + 1, 0))
        b = fluid * jnp.where(minus, moved(adj, adj_row, i + 1, 1), adj(i, 0))
        return a, b

    l0 = fluid * adj(0, 0)
    out_ref[0, x_index] = (1.0 - 2.0 * PLUS) * l0
    total = (2.0 * PLUS * W0) * l0
    m1 = [0.0, 0.0, 0.0]
    m2 = {}
    for n, i in enumerate(FIRST):
        a, b = push(i, n)
        s, d = a + b, a - b
        de = (0.5 - PLUS) * s
        do = (0.5 - MINUS) * d
        out_ref[i, x_index] = de + do
        out_ref[i + 1, x_index] = de - do
        w = weight(i)
        s = (2.0 * PLUS * w) * s
        d = (2.0 * MINUS * w) * d
        total = total + s
        c = LATTICE[i]
        for axis in range(3):
            if c[axis]:
                m1[axis] = m1[axis] + d if c[axis] > 0 else m1[axis] - d
            for other in range(axis, 3):
                sign = c[axis] * c[other]
                if sign:
                    old = m2.get((axis, other))
                    if old is None:
                        m2[axis, other] = s if sign > 0 else -s
                    else:
                        m2[axis, other] = old + s if sign > 0 else old - s
    h0 = fluid * adj(NF, 0)
    hsum = V0 * h0
    h1 = []
    hs = None
    for n, k in enumerate((1, 3, 5)):
        a, b = push(NF + k, n)
        hs = a + b if hs is None else hs + (a + b)
        h1.append(V1 * (a - b))
    hsum = hsum + V1 * hs

    base = 1.0 - 1.5 * (vx * vx + uy * uy + uz * uz)
    tx = m2[0, 0] * vx + m2[0, 1] * uy + m2[0, 2] * uz
    ty = m2[0, 1] * vx + m2[1, 1] * uy + m2[1, 2] * uz
    tz = m2[0, 2] * vx + m2[1, 2] * uy + m2[2, 2] * uz
    rhobar = (
        total * base
        + 4.5 * (vx * tx + uy * ty + uz * tz)
        + 3.0 * (m1[0] * vx + m1[1] * uy + m1[2] * uz)
    )
    total3 = 3.0 * total
    vxbar = rho * (9.0 * tx + 3.0 * m1[0] - total3 * vx)
    uybar = rho * (9.0 * ty + 3.0 * m1[1] - total3 * uy)
    uzbar = rho * (9.0 * tz + 3.0 * m1[2] - total3 * uz)
    slope = 4.0 * bval
    forcebar = (TAU_PLUS * vxbar) * inv
    rhobar = rhobar - forcebar * force * inv
    currentbar = (COUPLE * bcell) * forcebar
    shearbar = (SOURCE * bcell) * hsum
    dcell = COUPLE * current * forcebar + SOURCE * shear * hsum
    uxbar = vxbar + slope * h1[0]
    uybar = uybar + slope * h1[1] - bval * currentbar - momx * shearbar
    uzbar = uzbar + slope * h1[2]
    bbar = hsum + 4.0 * (h1[0] * ux + h1[1] * uy + h1[2] * uz) - uy * currentbar
    mxbar = uxbar * inv - uy * shearbar
    mybar = uybar * inv
    mzbar = uzbar * inv
    rhobar = rhobar - (ux * uxbar + uy * uybar + uz * uzbar) * inv

    out_ref[0, x_index] = out_ref[0, x_index] + rhobar
    for i in FIRST:
        cm = along(i, mxbar, mybar, mzbar)
        cx, cy, _ = LATTICE[i]
        common = rhobar
        if cx and cy:
            common = rhobar + shearbar if cx * cy > 0 else rhobar - shearbar
        out_ref[i, x_index] = out_ref[i, x_index] + (common + cm)
        out_ref[i + 1, x_index] = out_ref[i + 1, x_index] + (common - cm)
    for k in range(NG):
        value = bbar
        if k == 3:
            value = bbar + currentbar
        elif k == 4:
            value = bbar - currentbar
        out_ref[NF + k, x_index] = value

    share = dcell * profile
    for m in range(count):
        hit = jnp.where(magnet == m, share, 0.0)
        part = hit[:, 0:128]
        for z in range(128, sz, 128):
            part = part + hit[:, z : z + 128]
        sums_ref[m] = sums_ref[m] + part


def halo_slot(kind, i, dy):
    names = (UP, DOWN) if (dy == -1) == (kind == 0) else (DOWN, UP)
    return names[0].index(i) + 6 * kind


def face_slot(kind, i, dx):
    names = RIGHT if (dx == -1) == (kind == 0) else LEFT
    return names.index(i) + 6 * kind


def load_halo(first_ref, second_ref, halo_ref):
    odd = lax.rem(lax.axis_index("gy"), 2)
    halo_ref[1 - odd] = first_ref[...]
    halo_ref[odd] = second_ref[...]
    here = lax.axis_index("gy")
    keep_low = jnp.where(here == 0, 0.0, 1.0)
    keep_high = jnp.where(here == lax.axis_size("gy") - 1, 0.0, 1.0)
    halo_ref[0, MASK] = halo_ref[0, MASK] * keep_low
    halo_ref[1, MASK] = halo_ref[1, MASK] * keep_high
    return keep_low, keep_high


def plane_stores(n, x, new_v, out_v, newf_ref, newg_ref, outf_ref, outg_ref, sem):
    pairs = (
        (new_v.at[pl.ds(0, NF), n], newf_ref.at[:, x]),
        (new_v.at[pl.ds(NF, NG), n], newg_ref.at[:, x]),
        (out_v.at[pl.ds(0, NF), n], outf_ref.at[:, x]),
        (out_v.at[pl.ds(NF, NG), n], outg_ref.at[:, x]),
    )
    return [pltpu.make_async_copy(a, b, sem.at[k, n]) for k, (a, b) in enumerate(pairs)]


def inner_kernel(
    post_ref, adj_ref, fluid_ref, bcell_ref, first_ref, second_ref, profile_ref, magnet_ref,
    newf_ref, newg_ref, outf_ref, outg_ref, sums_ref,
    new_v, out_v, halo_v, near_v, store_sem,
):
    sx = fluid_ref.shape[0]
    count = sums_ref.shape[0]

    def stores(x):
        return plane_stores(
            x, x, new_v, out_v, newf_ref, newg_ref, outf_ref, outg_ref, store_sem
        )

    sums_ref[...] = jnp.zeros_like(sums_ref)
    load_halo(first_ref, second_ref, halo_v)

    def body(x, carry):
        def row_of(slot, dx, dy):
            return halo_v[0 if dy == -1 else 1, slot, pl.ds(x + dx, 1), :]

        plane_step(
            x,
            lambda i, dx: post_ref[i, x + dx],
            lambda i, dx, dy: row_of(halo_slot(0, i, dy), dx, dy),
            lambda i, dx: adj_ref[i, x + dx],
            lambda i, dx, dy: row_of(halo_slot(1, i, dy), dx, dy),
            lambda dx: fluid_ref[x + dx],
            lambda dx, dy: row_of(MASK, dx, dy),
            fluid_ref[x],
            bcell_ref[x],
            profile_ref[x],
            magnet_ref[x],
            near_v,
            new_v,
            out_v,
            sums_ref,
            count,
        )
        start_all(stores(x))
        return carry

    lax.fori_loop(1, sx - 1, body, 0)
    for x in range(1, sx - 1):
        wait_all(stores(x))


def inner_call(post, adj, fluid, bcell, first, second, profile, magnet, count):
    sx, sy, sz = profile.shape
    full = pltpu.VMEM((NP, sx, sy, sz), jnp.float32)
    flow = jax.ShapeDtypeStruct((NF, sx, sy, sz), jnp.float32)
    field = jax.ShapeDtypeStruct((NG, sx, sy, sz), jnp.float32)
    return pl.pallas_call(
        inner_kernel,
        in_specs=[VMEM] * 8,
        out_specs=[ANY, ANY, ANY, ANY, VMEM],
        out_shape=[flow, field, flow, field, pltpu.VMEM((count, 8, 128), jnp.float32)],
        scratch_shapes=[
            full,
            full,
            pltpu.VMEM((2, SLOTS, sx, sz), jnp.float32),
            pltpu.VMEM((18, sy, sz), jnp.float32),
            pltpu.SemaphoreType.DMA((4, sx)),
        ],
        compiler_params=pltpu.CompilerParams(vmem_limit_bytes=INNER_VMEM),
        cost_estimate=pl.CostEstimate(
            flops=700 * sx * sy * sz, bytes_accessed=16 * NP * sx * sy * sz, transcendentals=0
        ),
        name="inner",
    )(post, adj, fluid, bcell, first, second, profile, magnet)


def outer_kernel(
    post_ref, adj_ref, fluid_ref, bcell_ref, first_ref, second_ref, fromleft_ref, fromright_ref,
    cornerleft_ref, cornerright_ref, profile_ref, magnet_ref,
    partial_ref, newf_in, newg_in, outf_in, outg_in,
    newf_ref, newg_ref, outf_ref, outg_ref, share_ref,
    new_v, out_v, halo_v, near_v, sums_v, store_sem,
):
    del newf_in, newg_in, outf_in, outg_in
    sx = fluid_ref.shape[0]
    count = sums_v.shape[0]
    sums_v[...] = partial_ref[...]
    keep_low, keep_high = load_halo(first_ref, second_ref, halo_v)
    stores = []
    for n, (x, away) in enumerate(((0, -1), (sx - 1, 1))):
        face_ref, corner_ref = (
            (fromleft_ref, cornerleft_ref) if away == -1 else (fromright_ref, cornerright_ref)
        )

        def get(kind, i, dx, held, x=x, away=away, face_ref=face_ref):
            if dx == away:
                return face_ref[face_slot(kind, i, dx)]
            return held[i, x + dx]

        def row(kind, i, dx, dy, x=x, away=away, corner_ref=corner_ref):
            side = 0 if dy == -1 else 1
            if dx == away:
                line = corner_ref[2 * kind + side : 2 * kind + side + 1, :]
                if kind == 2:
                    line = line * (keep_low if side == 0 else keep_high)
                return line
            slot = MASK if kind == 2 else halo_slot(kind, i, dy)
            return halo_v[side, slot, x + dx : x + dx + 1, :]

        def mask(dx, x=x, away=away, face_ref=face_ref):
            return face_ref[MASK] if dx == away else fluid_ref[x + dx]

        plane_step(
            n,
            lambda i, dx, get=get: get(0, i, dx, post_ref),
            lambda i, dx, dy, row=row: row(0, i, dx, dy),
            lambda i, dx, get=get: get(1, i, dx, adj_ref),
            lambda i, dx, dy, row=row: row(1, i, dx, dy),
            mask,
            lambda dx, dy, row=row: row(2, 0, dx, dy),
            fluid_ref[x],
            bcell_ref[x],
            profile_ref[x],
            magnet_ref[x],
            near_v,
            new_v,
            out_v,
            sums_v,
            count,
        )
        these = plane_stores(
            n, x, new_v, out_v, newf_ref, newg_ref, outf_ref, outg_ref, store_sem
        )
        start_all(these)
        stores += these
    rows = jnp.concatenate(
        [jnp.sum(sums_v[m], axis=0, keepdims=True) for m in range(count)], axis=0
    )
    share_ref[...] = lax.dot_general(
        jnp.ones((share_ref.shape[0], 128), jnp.float32),
        rows,
        (((1,), (1,)), ((), ())),
        precision=lax.Precision.HIGHEST,
        preferred_element_type=jnp.float32,
    )
    wait_all(stores)


def outer_call(
    post, adj, fluid, bcell, first, second, fromleft, fromright, cornerleft, cornerright, profile,
    magnet, partial, newf, newg, outf, outg,
):
    sx, sy, sz = profile.shape
    count = partial.shape[0]
    flow = jax.ShapeDtypeStruct(newf.shape, jnp.float32)
    field = jax.ShapeDtypeStruct(newg.shape, jnp.float32)
    return pl.pallas_call(
        outer_kernel,
        in_specs=[VMEM] * 13 + [ANY] * 4,
        out_specs=[ANY] * 4 + [VMEM],
        out_shape=[
            flow,
            field,
            flow,
            field,
            jax.ShapeDtypeStruct((lax.axis_size(("gx", "gy")), count), jnp.float32),
        ],
        input_output_aliases={13: 0, 14: 1, 15: 2, 16: 3},
        scratch_shapes=[
            pltpu.VMEM((NP, 2, sy, sz), jnp.float32),
            pltpu.VMEM((NP, 2, sy, sz), jnp.float32),
            pltpu.VMEM((2, SLOTS, sx, sz), jnp.float32),
            pltpu.VMEM((18, sy, sz), jnp.float32),
            pltpu.VMEM((count, 8, 128), jnp.float32),
            pltpu.SemaphoreType.DMA((4, 2)),
        ],
        compiler_params=pltpu.CompilerParams(vmem_limit_bytes=OUTER_VMEM),
        name="outer",
    )(
        post, adj, fluid, bcell, first, second, fromleft, fromright, cornerleft, cornerright,
        profile, magnet, partial, newf, newg, outf, outg,
    )


def ring(count, step):
    return [(i, (i + step) % count) for i in range(count)]


def on_device(flow, field, adj_flow_in, adj_field_in, profile, strengths, wall, magnet):
    across, around = lax.axis_size("gy"), lax.axis_size("gx")
    count = strengths.shape[0]
    table = strengths.reshape(1, count)
    post, adj, fluid, bcell, profile, magnet, mine1, mine2, right, left = collide_call(
        flow, field, adj_flow_in, adj_field_in, profile, table, wall, magnet
    )
    inside = [(i, i ^ 1) for i in range(across)]
    between = [(i, (((i + 1) ^ 1) - 1) % across) for i in range(across)]
    second = lax.ppermute(mine2, "gy", between)
    first = lax.ppermute(mine1, "gy", inside)
    fromleft = lax.ppermute(right, "gx", ring(around, 1))
    fromright = lax.ppermute(left, "gx", ring(around, -1))
    corner_r, corner_l = corner_call(first, second)
    cornerleft = lax.ppermute(corner_r, "gx", ring(around, 1))
    cornerright = lax.ppermute(corner_l, "gx", ring(around, -1))
    newf, newg, outf, outg, partial = inner_call(
        post, adj, fluid, bcell, first, second, profile, magnet, count
    )
    newf, newg, outf, outg, share = outer_call(
        post, adj, fluid, bcell, first, second, fromleft, fromright, cornerleft, cornerright,
        profile, magnet, partial, newf, newg, outf, outg,
    )
    cells = flow.shape[1] * around * flow.shape[2] * across * flow.shape[3]
    totals = jnp.sum(lax.all_to_all(share, ("gx", "gy"), 0, 0, tiled=True), axis=0)
    return (newf, newg, outf, outg, totals / math.sqrt(cells / count))


def solution(mesh):
    stack = P(None, "gx", "gy", None)
    cell = P("gx", "gy", None)
    return jax.shard_map(
        on_device,
        mesh=mesh,
        in_specs=(stack, stack, stack, stack, cell, P(), cell, cell),
        out_specs=(stack, stack, stack, stack, P()),
        check_vma=False,
    )
```

```python
import functools
import math

import jax
import jax.numpy as jnp
from jax import lax
from jax.experimental import pallas as pl
from jax.experimental.pallas import tpu as pltpu
from jax.sharding import PartitionSpec as P

LATTICE = [
    (0, 0, 0),
    (1, 0, 0),
    (-1, 0, 0),
    (0, 1, 0),
    (0, -1, 0),
    (0, 0, 1),
    (0, 0, -1),
    (1, 1, 0),
    (-1, -1, 0),
    (1, -1, 0),
    (-1, 1, 0),
    (1, 0, 1),
    (-1, 0, -1),
    (1, 0, -1),
    (-1, 0, 1),
    (0, 1, 1),
    (0, -1, -1),
    (0, 1, -1),
    (0, -1, 1),
]
NF, NG = 19, 7
NP = NF + NG
FIRST = [1, 3, 5, 7, 9, 11, 13, 15, 17]
W0, W1, W2 = 1.0 / 3.0, 1.0 / 18.0, 1.0 / 36.0
V0, V1 = 0.25, 0.125
PLUS = 0.625
MINUS = 0.5 / 1.125
TAU_PLUS = 0.8
COUPLE = 2.0
SOURCE = 2.0

UP = [3, 7, 10, 15, 17, NF + 3]
DOWN = [4, 8, 9, 16, 18, NF + 4]
RIGHT = [1, 7, 9, 11, 13, NF + 1]
LEFT = [2, 8, 10, 12, 14, NF + 2]
SLOTS = 13
MASK = 12

RIM_VMEM = 60 << 20
COLLIDE_VMEM = 48 << 20
INNER_VMEM = 42 << 20
OUTER_VMEM = 42 << 20


def weight(i):
    return W1 if i <= 6 else W2


def gather_strength(table, magnet):
    parts = [
        jnp.take_along_axis(table, magnet[:, z : z + 128], axis=1, mode="promise_in_bounds")
        for z in range(0, magnet.shape[1], 128)
    ]
    return jnp.concatenate(parts, axis=1)


def lane_table(strengths_ref):
    row = strengths_ref[...]
    rest = 128 - row.shape[1]
    if rest:
        row = jnp.concatenate([row, jnp.zeros((1, rest), jnp.float32)], axis=1)
    return jnp.broadcast_to(row, (8, 128))


def vector_sums(pair):
    x = pair[1] + pair[7] + pair[9] + pair[11] + pair[13]
    y = pair[3] + pair[7] - pair[9] + pair[15] + pair[17]
    z = pair[5] + pair[11] - pair[13] + pair[15] - pair[17]
    return x, y, z


def along(i, vx, vy, vz):
    out = None
    for c, v in zip(LATTICE[i], (vx, vy, vz)):
        if c:
            if out is None:
                out = v if c > 0 else -v
            else:
                out = out + v if c > 0 else out - v
    return out


def start_all(copies):
    for c in copies:
        c.start()


def wait_all(copies):
    for c in copies:
        c.wait()


def collide(f, g, fluid, bcell, wanted):
    even = {i: f[i] + f[i + 1] for i in FIRST}
    diff = {i: f[i] - f[i + 1] for i in FIRST}
    rho = f[0] + (1.0 - fluid)
    for i in FIRST:
        rho = rho + even[i]
    momx, momy, momz = vector_sums(diff)
    inv = 1.0 / rho
    ux, uy, uz = momx * inv, momy * inv, momz * inv
    bval = g[0] + g[1] + g[2] + g[3] + g[4] + g[5] + g[6]
    current = (g[3] - g[4]) - bval * uy
    shear = (even[7] - even[9]) - momx * uy
    force = (COUPLE * bcell) * current
    vx = ux + TAU_PLUS * force * inv
    base = 1.0 - 1.5 * (vx * vx + uy * uy + uz * uz)
    post = {}
    if 0 in wanted:
        post[0] = f[0] - 2.0 * PLUS * (f[0] - (W0 * rho) * base)
    rho1, rho2 = W1 * rho, W2 * rho
    for i in FIRST:
        if i not in wanted and i + 1 not in wanted:
            continue
        wr = rho1 if i <= 6 else rho2
        a = along(i, vx, uy, uz)
        ne = PLUS * (even[i] - (2.0 * wr) * (base + 4.5 * a * a))
        no = MINUS * (diff[i] - (6.0 * wr) * a)
        if i in wanted:
            post[i] = f[i] - ne - no
        if i + 1 in wanted:
            post[i + 1] = f[i + 1] - ne + no
    common = bval + (SOURCE * bcell) * shear
    slope = 4.0 * bval
    if NF in wanted:
        post[NF] = V0 * common
    for k, u in ((1, ux), (3, uy), (5, uz)):
        if NF + k in wanted:
            post[NF + k] = V1 * (common + slope * u)
        if NF + k + 1 in wanted:
            post[NF + k + 1] = V1 * (common - slope * u)
    return post


def rim_kernel(
    flow_ref, field_ref, adjf_ref, adjg_ref, profile_ref, strengths_ref, wall_ref, magnet_ref,
    first_ref, second_ref, right_ref, left_ref,
    rows_v, faces_v, profile_v, wall_v, magnet_v, message_v, cell_sem, rows_sem, faces_sem, adj_sem,
):
    sx, sy = profile_v.shape[:2]
    odd = lax.rem(lax.axis_index("gy"), 2)
    ends = (sy - 1, 0)
    sides = (0, sx - 1)

    def adj_at(i, where):
        return adjf_ref.at[(i, *where)] if i < NF else adjg_ref.at[(i - NF, *where)]

    rows = []
    for n, y in enumerate(ends):
        rows += [
            pltpu.make_async_copy(
                flow_ref.at[:, :, y], rows_v.at[n, pl.ds(0, NF)], rows_sem.at[n, 0]
            ),
            pltpu.make_async_copy(
                field_ref.at[:, :, y], rows_v.at[n, pl.ds(NF, NG)], rows_sem.at[n, 1]
            ),
        ]
    cells = [
        pltpu.make_async_copy(a, b, cell_sem.at[n])
        for n, (a, b) in enumerate(
            ((wall_ref, wall_v), (magnet_ref, magnet_v), (profile_ref, profile_v))
        )
    ]
    faces = []
    for n, x in enumerate(sides):
        faces += [
            pltpu.make_async_copy(
                flow_ref.at[:, x], faces_v.at[n, pl.ds(0, NF)], faces_sem.at[n, 0]
            ),
            pltpu.make_async_copy(
                field_ref.at[:, x], faces_v.at[n, pl.ds(NF, NG)], faces_sem.at[n, 1]
            ),
        ]
    adjs = []
    for s in range(6):
        for n, (i, where, out) in enumerate(
            (
                (DOWN[s], (slice(None), ends[0]), message_v.at[0]),
                (UP[s], (slice(None), ends[1]), message_v.at[1]),
                (RIGHT[s], (sides[0],), left_ref),
                (LEFT[s], (sides[1],), right_ref),
            )
        ):
            adjs.append(pltpu.make_async_copy(adj_at(i, where), out.at[6 + s], adj_sem.at[n, s]))
    start_all(rows[:2])
    start_all(cells)
    start_all(rows[2:])
    start_all(faces)
    start_all(adjs)
    table = lane_table(strengths_ref)
    wait_all(cells)
    for n, (y, wanted) in enumerate(zip(ends, (UP, DOWN))):
        wait_all(rows[2 * n : 2 * n + 2])
        fluid = 1.0 - wall_v[:, y, :].astype(jnp.float32)
        bcell = gather_strength(table, magnet_v[:, y, :]) * profile_v[:, y, :]
        post = collide(
            [rows_v[n, i] for i in range(NF)],
            [rows_v[n, NF + k] for k in range(NG)],
            fluid,
            bcell,
            wanted,
        )
        for s in range(6):
            message_v[n, s] = post[wanted[s]]
        message_v[n, MASK] = fluid
    for n, (x, wanted, out) in enumerate(
        ((sides[0], LEFT, left_ref), (sides[1], RIGHT, right_ref))
    ):
        wait_all(faces[2 * n : 2 * n + 2])
        fluid = 1.0 - wall_v[x].astype(jnp.float32)
        bcell = gather_strength(table, magnet_v[x]) * profile_v[x]
        post = collide(
            [faces_v[n, i] for i in range(NF)],
            [faces_v[n, NF + k] for k in range(NG)],
            fluid,
            bcell,
            wanted,
        )
        for s in range(6):
            out[s] = post[wanted[s]]
        out[MASK] = fluid
    wait_all(adjs)
    first_ref[...] = message_v[odd]
    second_ref[...] = message_v[1 - odd]


ANY = pl.BlockSpec(memory_space=pl.ANY)
VMEM = pl.BlockSpec(memory_space=pltpu.VMEM)


def rim_call(flow, field, adjf, adjg, profile, strengths, wall, magnet):
    sx, sy, sz = profile.shape
    cells = pltpu.VMEM((sx, sy, sz), jnp.float32)
    names = pltpu.VMEM((sx, sy, sz), jnp.int32)
    rows = pltpu.VMEM((SLOTS, sx, sz), jnp.float32)
    faces = pltpu.VMEM((SLOTS, sy, sz), jnp.float32)
    dma = pltpu.SemaphoreType.DMA
    return pl.pallas_call(
        rim_kernel,
        in_specs=[ANY, ANY, ANY, ANY, ANY, VMEM, ANY, ANY],
        out_specs=[VMEM] * 4,
        out_shape=[rows, rows, faces, faces],
        scratch_shapes=[
            pltpu.VMEM((2, NP, sx, sz), jnp.float32),
            pltpu.VMEM((2, NP, sy, sz), jnp.float32),
            cells,
            names,
            names,
            pltpu.VMEM((2, SLOTS, sx, sz), jnp.float32),
            dma((3,)),
            dma((2, 2)),
            dma((2, 2)),
            dma((4, 6)),
        ],
        compiler_params=pltpu.CompilerParams(vmem_limit_bytes=RIM_VMEM),
        name="rims",
    )(flow, field, adjf, adjg, profile, strengths, wall, magnet)


def collide_kernel(
    flow_ref, field_ref, adjf_ref, adjg_ref, profile_ref, strengths_ref, wall_ref, magnet_ref,
    post_ref, adj_ref, fluid_ref, bcell_ref, profile_v, magnet_v,
    flow_v, field_v, wall_v, plane_sem, adj_sem,
):
    sx = fluid_ref.shape[0]

    def loads(x):
        pairs = (
            (wall_ref.at[x], wall_v.at[x]),
            (magnet_ref.at[x], magnet_v.at[x]),
            (profile_ref.at[x], profile_v.at[x]),
            (flow_ref.at[:, x], flow_v.at[:, x]),
            (field_ref.at[:, x], field_v.at[:, x]),
        )
        return [pltpu.make_async_copy(a, b, plane_sem.at[n, x]) for n, (a, b) in enumerate(pairs)]

    for x in range(sx):
        start_all(loads(x))
    adj_loads = [
        pltpu.make_async_copy(adjf_ref, adj_ref.at[pl.ds(0, NF)], adj_sem.at[0]),
        pltpu.make_async_copy(adjg_ref, adj_ref.at[pl.ds(NF, NG)], adj_sem.at[1]),
    ]
    start_all(adj_loads)
    table = lane_table(strengths_ref)

    def body(x, carry):
        wait_all(loads(x))
        fluid = 1.0 - wall_v[x].astype(jnp.float32)
        bcell = gather_strength(table, magnet_v[x]) * profile_v[x]
        fluid_ref[x] = fluid
        bcell_ref[x] = bcell
        f = [flow_v[i, x] for i in range(NF)]
        g = [field_v[k, x] for k in range(NG)]
        for i, value in collide(f, g, fluid, bcell, range(NP)).items():
            post_ref[i, x] = value
        return carry

    lax.fori_loop(0, sx, body, 0)
    wait_all(adj_loads)


def collide_call(flow, field, adjf, adjg, profile, strengths, wall, magnet):
    sx, sy, sz = profile.shape
    full = pltpu.VMEM((NP, sx, sy, sz), jnp.float32)
    cells = pltpu.VMEM((sx, sy, sz), jnp.float32)
    names = pltpu.VMEM((sx, sy, sz), jnp.int32)
    dma = pltpu.SemaphoreType.DMA
    return pl.pallas_call(
        collide_kernel,
        in_specs=[ANY, ANY, ANY, ANY, ANY, VMEM, ANY, ANY],
        out_specs=[VMEM] * 6,
        out_shape=[full, full, cells, cells, cells, names],
        scratch_shapes=[
            pltpu.VMEM(flow.shape, jnp.float32),
            pltpu.VMEM(field.shape, jnp.float32),
            names,
            dma((5, sx)),
            dma((2,)),
        ],
        compiler_params=pltpu.CompilerParams(vmem_limit_bytes=COLLIDE_VMEM),
        cost_estimate=pl.CostEstimate(
            flops=300 * sx * sy * sz, bytes_accessed=12 * NP * sx * sy * sz, transcendentals=0
        ),
        name="collide",
    )(flow, field, adjf, adjg, profile, strengths, wall, magnet)


CORNER_RIGHT = ((0, 7, 0, 8), (1, 9, 1, 10))
CORNER_LEFT = ((0, 10, 0, 9), (1, 8, 1, 7))


def corner_slots(side, post, adj):
    posts, adjs = (UP, DOWN) if side == 0 else (DOWN, UP)
    return posts.index(post), 6 + adjs.index(adj), MASK


def corner_kernel(first_ref, second_ref, after_ref, right_ref, left_ref):
    del after_ref
    odd = lax.rem(lax.axis_index("gy"), 2) == 1
    sx = first_ref.shape[1]

    def row(side, slot, x):
        a, b = first_ref[slot, x : x + 1, :], second_ref[slot, x : x + 1, :]
        return jnp.where(odd, a, b) if side == 0 else jnp.where(odd, b, a)

    for out, table, x in ((right_ref, CORNER_RIGHT, sx - 1), (left_ref, CORNER_LEFT, 0)):
        out[...] = jnp.zeros_like(out)
        for side, post, _, adj in table:
            for n, slot in enumerate(corner_slots(side, post, adj)):
                out[2 * n + side : 2 * n + side + 1, :] = row(side, slot, x)


def corner_call(first, second, after):
    sz = first.shape[2]
    out = pltpu.VMEM((8, sz), jnp.float32)
    return pl.pallas_call(
        corner_kernel,
        in_specs=[VMEM, VMEM, ANY],
        out_specs=[VMEM, VMEM],
        out_shape=[out, out],
        compiler_params=pltpu.CompilerParams(vmem_limit_bytes=2 << 20),
        name="corners",
    )(first, second, after)


def plane_step(
    x_index, post, post_row, adj, adj_row, mask, mask_row, fluid, bcell, profile, magnet,
    near_ref, new_ref, out_ref, sums_ref, count,
):
    sy, sz = fluid.shape
    yi = lax.broadcasted_iota(jnp.int32, (sy, sz), 0)
    zi = lax.broadcasted_iota(jnp.int32, (sy, sz), 1)
    top, bottom = yi == sy - 1, yi == 0
    zlast, zfirst = zi == sz - 1, zi == 0

    def shift(value, row, dy, dz):
        if dy == -1:
            value = jnp.where(bottom, row(), pltpu.roll(value, 1, 0))
        elif dy == 1:
            value = jnp.where(top, row(), pltpu.roll(value, sy - 1, 0))
        if dz == -1:
            value = pltpu.roll(value, 1, 1)
        elif dz == 1:
            value = pltpu.roll(value, sz - 1, 1)
        return value

    def moved(get, get_row, i, sign):
        dx, dy, dz = (sign * c for c in LATTICE[i if i < NF else i - NF])
        return shift(get(i, dx), lambda: get_row(i, dx, dy), dy, dz)

    def near_of(i, sign):
        dx, dy, dz = (sign * c for c in LATTICE[i])
        value = shift(mask(dx), lambda: mask_row(dx, dy), dy, dz)
        if dz == -1:
            value = jnp.where(zfirst, 0.0, value)
        elif dz == 1:
            value = jnp.where(zlast, 0.0, value)
        return value

    for n, i in enumerate(FIRST):
        near_ref[2 * n] = near_of(i, -1)
        near_ref[2 * n + 1] = near_of(i, 1)

    def near(n):
        return near_ref[2 * n] > 0.5, near_ref[2 * n + 1] > 0.5

    def pull(i, n):
        minus, plus = near(n)
        a = fluid * jnp.where(minus, moved(post, post_row, i, -1), post(i + 1, 0))
        b = fluid * jnp.where(plus, moved(post, post_row, i + 1, -1), post(i, 0))
        new_ref[i, x_index] = a
        new_ref[i + 1, x_index] = b
        return a, b

    f0 = fluid * post(0, 0)
    new_ref[0, x_index] = f0
    rho = f0 + (1.0 - fluid)
    momx = momy = momz = shear0 = 0.0
    for n, i in enumerate(FIRST):
        a, b = pull(i, n)
        s, d = a + b, a - b
        rho = rho + s
        cx, cy, cz = LATTICE[i]
        if cx:
            momx = momx + d
        if cy:
            momy = momy + d if cy > 0 else momy - d
        if cz:
            momz = momz + d if cz > 0 else momz - d
        if cx and cy:
            shear0 = shear0 + s if cx * cy > 0 else shear0 - s
    g0 = fluid * post(NF, 0)
    new_ref[NF, x_index] = g0
    bval = g0
    gy = None
    for n, k in enumerate((1, 3, 5)):
        a, b = pull(NF + k, n)
        bval = bval + (a + b)
        if k == 3:
            gy = a - b
    inv = 1.0 / rho
    ux, uy, uz = momx * inv, momy * inv, momz * inv
    current = gy - bval * uy
    shear = shear0 - momx * uy
    force = (COUPLE * bcell) * current
    vx = ux + TAU_PLUS * force * inv

    def push(i, n):
        minus, plus = near(n)
        a = fluid * jnp.where(plus, moved(adj, adj_row, i, 1), adj(i + 1, 0))
        b = fluid * jnp.where(minus, moved(adj, adj_row, i + 1, 1), adj(i, 0))
        return a, b

    l0 = fluid * adj(0, 0)
    out_ref[0, x_index] = (1.0 - 2.0 * PLUS) * l0
    total = (2.0 * PLUS * W0) * l0
    m1 = [0.0, 0.0, 0.0]
    m2 = {}
    for n, i in enumerate(FIRST):
        a, b = push(i, n)
        s, d = a + b, a - b
        de = (0.5 - PLUS) * s
        do = (0.5 - MINUS) * d
        out_ref[i, x_index] = de + do
        out_ref[i + 1, x_index] = de - do
        w = weight(i)
        s = (2.0 * PLUS * w) * s
        d = (2.0 * MINUS * w) * d
        total = total + s
        c = LATTICE[i]
        for axis in range(3):
            if c[axis]:
                m1[axis] = m1[axis] + d if c[axis] > 0 else m1[axis] - d
            for other in range(axis, 3):
                sign = c[axis] * c[other]
                if sign:
                    old = m2.get((axis, other))
                    if old is None:
                        m2[axis, other] = s if sign > 0 else -s
                    else:
                        m2[axis, other] = old + s if sign > 0 else old - s
    h0 = fluid * adj(NF, 0)
    hsum = V0 * h0
    h1 = []
    hs = None
    for n, k in enumerate((1, 3, 5)):
        a, b = push(NF + k, n)
        hs = a + b if hs is None else hs + (a + b)
        h1.append(V1 * (a - b))
    hsum = hsum + V1 * hs

    base = 1.0 - 1.5 * (vx * vx + uy * uy + uz * uz)
    tx = m2[0, 0] * vx + m2[0, 1] * uy + m2[0, 2] * uz
    ty = m2[0, 1] * vx + m2[1, 1] * uy + m2[1, 2] * uz
    tz = m2[0, 2] * vx + m2[1, 2] * uy + m2[2, 2] * uz
    rhobar = (
        total * base
        + 4.5 * (vx * tx + uy * ty + uz * tz)
        + 3.0 * (m1[0] * vx + m1[1] * uy + m1[2] * uz)
    )
    total3 = 3.0 * total
    vxbar = rho * (9.0 * tx + 3.0 * m1[0] - total3 * vx)
    uybar = rho * (9.0 * ty + 3.0 * m1[1] - total3 * uy)
    uzbar = rho * (9.0 * tz + 3.0 * m1[2] - total3 * uz)
    slope = 4.0 * bval
    forcebar = (TAU_PLUS * vxbar) * inv
    rhobar = rhobar - forcebar * force * inv
    currentbar = (COUPLE * bcell) * forcebar
    shearbar = (SOURCE * bcell) * hsum
    dcell = COUPLE * current * forcebar + SOURCE * shear * hsum
    uxbar = vxbar + slope * h1[0]
    uybar = uybar + slope * h1[1] - bval * currentbar - momx * shearbar
    uzbar = uzbar + slope * h1[2]
    bbar = hsum + 4.0 * (h1[0] * ux + h1[1] * uy + h1[2] * uz) - uy * currentbar
    mxbar = uxbar * inv - uy * shearbar
    mybar = uybar * inv
    mzbar = uzbar * inv
    rhobar = rhobar - (ux * uxbar + uy * uybar + uz * uzbar) * inv

    out_ref[0, x_index] = out_ref[0, x_index] + rhobar
    for i in FIRST:
        cm = along(i, mxbar, mybar, mzbar)
        cx, cy, _ = LATTICE[i]
        common = rhobar
        if cx and cy:
            common = rhobar + shearbar if cx * cy > 0 else rhobar - shearbar
        out_ref[i, x_index] = out_ref[i, x_index] + (common + cm)
        out_ref[i + 1, x_index] = out_ref[i + 1, x_index] + (common - cm)
    for k in range(NG):
        value = bbar
        if k == 3:
            value = bbar + currentbar
        elif k == 4:
            value = bbar - currentbar
        out_ref[NF + k, x_index] = value

    share = dcell * profile
    for m in range(count):
        hit = jnp.where(magnet == m, share, 0.0)
        part = hit[:, 0:128]
        for z in range(128, sz, 128):
            part = part + hit[:, z : z + 128]
        sums_ref[m] = sums_ref[m] + part


def halo_slot(kind, i, dy):
    names = (UP, DOWN) if (dy == -1) == (kind == 0) else (DOWN, UP)
    return names[0].index(i) + 6 * kind


def face_slot(kind, i, dx):
    names = RIGHT if (dx == -1) == (kind == 0) else LEFT
    return names.index(i) + 6 * kind


def load_halo(first_ref, second_ref, halo_ref):
    odd = lax.rem(lax.axis_index("gy"), 2)
    halo_ref[1 - odd] = first_ref[...]
    halo_ref[odd] = second_ref[...]
    here = lax.axis_index("gy")
    keep_low = jnp.where(here == 0, 0.0, 1.0)
    keep_high = jnp.where(here == lax.axis_size("gy") - 1, 0.0, 1.0)
    halo_ref[0, MASK] = halo_ref[0, MASK] * keep_low
    halo_ref[1, MASK] = halo_ref[1, MASK] * keep_high
    return keep_low, keep_high


def plane_stores(n, x, new_v, out_v, newf_ref, newg_ref, outf_ref, outg_ref, sem):
    pairs = (
        (new_v.at[pl.ds(0, NF), n], newf_ref.at[:, x]),
        (new_v.at[pl.ds(NF, NG), n], newg_ref.at[:, x]),
        (out_v.at[pl.ds(0, NF), n], outf_ref.at[:, x]),
        (out_v.at[pl.ds(NF, NG), n], outg_ref.at[:, x]),
    )
    return [pltpu.make_async_copy(a, b, sem.at[k, n]) for k, (a, b) in enumerate(pairs)]


def inner_kernel(
    post_ref, adj_ref, fluid_ref, bcell_ref, first_ref, second_ref, profile_ref, magnet_ref,
    newf_ref, newg_ref, outf_ref, outg_ref, sums_ref,
    new_v, out_v, halo_v, near_v, store_sem,
):
    sx = fluid_ref.shape[0]
    count = sums_ref.shape[0]

    def stores(x):
        return plane_stores(
            x, x, new_v, out_v, newf_ref, newg_ref, outf_ref, outg_ref, store_sem
        )

    sums_ref[...] = jnp.zeros_like(sums_ref)
    load_halo(first_ref, second_ref, halo_v)

    def body(x, carry):
        def row_of(slot, dx, dy):
            return halo_v[0 if dy == -1 else 1, slot, pl.ds(x + dx, 1), :]

        plane_step(
            x,
            lambda i, dx: post_ref[i, x + dx],
            lambda i, dx, dy: row_of(halo_slot(0, i, dy), dx, dy),
            lambda i, dx: adj_ref[i, x + dx],
            lambda i, dx, dy: row_of(halo_slot(1, i, dy), dx, dy),
            lambda dx: fluid_ref[x + dx],
            lambda dx, dy: row_of(MASK, dx, dy),
            fluid_ref[x],
            bcell_ref[x],
            profile_ref[x],
            magnet_ref[x],
            near_v,
            new_v,
            out_v,
            sums_ref,
            count,
        )
        start_all(stores(x))
        return carry

    lax.fori_loop(1, sx - 1, body, 0)
    for x in range(1, sx - 1):
        wait_all(stores(x))


def inner_call(post, adj, fluid, bcell, first, second, profile, magnet, count):
    sx, sy, sz = profile.shape
    full = pltpu.VMEM((NP, sx, sy, sz), jnp.float32)
    flow = jax.ShapeDtypeStruct((NF, sx, sy, sz), jnp.float32)
    field = jax.ShapeDtypeStruct((NG, sx, sy, sz), jnp.float32)
    return pl.pallas_call(
        inner_kernel,
        in_specs=[VMEM] * 8,
        out_specs=[ANY, ANY, ANY, ANY, VMEM],
        out_shape=[flow, field, flow, field, pltpu.VMEM((count, 8, 128), jnp.float32)],
        scratch_shapes=[
            full,
            full,
            pltpu.VMEM((2, SLOTS, sx, sz), jnp.float32),
            pltpu.VMEM((18, sy, sz), jnp.float32),
            pltpu.SemaphoreType.DMA((4, sx)),
        ],
        compiler_params=pltpu.CompilerParams(vmem_limit_bytes=INNER_VMEM),
        cost_estimate=pl.CostEstimate(
            flops=700 * sx * sy * sz, bytes_accessed=16 * NP * sx * sy * sz, transcendentals=0
        ),
        name="inner",
    )(post, adj, fluid, bcell, first, second, profile, magnet)


def outer_kernel(
    scale, post_ref, adj_ref, fluid_ref, bcell_ref, first_ref, second_ref, fromleft_ref, fromright_ref,
    cornerleft_ref, cornerright_ref, profile_ref, magnet_ref,
    partial_ref, newf_in, newg_in, outf_in, outg_in,
    newf_ref, newg_ref, outf_ref, outg_ref, share_ref,
    new_v, out_v, halo_v, near_v, sums_v, store_sem,
):
    del newf_in, newg_in, outf_in, outg_in
    sx = fluid_ref.shape[0]
    count = sums_v.shape[0]
    sums_v[...] = partial_ref[...]
    keep_low, keep_high = load_halo(first_ref, second_ref, halo_v)
    stores = []
    for n, (x, away) in enumerate(((0, -1), (sx - 1, 1))):
        face_ref, corner_ref = (
            (fromleft_ref, cornerleft_ref) if away == -1 else (fromright_ref, cornerright_ref)
        )

        def get(kind, i, dx, held, x=x, away=away, face_ref=face_ref):
            if dx == away:
                return face_ref[face_slot(kind, i, dx)]
            return held[i, x + dx]

        def row(kind, i, dx, dy, x=x, away=away, corner_ref=corner_ref):
            side = 0 if dy == -1 else 1
            if dx == away:
                line = corner_ref[2 * kind + side : 2 * kind + side + 1, :]
                if kind == 2:
                    line = line * (keep_low if side == 0 else keep_high)
                return line
            slot = MASK if kind == 2 else halo_slot(kind, i, dy)
            return halo_v[side, slot, x + dx : x + dx + 1, :]

        def mask(dx, x=x, away=away, face_ref=face_ref):
            return face_ref[MASK] if dx == away else fluid_ref[x + dx]

        plane_step(
            n,
            lambda i, dx, get=get: get(0, i, dx, post_ref),
            lambda i, dx, dy, row=row: row(0, i, dx, dy),
            lambda i, dx, get=get: get(1, i, dx, adj_ref),
            lambda i, dx, dy, row=row: row(1, i, dx, dy),
            mask,
            lambda dx, dy, row=row: row(2, 0, dx, dy),
            fluid_ref[x],
            bcell_ref[x],
            profile_ref[x],
            magnet_ref[x],
            near_v,
            new_v,
            out_v,
            sums_v,
            count,
        )
        these = plane_stores(
            n, x, new_v, out_v, newf_ref, newg_ref, outf_ref, outg_ref, store_sem
        )
        start_all(these)
        stores += these
    rows = jnp.concatenate(
        [jnp.sum(sums_v[m], axis=0, keepdims=True) for m in range(count)], axis=0
    )
    share_ref[...] = lax.dot_general(
        jnp.ones((share_ref.shape[0], 128), jnp.float32),
        rows * scale,
        (((1,), (1,)), ((), ())),
        precision=lax.Precision.HIGHEST,
        preferred_element_type=jnp.float32,
    )
    wait_all(stores)


def outer_call(
    post, adj, fluid, bcell, first, second, fromleft, fromright, cornerleft, cornerright, profile,
    magnet, partial, newf, newg, outf, outg, scale,
):
    sx, sy, sz = profile.shape
    count = partial.shape[0]
    flow = jax.ShapeDtypeStruct(newf.shape, jnp.float32)
    field = jax.ShapeDtypeStruct(newg.shape, jnp.float32)
    return pl.pallas_call(
        functools.partial(outer_kernel, scale),
        in_specs=[VMEM] * 13 + [ANY] * 4,
        out_specs=[ANY] * 4 + [VMEM],
        out_shape=[
            flow,
            field,
            flow,
            field,
            jax.ShapeDtypeStruct((lax.axis_size(("gx", "gy")), count), jnp.float32),
        ],
        input_output_aliases={13: 0, 14: 1, 15: 2, 16: 3},
        scratch_shapes=[
            pltpu.VMEM((NP, 2, sy, sz), jnp.float32),
            pltpu.VMEM((NP, 2, sy, sz), jnp.float32),
            pltpu.VMEM((2, SLOTS, sx, sz), jnp.float32),
            pltpu.VMEM((18, sy, sz), jnp.float32),
            pltpu.VMEM((count, 8, 128), jnp.float32),
            pltpu.SemaphoreType.DMA((4, 2)),
        ],
        compiler_params=pltpu.CompilerParams(vmem_limit_bytes=OUTER_VMEM),
        name="outer",
    )(
        post, adj, fluid, bcell, first, second, fromleft, fromright, cornerleft, cornerright,
        profile, magnet, partial, newf, newg, outf, outg,
    )


def ring(count, step):
    return [(i, (i + step) % count) for i in range(count)]


def on_device(flow, field, adj_flow_in, adj_field_in, profile, strengths, wall, magnet):
    across, around = lax.axis_size("gy"), lax.axis_size("gx")
    count = strengths.shape[0]
    table = strengths.reshape(1, count)
    arrays = (flow, field, adj_flow_in, adj_field_in, profile, table, wall, magnet)
    mine1, mine2, right, left = rim_call(*arrays)
    inside = [(i, i ^ 1) for i in range(across)]
    between = [(i, (((i + 1) ^ 1) - 1) % across) for i in range(across)]
    second = lax.ppermute(mine2, "gy", between)
    first = lax.ppermute(mine1, "gy", inside)
    fromleft = lax.ppermute(right, "gx", ring(around, 1))
    fromright = lax.ppermute(left, "gx", ring(around, -1))
    post, adj, fluid, bcell, profile, magnet = collide_call(*arrays)
    corner_r, corner_l = corner_call(first, second, bcell)
    cornerleft = lax.ppermute(corner_r, "gx", ring(around, 1))
    cornerright = lax.ppermute(corner_l, "gx", ring(around, -1))
    newf, newg, outf, outg, partial = inner_call(
        post, adj, fluid, bcell, first, second, profile, magnet, count
    )
    cells = flow.shape[1] * around * flow.shape[2] * across * flow.shape[3]
    newf, newg, outf, outg, share = outer_call(
        post, adj, fluid, bcell, first, second, fromleft, fromright, cornerleft, cornerright,
        profile, magnet, partial, newf, newg, outf, outg, 1.0 / math.sqrt(cells / count),
    )
    totals = jnp.sum(lax.all_to_all(share, ("gx", "gy"), 0, 0, tiled=True), axis=0)
    return (newf, newg, outf, outg, totals)


def solution(mesh):
    stack = P(None, "gx", "gy", None)
    cell = P("gx", "gy", None)
    return jax.shard_map(
        on_device,
        mesh=mesh,
        in_specs=(stack, stack, stack, stack, cell, P(), cell, cell),
        out_specs=(stack, stack, stack, stack, P()),
        check_vma=False,
    )
```

```python
import functools
import math

import jax
import jax.numpy as jnp
from jax import lax
from jax.experimental import pallas as pl
from jax.experimental.pallas import tpu as pltpu
from jax.sharding import PartitionSpec as P

LATTICE = [
    (0, 0, 0),
    (1, 0, 0),
    (-1, 0, 0),
    (0, 1, 0),
    (0, -1, 0),
    (0, 0, 1),
    (0, 0, -1),
    (1, 1, 0),
    (-1, -1, 0),
    (1, -1, 0),
    (-1, 1, 0),
    (1, 0, 1),
    (-1, 0, -1),
    (1, 0, -1),
    (-1, 0, 1),
    (0, 1, 1),
    (0, -1, -1),
    (0, 1, -1),
    (0, -1, 1),
]
NF, NG = 19, 7
NP = NF + NG
FIRST = [1, 3, 5, 7, 9, 11, 13, 15, 17]
W0, W1, W2 = 1.0 / 3.0, 1.0 / 18.0, 1.0 / 36.0
V0, V1 = 0.25, 0.125
PLUS = 0.625
MINUS = 0.5 / 1.125
TAU_PLUS = 0.8
COUPLE = 2.0
SOURCE = 2.0

UP = [3, 7, 10, 15, 17, NF + 3]
DOWN = [4, 8, 9, 16, 18, NF + 4]
RIGHT = [1, 7, 9, 11, 13, NF + 1]
LEFT = [2, 8, 10, 12, 14, NF + 2]
SLOTS = 13
MASK = 12

RIM_VMEM = 58 << 20
COLLIDE_VMEM = 4 << 20
INNER_VMEM = 12 << 20
OUTER_VMEM = 8 << 20


def weight(i):
    return W1 if i <= 6 else W2


def gather_strength(table, magnet):
    parts = [
        jnp.take_along_axis(table, magnet[:, z : z + 128], axis=1, mode="promise_in_bounds")
        for z in range(0, magnet.shape[1], 128)
    ]
    return jnp.concatenate(parts, axis=1)


def lane_table(strengths_ref):
    row = strengths_ref[...]
    rest = 128 - row.shape[1]
    if rest:
        row = jnp.concatenate([row, jnp.zeros((1, rest), jnp.float32)], axis=1)
    return jnp.broadcast_to(row, (8, 128))


def vector_sums(pair):
    x = pair[1] + pair[7] + pair[9] + pair[11] + pair[13]
    y = pair[3] + pair[7] - pair[9] + pair[15] + pair[17]
    z = pair[5] + pair[11] - pair[13] + pair[15] - pair[17]
    return x, y, z


def along(i, vx, vy, vz):
    out = None
    for c, v in zip(LATTICE[i], (vx, vy, vz)):
        if c:
            if out is None:
                out = v if c > 0 else -v
            else:
                out = out + v if c > 0 else out - v
    return out


def start_all(copies):
    for c in copies:
        c.start()


def wait_all(copies):
    for c in copies:
        c.wait()


def collide(f, g, fluid, bcell, wanted):
    even = {i: f[i] + f[i + 1] for i in FIRST}
    diff = {i: f[i] - f[i + 1] for i in FIRST}
    rho = f[0] + (1.0 - fluid)
    for i in FIRST:
        rho = rho + even[i]
    momx, momy, momz = vector_sums(diff)
    inv = 1.0 / rho
    ux, uy, uz = momx * inv, momy * inv, momz * inv
    bval = g[0] + g[1] + g[2] + g[3] + g[4] + g[5] + g[6]
    current = (g[3] - g[4]) - bval * uy
    shear = (even[7] - even[9]) - momx * uy
    force = (COUPLE * bcell) * current
    vx = ux + TAU_PLUS * force * inv
    base = 1.0 - 1.5 * (vx * vx + uy * uy + uz * uz)
    post = {}
    if 0 in wanted:
        post[0] = f[0] - 2.0 * PLUS * (f[0] - (W0 * rho) * base)
    rho1, rho2 = W1 * rho, W2 * rho
    for i in FIRST:
        if i not in wanted and i + 1 not in wanted:
            continue
        wr = rho1 if i <= 6 else rho2
        a = along(i, vx, uy, uz)
        ne = PLUS * (even[i] - (2.0 * wr) * (base + 4.5 * a * a))
        no = MINUS * (diff[i] - (6.0 * wr) * a)
        if i in wanted:
            post[i] = f[i] - ne - no
        if i + 1 in wanted:
            post[i + 1] = f[i + 1] - ne + no
    common = bval + (SOURCE * bcell) * shear
    slope = 4.0 * bval
    if NF in wanted:
        post[NF] = V0 * common
    for k, u in ((1, ux), (3, uy), (5, uz)):
        if NF + k in wanted:
            post[NF + k] = V1 * (common + slope * u)
        if NF + k + 1 in wanted:
            post[NF + k + 1] = V1 * (common - slope * u)
    return post


def rim_kernel(
    flow_ref, field_ref, adjf_ref, adjg_ref, profile_ref, strengths_ref, wall_ref, magnet_ref,
    first_ref, second_ref, right_ref, left_ref,
    rows_v, faces_v, profile_v, wall_v, magnet_v, message_v, cell_sem, rows_sem, faces_sem, adj_sem,
):
    sx, sy = profile_v.shape[:2]
    odd = lax.rem(lax.axis_index("gy"), 2)
    ends = (sy - 1, 0)
    sides = (0, sx - 1)

    def adj_at(i, where):
        return adjf_ref.at[(i, *where)] if i < NF else adjg_ref.at[(i - NF, *where)]

    rows = []
    for n, y in enumerate(ends):
        rows += [
            pltpu.make_async_copy(
                flow_ref.at[:, :, y], rows_v.at[n, pl.ds(0, NF)], rows_sem.at[n, 0]
            ),
            pltpu.make_async_copy(
                field_ref.at[:, :, y], rows_v.at[n, pl.ds(NF, NG)], rows_sem.at[n, 1]
            ),
        ]
    cells = [
        pltpu.make_async_copy(a, b, cell_sem.at[n])
        for n, (a, b) in enumerate(
            ((wall_ref, wall_v), (magnet_ref, magnet_v), (profile_ref, profile_v))
        )
    ]
    faces = []
    for n, x in enumerate(sides):
        faces += [
            pltpu.make_async_copy(
                flow_ref.at[:, x], faces_v.at[n, pl.ds(0, NF)], faces_sem.at[n, 0]
            ),
            pltpu.make_async_copy(
                field_ref.at[:, x], faces_v.at[n, pl.ds(NF, NG)], faces_sem.at[n, 1]
            ),
        ]
    adjs = []
    for s in range(6):
        for n, (i, where, out) in enumerate(
            (
                (DOWN[s], (slice(None), ends[0]), message_v.at[0]),
                (UP[s], (slice(None), ends[1]), message_v.at[1]),
                (RIGHT[s], (sides[0],), left_ref),
                (LEFT[s], (sides[1],), right_ref),
            )
        ):
            adjs.append(pltpu.make_async_copy(adj_at(i, where), out.at[6 + s], adj_sem.at[n, s]))
    start_all(rows[:2])
    start_all(cells)
    start_all(rows[2:])
    start_all(faces)
    start_all(adjs)
    table = lane_table(strengths_ref)
    wait_all(cells)
    for n, (y, wanted) in enumerate(zip(ends, (UP, DOWN))):
        wait_all(rows[2 * n : 2 * n + 2])
        fluid = 1.0 - wall_v[:, y, :].astype(jnp.float32)
        bcell = gather_strength(table, magnet_v[:, y, :]) * profile_v[:, y, :]
        post = collide(
            [rows_v[n, i] for i in range(NF)],
            [rows_v[n, NF + k] for k in range(NG)],
            fluid,
            bcell,
            wanted,
        )
        for s in range(6):
            message_v[n, s] = post[wanted[s]]
        message_v[n, MASK] = fluid
    for n, (x, wanted, out) in enumerate(
        ((sides[0], LEFT, left_ref), (sides[1], RIGHT, right_ref))
    ):
        wait_all(faces[2 * n : 2 * n + 2])
        fluid = 1.0 - wall_v[x].astype(jnp.float32)
        bcell = gather_strength(table, magnet_v[x]) * profile_v[x]
        post = collide(
            [faces_v[n, i] for i in range(NF)],
            [faces_v[n, NF + k] for k in range(NG)],
            fluid,
            bcell,
            wanted,
        )
        for s in range(6):
            out[s] = post[wanted[s]]
        out[MASK] = fluid
    wait_all(adjs)
    first_ref[...] = message_v[odd]
    second_ref[...] = message_v[1 - odd]


ANY = pl.BlockSpec(memory_space=pl.ANY)
VMEM = pl.BlockSpec(memory_space=pltpu.VMEM)


def rim_call(flow, field, adjf, adjg, profile, strengths, wall, magnet):
    sx, sy, sz = profile.shape
    cells = pltpu.VMEM((sx, sy, sz), jnp.float32)
    names = pltpu.VMEM((sx, sy, sz), jnp.int32)
    rows = pltpu.VMEM((SLOTS, sx, sz), jnp.float32)
    faces = pltpu.VMEM((SLOTS, sy, sz), jnp.float32)
    dma = pltpu.SemaphoreType.DMA
    return pl.pallas_call(
        rim_kernel,
        in_specs=[ANY, ANY, ANY, ANY, ANY, VMEM, ANY, ANY],
        out_specs=[VMEM] * 4,
        out_shape=[rows, rows, faces, faces],
        scratch_shapes=[
            pltpu.VMEM((2, NP, sx, sz), jnp.float32),
            pltpu.VMEM((2, NP, sy, sz), jnp.float32),
            cells,
            names,
            names,
            pltpu.VMEM((2, SLOTS, sx, sz), jnp.float32),
            dma((3,)),
            dma((2, 2)),
            dma((2, 2)),
            dma((4, 6)),
        ],
        compiler_params=pltpu.CompilerParams(vmem_limit_bytes=RIM_VMEM),
        name="rims",
    )(flow, field, adjf, adjg, profile, strengths, wall, magnet)


def collide_kernel(
    flow_ref, field_ref, profile_ref, strengths_ref, wall_ref, magnet_ref,
    post_ref, fluid_ref, bcell_ref,
):
    table = lane_table(strengths_ref)

    def body(x, carry):
        fluid = 1.0 - wall_ref[x].astype(jnp.float32)
        bcell = gather_strength(table, magnet_ref[x]) * profile_ref[x]
        fluid_ref[x] = fluid
        bcell_ref[x] = bcell
        f = [flow_ref[i, x] for i in range(NF)]
        g = [field_ref[k, x] for k in range(NG)]
        for i, value in collide(f, g, fluid, bcell, range(NP)).items():
            post_ref[i, x] = value
        return carry

    lax.fori_loop(0, fluid_ref.shape[0], body, 0)


def collide_call(flow, field, profile, strengths, wall, magnet):
    sx, sy, sz = profile.shape
    full = pltpu.VMEM((NP, sx, sy, sz), jnp.float32)
    cells = pltpu.VMEM((sx, sy, sz), jnp.float32)
    return pl.pallas_call(
        collide_kernel,
        in_specs=[VMEM] * 6,
        out_specs=[VMEM] * 3,
        out_shape=[full, cells, cells],
        compiler_params=pltpu.CompilerParams(vmem_limit_bytes=COLLIDE_VMEM),
        cost_estimate=pl.CostEstimate(
            flops=300 * sx * sy * sz, bytes_accessed=12 * NP * sx * sy * sz, transcendentals=0
        ),
        name="collide",
    )(flow, field, profile, strengths, wall, magnet)


CORNER_RIGHT = ((0, 7, 0, 8), (1, 9, 1, 10))
CORNER_LEFT = ((0, 10, 0, 9), (1, 8, 1, 7))


def corner_slots(side, post, adj):
    posts, adjs = (UP, DOWN) if side == 0 else (DOWN, UP)
    return posts.index(post), 6 + adjs.index(adj), MASK


def corner_kernel(first_ref, second_ref, after_ref, right_ref, left_ref):
    del after_ref
    odd = lax.rem(lax.axis_index("gy"), 2) == 1
    sx = first_ref.shape[1]

    def row(side, slot, x):
        a, b = first_ref[slot, x : x + 1, :], second_ref[slot, x : x + 1, :]
        return jnp.where(odd, a, b) if side == 0 else jnp.where(odd, b, a)

    for out, table, x in ((right_ref, CORNER_RIGHT, sx - 1), (left_ref, CORNER_LEFT, 0)):
        out[...] = jnp.zeros_like(out)
        for side, post, _, adj in table:
            for n, slot in enumerate(corner_slots(side, post, adj)):
                out[2 * n + side : 2 * n + side + 1, :] = row(side, slot, x)


def corner_call(first, second, after):
    sz = first.shape[2]
    out = pltpu.VMEM((8, sz), jnp.float32)
    return pl.pallas_call(
        corner_kernel,
        in_specs=[VMEM, VMEM, ANY],
        out_specs=[VMEM, VMEM],
        out_shape=[out, out],
        compiler_params=pltpu.CompilerParams(vmem_limit_bytes=2 << 20),
        name="corners",
    )(first, second, after)


def plane_step(
    x_index, post, post_row, adj, adj_row, mask, mask_row, fluid, bcell, profile, magnet,
    near_ref, new_ref, out_ref, sums_ref, count,
):
    sy, sz = fluid.shape
    yi = lax.broadcasted_iota(jnp.int32, (sy, sz), 0)
    zi = lax.broadcasted_iota(jnp.int32, (sy, sz), 1)
    top, bottom = yi == sy - 1, yi == 0
    zlast, zfirst = zi == sz - 1, zi == 0

    def shift(value, row, dy, dz):
        if dy == -1:
            value = jnp.where(bottom, row(), pltpu.roll(value, 1, 0))
        elif dy == 1:
            value = jnp.where(top, row(), pltpu.roll(value, sy - 1, 0))
        if dz == -1:
            value = pltpu.roll(value, 1, 1)
        elif dz == 1:
            value = pltpu.roll(value, sz - 1, 1)
        return value

    def moved(get, get_row, i, sign):
        dx, dy, dz = (sign * c for c in LATTICE[i if i < NF else i - NF])
        return shift(get(i, dx), lambda: get_row(i, dx, dy), dy, dz)

    def near_of(i, sign):
        dx, dy, dz = (sign * c for c in LATTICE[i])
        value = shift(mask(dx), lambda: mask_row(dx, dy), dy, dz)
        if dz == -1:
            value = jnp.where(zfirst, 0.0, value)
        elif dz == 1:
            value = jnp.where(zlast, 0.0, value)
        return value

    for n, i in enumerate(FIRST):
        near_ref[2 * n] = near_of(i, -1)
        near_ref[2 * n + 1] = near_of(i, 1)

    def near(n):
        return near_ref[2 * n] > 0.5, near_ref[2 * n + 1] > 0.5

    def pull(i, n):
        minus, plus = near(n)
        a = fluid * jnp.where(minus, moved(post, post_row, i, -1), post(i + 1, 0))
        b = fluid * jnp.where(plus, moved(post, post_row, i + 1, -1), post(i, 0))
        new_ref[i, x_index] = a
        new_ref[i + 1, x_index] = b
        return a, b

    f0 = fluid * post(0, 0)
    new_ref[0, x_index] = f0
    rho = f0 + (1.0 - fluid)
    momx = momy = momz = shear0 = 0.0
    for n, i in enumerate(FIRST):
        a, b = pull(i, n)
        s, d = a + b, a - b
        rho = rho + s
        cx, cy, cz = LATTICE[i]
        if cx:
            momx = momx + d
        if cy:
            momy = momy + d if cy > 0 else momy - d
        if cz:
            momz = momz + d if cz > 0 else momz - d
        if cx and cy:
            shear0 = shear0 + s if cx * cy > 0 else shear0 - s
    g0 = fluid * post(NF, 0)
    new_ref[NF, x_index] = g0
    bval = g0
    gy = None
    for n, k in enumerate((1, 3, 5)):
        a, b = pull(NF + k, n)
        bval = bval + (a + b)
        if k == 3:
            gy = a - b
    inv = 1.0 / rho
    ux, uy, uz = momx * inv, momy * inv, momz * inv
    current = gy - bval * uy
    shear = shear0 - momx * uy
    force = (COUPLE * bcell) * current
    vx = ux + TAU_PLUS * force * inv

    def push(i, n):
        minus, plus = near(n)
        a = fluid * jnp.where(plus, moved(adj, adj_row, i, 1), adj(i + 1, 0))
        b = fluid * jnp.where(minus, moved(adj, adj_row, i + 1, 1), adj(i, 0))
        return a, b

    l0 = fluid * adj(0, 0)
    out_ref[0, x_index] = (1.0 - 2.0 * PLUS) * l0
    total = (2.0 * PLUS * W0) * l0
    m1 = [0.0, 0.0, 0.0]
    m2 = {}
    for n, i in enumerate(FIRST):
        a, b = push(i, n)
        s, d = a + b, a - b
        de = (0.5 - PLUS) * s
        do = (0.5 - MINUS) * d
        out_ref[i, x_index] = de + do
        out_ref[i + 1, x_index] = de - do
        w = weight(i)
        s = (2.0 * PLUS * w) * s
        d = (2.0 * MINUS * w) * d
        total = total + s
        c = LATTICE[i]
        for axis in range(3):
            if c[axis]:
                m1[axis] = m1[axis] + d if c[axis] > 0 else m1[axis] - d
            for other in range(axis, 3):
                sign = c[axis] * c[other]
                if sign:
                    old = m2.get((axis, other))
                    if old is None:
                        m2[axis, other] = s if sign > 0 else -s
                    else:
                        m2[axis, other] = old + s if sign > 0 else old - s
    h0 = fluid * adj(NF, 0)
    hsum = V0 * h0
    h1 = []
    hs = None
    for n, k in enumerate((1, 3, 5)):
        a, b = push(NF + k, n)
        hs = a + b if hs is None else hs + (a + b)
        h1.append(V1 * (a - b))
    hsum = hsum + V1 * hs

    base = 1.0 - 1.5 * (vx * vx + uy * uy + uz * uz)
    tx = m2[0, 0] * vx + m2[0, 1] * uy + m2[0, 2] * uz
    ty = m2[0, 1] * vx + m2[1, 1] * uy + m2[1, 2] * uz
    tz = m2[0, 2] * vx + m2[1, 2] * uy + m2[2, 2] * uz
    rhobar = (
        total * base
        + 4.5 * (vx * tx + uy * ty + uz * tz)
        + 3.0 * (m1[0] * vx + m1[1] * uy + m1[2] * uz)
    )
    total3 = 3.0 * total
    vxbar = rho * (9.0 * tx + 3.0 * m1[0] - total3 * vx)
    uybar = rho * (9.0 * ty + 3.0 * m1[1] - total3 * uy)
    uzbar = rho * (9.0 * tz + 3.0 * m1[2] - total3 * uz)
    slope = 4.0 * bval
    forcebar = (TAU_PLUS * vxbar) * inv
    rhobar = rhobar - forcebar * force * inv
    currentbar = (COUPLE * bcell) * forcebar
    shearbar = (SOURCE * bcell) * hsum
    dcell = COUPLE * current * forcebar + SOURCE * shear * hsum
    uxbar = vxbar + slope * h1[0]
    uybar = uybar + slope * h1[1] - bval * currentbar - momx * shearbar
    uzbar = uzbar + slope * h1[2]
    bbar = hsum + 4.0 * (h1[0] * ux + h1[1] * uy + h1[2] * uz) - uy * currentbar
    mxbar = uxbar * inv - uy * shearbar
    mybar = uybar * inv
    mzbar = uzbar * inv
    rhobar = rhobar - (ux * uxbar + uy * uybar + uz * uzbar) * inv

    out_ref[0, x_index] = out_ref[0, x_index] + rhobar
    for i in FIRST:
        cm = along(i, mxbar, mybar, mzbar)
        cx, cy, _ = LATTICE[i]
        common = rhobar
        if cx and cy:
            common = rhobar + shearbar if cx * cy > 0 else rhobar - shearbar
        out_ref[i, x_index] = out_ref[i, x_index] + (common + cm)
        out_ref[i + 1, x_index] = out_ref[i + 1, x_index] + (common - cm)
    for k in range(NG):
        value = bbar
        if k == 3:
            value = bbar + currentbar
        elif k == 4:
            value = bbar - currentbar
        out_ref[NF + k, x_index] = value

    share = dcell * profile
    for m in range(count):
        hit = jnp.where(magnet == m, share, 0.0)
        part = hit[:, 0:128]
        for z in range(128, sz, 128):
            part = part + hit[:, z : z + 128]
        sums_ref[m] = sums_ref[m] + part


def halo_slot(kind, i, dy):
    names = (UP, DOWN) if (dy == -1) == (kind == 0) else (DOWN, UP)
    return names[0].index(i) + 6 * kind


def face_slot(kind, i, dx):
    names = RIGHT if (dx == -1) == (kind == 0) else LEFT
    return names.index(i) + 6 * kind


def adj_plane(adjf_ref, adjg_ref, i, x):
    return adjf_ref[i, x] if i < NF else adjg_ref[i - NF, x]


def load_halo(first_ref, second_ref, halo_ref):
    odd = lax.rem(lax.axis_index("gy"), 2)
    halo_ref[1 - odd] = first_ref[...]
    halo_ref[odd] = second_ref[...]
    here = lax.axis_index("gy")
    keep_low = jnp.where(here == 0, 0.0, 1.0)
    keep_high = jnp.where(here == lax.axis_size("gy") - 1, 0.0, 1.0)
    halo_ref[0, MASK] = halo_ref[0, MASK] * keep_low
    halo_ref[1, MASK] = halo_ref[1, MASK] * keep_high
    return keep_low, keep_high


def plane_stores(n, x, new_v, out_v, newf_ref, newg_ref, outf_ref, outg_ref, sem):
    pairs = (
        (new_v.at[pl.ds(0, NF), n], newf_ref.at[:, x]),
        (new_v.at[pl.ds(NF, NG), n], newg_ref.at[:, x]),
        (out_v.at[pl.ds(0, NF), n], outf_ref.at[:, x]),
        (out_v.at[pl.ds(NF, NG), n], outg_ref.at[:, x]),
    )
    return [pltpu.make_async_copy(a, b, sem.at[k, n]) for k, (a, b) in enumerate(pairs)]


def inner_kernel(
    post_ref, adjf_ref, adjg_ref, fluid_ref, bcell_ref, first_ref, second_ref, profile_ref,
    magnet_ref,
    newf_ref, newg_ref, outf_ref, outg_ref, sums_ref,
    new_v, out_v, halo_v, near_v, store_sem,
):
    sx = fluid_ref.shape[0]
    count = sums_ref.shape[0]

    def stores(x):
        return plane_stores(
            x, x, new_v, out_v, newf_ref, newg_ref, outf_ref, outg_ref, store_sem
        )

    sums_ref[...] = jnp.zeros_like(sums_ref)
    load_halo(first_ref, second_ref, halo_v)

    def body(x, carry):
        def row_of(slot, dx, dy):
            return halo_v[0 if dy == -1 else 1, slot, pl.ds(x + dx, 1), :]

        plane_step(
            x,
            lambda i, dx: post_ref[i, x + dx],
            lambda i, dx, dy: row_of(halo_slot(0, i, dy), dx, dy),
            lambda i, dx: adj_plane(adjf_ref, adjg_ref, i, x + dx),
            lambda i, dx, dy: row_of(halo_slot(1, i, dy), dx, dy),
            lambda dx: fluid_ref[x + dx],
            lambda dx, dy: row_of(MASK, dx, dy),
            fluid_ref[x],
            bcell_ref[x],
            profile_ref[x],
            magnet_ref[x],
            near_v,
            new_v,
            out_v,
            sums_ref,
            count,
        )
        start_all(stores(x))
        return carry

    lax.fori_loop(1, sx - 1, body, 0)
    for x in range(1, sx - 1):
        wait_all(stores(x))


def inner_call(post, adjf, adjg, fluid, bcell, first, second, profile, magnet, count):
    sx, sy, sz = profile.shape
    full = pltpu.VMEM((NP, sx, sy, sz), jnp.float32)
    flow = jax.ShapeDtypeStruct((NF, sx, sy, sz), jnp.float32)
    field = jax.ShapeDtypeStruct((NG, sx, sy, sz), jnp.float32)
    return pl.pallas_call(
        inner_kernel,
        in_specs=[VMEM] * 9,
        out_specs=[ANY, ANY, ANY, ANY, VMEM],
        out_shape=[flow, field, flow, field, pltpu.VMEM((count, 8, 128), jnp.float32)],
        scratch_shapes=[
            full,
            full,
            pltpu.VMEM((2, SLOTS, sx, sz), jnp.float32),
            pltpu.VMEM((18, sy, sz), jnp.float32),
            pltpu.SemaphoreType.DMA((4, sx)),
        ],
        compiler_params=pltpu.CompilerParams(vmem_limit_bytes=INNER_VMEM),
        cost_estimate=pl.CostEstimate(
            flops=700 * sx * sy * sz, bytes_accessed=16 * NP * sx * sy * sz, transcendentals=0
        ),
        name="inner",
    )(post, adjf, adjg, fluid, bcell, first, second, profile, magnet)


def outer_kernel(
    scale, post_ref, adjf_ref, adjg_ref, fluid_ref, bcell_ref, first_ref, second_ref, fromleft_ref, fromright_ref,
    cornerleft_ref, cornerright_ref, profile_ref, magnet_ref,
    partial_ref, newf_in, newg_in, outf_in, outg_in,
    newf_ref, newg_ref, outf_ref, outg_ref, share_ref,
    new_v, out_v, halo_v, near_v, sums_v, store_sem,
):
    del newf_in, newg_in, outf_in, outg_in
    sx = fluid_ref.shape[0]
    count = sums_v.shape[0]
    sums_v[...] = partial_ref[...]
    keep_low, keep_high = load_halo(first_ref, second_ref, halo_v)
    stores = []
    for n, (x, away) in enumerate(((0, -1), (sx - 1, 1))):
        face_ref, corner_ref = (
            (fromleft_ref, cornerleft_ref) if away == -1 else (fromright_ref, cornerright_ref)
        )

        def get(kind, i, dx, x=x, away=away, face_ref=face_ref):
            if dx == away:
                return face_ref[face_slot(kind, i, dx)]
            if kind == 1:
                return adj_plane(adjf_ref, adjg_ref, i, x + dx)
            return post_ref[i, x + dx]

        def row(kind, i, dx, dy, x=x, away=away, corner_ref=corner_ref):
            side = 0 if dy == -1 else 1
            if dx == away:
                line = corner_ref[2 * kind + side : 2 * kind + side + 1, :]
                if kind == 2:
                    line = line * (keep_low if side == 0 else keep_high)
                return line
            slot = MASK if kind == 2 else halo_slot(kind, i, dy)
            return halo_v[side, slot, x + dx : x + dx + 1, :]

        def mask(dx, x=x, away=away, face_ref=face_ref):
            return face_ref[MASK] if dx == away else fluid_ref[x + dx]

        plane_step(
            n,
            lambda i, dx, get=get: get(0, i, dx),
            lambda i, dx, dy, row=row: row(0, i, dx, dy),
            lambda i, dx, get=get: get(1, i, dx),
            lambda i, dx, dy, row=row: row(1, i, dx, dy),
            mask,
            lambda dx, dy, row=row: row(2, 0, dx, dy),
            fluid_ref[x],
            bcell_ref[x],
            profile_ref[x],
            magnet_ref[x],
            near_v,
            new_v,
            out_v,
            sums_v,
            count,
        )
        these = plane_stores(
            n, x, new_v, out_v, newf_ref, newg_ref, outf_ref, outg_ref, store_sem
        )
        start_all(these)
        stores += these
    rows = jnp.concatenate(
        [jnp.sum(sums_v[m], axis=0, keepdims=True) for m in range(count)], axis=0
    )
    share_ref[...] = lax.dot_general(
        jnp.ones((share_ref.shape[0], 128), jnp.float32),
        rows * scale,
        (((1,), (1,)), ((), ())),
        precision=lax.Precision.HIGHEST,
        preferred_element_type=jnp.float32,
    )
    wait_all(stores)


def outer_call(
    post, adjf, adjg, fluid, bcell, first, second, fromleft, fromright, cornerleft, cornerright,
    profile, magnet, partial, newf, newg, outf, outg, scale,
):
    sx, sy, sz = profile.shape
    count = partial.shape[0]
    flow = jax.ShapeDtypeStruct(newf.shape, jnp.float32)
    field = jax.ShapeDtypeStruct(newg.shape, jnp.float32)
    return pl.pallas_call(
        functools.partial(outer_kernel, scale),
        in_specs=[VMEM] * 14 + [ANY] * 4,
        out_specs=[ANY] * 4 + [VMEM],
        out_shape=[
            flow,
            field,
            flow,
            field,
            jax.ShapeDtypeStruct((lax.axis_size(("gx", "gy")), count), jnp.float32),
        ],
        input_output_aliases={14: 0, 15: 1, 16: 2, 17: 3},
        scratch_shapes=[
            pltpu.VMEM((NP, 2, sy, sz), jnp.float32),
            pltpu.VMEM((NP, 2, sy, sz), jnp.float32),
            pltpu.VMEM((2, SLOTS, sx, sz), jnp.float32),
            pltpu.VMEM((18, sy, sz), jnp.float32),
            pltpu.VMEM((count, 8, 128), jnp.float32),
            pltpu.SemaphoreType.DMA((4, 2)),
        ],
        compiler_params=pltpu.CompilerParams(vmem_limit_bytes=OUTER_VMEM),
        name="outer",
    )(
        post, adjf, adjg, fluid, bcell, first, second, fromleft, fromright, cornerleft, cornerright,
        profile, magnet, partial, newf, newg, outf, outg,
    )


def ring(count, step):
    return [(i, (i + step) % count) for i in range(count)]


def on_device(flow, field, adj_flow_in, adj_field_in, profile, strengths, wall, magnet):
    across, around = lax.axis_size("gy"), lax.axis_size("gx")
    count = strengths.shape[0]
    table = strengths.reshape(1, count)
    arrays = (flow, field, adj_flow_in, adj_field_in, profile, table, wall, magnet)
    mine1, mine2, right, left = rim_call(*arrays)
    inside = [(i, i ^ 1) for i in range(across)]
    between = [(i, (((i + 1) ^ 1) - 1) % across) for i in range(across)]
    second = lax.ppermute(mine2, "gy", between)
    first = lax.ppermute(mine1, "gy", inside)
    fromleft = lax.ppermute(right, "gx", ring(around, 1))
    fromright = lax.ppermute(left, "gx", ring(around, -1))
    post, fluid, bcell = collide_call(flow, field, profile, table, wall, magnet)
    corner_r, corner_l = corner_call(first, second, bcell)
    cornerleft = lax.ppermute(corner_r, "gx", ring(around, 1))
    cornerright = lax.ppermute(corner_l, "gx", ring(around, -1))
    newf, newg, outf, outg, partial = inner_call(
        post, adj_flow_in, adj_field_in, fluid, bcell, first, second, profile, magnet, count
    )
    cells = flow.shape[1] * around * flow.shape[2] * across * flow.shape[3]
    newf, newg, outf, outg, share = outer_call(
        post, adj_flow_in, adj_field_in, fluid, bcell, first, second, fromleft, fromright, cornerleft, cornerright,
        profile, magnet, partial, newf, newg, outf, outg, 1.0 / math.sqrt(cells / count),
    )
    totals = jnp.sum(lax.all_to_all(share, ("gx", "gy"), 0, 0, tiled=True), axis=0)
    return (newf, newg, outf, outg, totals)


def solution(mesh):
    stack = P(None, "gx", "gy", None)
    cell = P("gx", "gy", None)
    return jax.shard_map(
        on_device,
        mesh=mesh,
        in_specs=(stack, stack, stack, stack, cell, P(), cell, cell),
        out_specs=(stack, stack, stack, stack, P()),
        check_vma=False,
    )
```

```python
import functools
import math

import jax
import jax.numpy as jnp
from jax import lax
from jax.experimental import pallas as pl
from jax.experimental.pallas import tpu as pltpu
from jax.sharding import PartitionSpec as P

LATTICE = [
    (0, 0, 0),
    (1, 0, 0),
    (-1, 0, 0),
    (0, 1, 0),
    (0, -1, 0),
    (0, 0, 1),
    (0, 0, -1),
    (1, 1, 0),
    (-1, -1, 0),
    (1, -1, 0),
    (-1, 1, 0),
    (1, 0, 1),
    (-1, 0, -1),
    (1, 0, -1),
    (-1, 0, 1),
    (0, 1, 1),
    (0, -1, -1),
    (0, 1, -1),
    (0, -1, 1),
]
NF, NG = 19, 7
NP = NF + NG
FIRST = [1, 3, 5, 7, 9, 11, 13, 15, 17]
W0, W1, W2 = 1.0 / 3.0, 1.0 / 18.0, 1.0 / 36.0
V0, V1 = 0.25, 0.125
PLUS = 0.625
MINUS = 0.5 / 1.125
TAU_PLUS = 0.8
COUPLE = 2.0
SOURCE = 2.0

UP = [3, 7, 10, 15, 17, NF + 3]
DOWN = [4, 8, 9, 16, 18, NF + 4]
RIGHT = [1, 7, 9, 11, 13, NF + 1]
LEFT = [2, 8, 10, 12, 14, NF + 2]
SLOTS = 13
MASK = 12

RIM_VMEM = 63 << 20
COLLIDE_VMEM = 54 << 20
INNER_VMEM = 12 << 20
OUTER_VMEM = 8 << 20


def weight(i):
    return W1 if i <= 6 else W2


def gather_strength(table, magnet):
    parts = [
        jnp.take_along_axis(table, magnet[:, z : z + 128], axis=1, mode="promise_in_bounds")
        for z in range(0, magnet.shape[1], 128)
    ]
    return jnp.concatenate(parts, axis=1)


def lane_table(strengths_v):
    row = strengths_v[...]
    rest = 128 - row.shape[1]
    if rest:
        row = jnp.concatenate([row, jnp.zeros((1, rest), jnp.float32)], axis=1)
    return jnp.broadcast_to(row, (8, 128))


def vector_sums(pair):
    x = pair[1] + pair[7] + pair[9] + pair[11] + pair[13]
    y = pair[3] + pair[7] - pair[9] + pair[15] + pair[17]
    z = pair[5] + pair[11] - pair[13] + pair[15] - pair[17]
    return x, y, z


def along(i, vx, vy, vz):
    out = None
    for c, v in zip(LATTICE[i], (vx, vy, vz)):
        if c:
            if out is None:
                out = v if c > 0 else -v
            else:
                out = out + v if c > 0 else out - v
    return out


def start_all(copies):
    for c in copies:
        c.start()


def wait_all(copies):
    for c in copies:
        c.wait()


def collide(f, g, fluid, bcell, wanted):
    even = {i: f[i] + f[i + 1] for i in FIRST}
    diff = {i: f[i] - f[i + 1] for i in FIRST}
    rho = f[0] + (1.0 - fluid)
    for i in FIRST:
        rho = rho + even[i]
    momx, momy, momz = vector_sums(diff)
    inv = 1.0 / rho
    ux, uy, uz = momx * inv, momy * inv, momz * inv
    bval = g[0] + g[1] + g[2] + g[3] + g[4] + g[5] + g[6]
    current = (g[3] - g[4]) - bval * uy
    shear = (even[7] - even[9]) - momx * uy
    force = (COUPLE * bcell) * current
    vx = ux + TAU_PLUS * force * inv
    base = 1.0 - 1.5 * (vx * vx + uy * uy + uz * uz)
    post = {}
    if 0 in wanted:
        post[0] = f[0] - 2.0 * PLUS * (f[0] - (W0 * rho) * base)
    rho1, rho2 = W1 * rho, W2 * rho
    for i in FIRST:
        if i not in wanted and i + 1 not in wanted:
            continue
        wr = rho1 if i <= 6 else rho2
        a = along(i, vx, uy, uz)
        ne = PLUS * (even[i] - (2.0 * wr) * (base + 4.5 * a * a))
        no = MINUS * (diff[i] - (6.0 * wr) * a)
        if i in wanted:
            post[i] = f[i] - ne - no
        if i + 1 in wanted:
            post[i + 1] = f[i + 1] - ne + no
    common = bval + (SOURCE * bcell) * shear
    slope = 4.0 * bval
    if NF in wanted:
        post[NF] = V0 * common
    for k, u in ((1, ux), (3, uy), (5, uz)):
        if NF + k in wanted:
            post[NF + k] = V1 * (common + slope * u)
        if NF + k + 1 in wanted:
            post[NF + k + 1] = V1 * (common - slope * u)
    return post


def rim_kernel(
    flow_ref, field_ref, adjf_ref, adjg_ref, profile_ref, strengths_ref, wall_ref, magnet_ref,
    first_ref, second_ref, right_ref, left_ref,
    rows_v, faces_v, profile_v, wall_v, magnet_v, strengths_v, message_v, cell_sem, rows_sem,
    faces_sem, adj_sem,
):
    sx, sy = profile_v.shape[:2]
    odd = lax.rem(lax.axis_index("gy"), 2)
    ends = (sy - 1, 0)
    sides = (0, sx - 1)

    def adj_at(i, where):
        return adjf_ref.at[(i, *where)] if i < NF else adjg_ref.at[(i - NF, *where)]

    rows = []
    for n, y in enumerate(ends):
        rows += [
            pltpu.make_async_copy(
                flow_ref.at[:, :, y], rows_v.at[n, pl.ds(0, NF)], rows_sem.at[n, 0]
            ),
            pltpu.make_async_copy(
                field_ref.at[:, :, y], rows_v.at[n, pl.ds(NF, NG)], rows_sem.at[n, 1]
            ),
        ]
    cells = [
        pltpu.make_async_copy(a, b, cell_sem.at[n])
        for n, (a, b) in enumerate(
            (
                (wall_ref, wall_v),
                (magnet_ref, magnet_v),
                (strengths_ref, strengths_v),
                (profile_ref, profile_v),
            )
        )
    ]
    faces = []
    for n, x in enumerate(sides):
        faces += [
            pltpu.make_async_copy(
                flow_ref.at[:, x], faces_v.at[n, pl.ds(0, NF)], faces_sem.at[n, 0]
            ),
            pltpu.make_async_copy(
                field_ref.at[:, x], faces_v.at[n, pl.ds(NF, NG)], faces_sem.at[n, 1]
            ),
        ]
    adjs = []
    for s in range(6):
        for n, (i, where, out) in enumerate(
            (
                (DOWN[s], (slice(None), ends[0]), message_v.at[0]),
                (UP[s], (slice(None), ends[1]), message_v.at[1]),
                (RIGHT[s], (sides[0],), left_ref),
                (LEFT[s], (sides[1],), right_ref),
            )
        ):
            adjs.append(pltpu.make_async_copy(adj_at(i, where), out.at[6 + s], adj_sem.at[n, s]))
    start_all(rows[:2])
    start_all(cells)
    start_all(rows[2:])
    start_all(faces)
    start_all(adjs)
    wait_all(cells)
    table = lane_table(strengths_v)
    for n, (y, wanted) in enumerate(zip(ends, (UP, DOWN))):
        wait_all(rows[2 * n : 2 * n + 2])
        fluid = 1.0 - wall_v[:, y, :].astype(jnp.float32)
        bcell = gather_strength(table, magnet_v[:, y, :]) * profile_v[:, y, :]
        post = collide(
            [rows_v[n, i] for i in range(NF)],
            [rows_v[n, NF + k] for k in range(NG)],
            fluid,
            bcell,
            wanted,
        )
        for s in range(6):
            message_v[n, s] = post[wanted[s]]
        message_v[n, MASK] = fluid
    for n, (x, wanted, out) in enumerate(
        ((sides[0], LEFT, left_ref), (sides[1], RIGHT, right_ref))
    ):
        wait_all(faces[2 * n : 2 * n + 2])
        fluid = 1.0 - wall_v[x].astype(jnp.float32)
        bcell = gather_strength(table, magnet_v[x]) * profile_v[x]
        post = collide(
            [faces_v[n, i] for i in range(NF)],
            [faces_v[n, NF + k] for k in range(NG)],
            fluid,
            bcell,
            wanted,
        )
        for s in range(6):
            out[s] = post[wanted[s]]
        out[MASK] = fluid
    wait_all(adjs)
    first_ref[...] = message_v[odd]
    second_ref[...] = message_v[1 - odd]


ANY = pl.BlockSpec(memory_space=pl.ANY)
VMEM = pl.BlockSpec(memory_space=pltpu.VMEM)


def rim_call(flow, field, adjf, adjg, profile, strengths, wall, magnet):
    sx, sy, sz = profile.shape
    cells = pltpu.VMEM((sx, sy, sz), jnp.float32)
    names = pltpu.VMEM((sx, sy, sz), jnp.int32)
    rows = pltpu.VMEM((SLOTS, sx, sz), jnp.float32)
    faces = pltpu.VMEM((SLOTS, sy, sz), jnp.float32)
    dma = pltpu.SemaphoreType.DMA
    return pl.pallas_call(
        rim_kernel,
        in_specs=[ANY] * 8,
        out_specs=[VMEM] * 4,
        out_shape=[rows, rows, faces, faces],
        scratch_shapes=[
            pltpu.VMEM((2, NP, sx, sz), jnp.float32),
            pltpu.VMEM((2, NP, sy, sz), jnp.float32),
            cells,
            names,
            names,
            pltpu.VMEM(strengths.shape, jnp.float32),
            pltpu.VMEM((2, SLOTS, sx, sz), jnp.float32),
            dma((4,)),
            dma((2, 2)),
            dma((2, 2)),
            dma((4, 6)),
        ],
        compiler_params=pltpu.CompilerParams(vmem_limit_bytes=RIM_VMEM),
        name="rims",
    )(flow, field, adjf, adjg, profile, strengths, wall, magnet)


def collide_kernel(
    flow_ref, field_ref, profile_ref, strengths_ref, wall_ref, magnet_ref,
    post_ref, fluid_ref, bcell_ref, profile_v, magnet_v,
    flow_v, field_v, wall_v, strengths_v, plane_sem, table_sem,
):
    sx = fluid_ref.shape[0]

    def loads(x):
        pairs = (
            (wall_ref.at[x], wall_v.at[x]),
            (magnet_ref.at[x], magnet_v.at[x]),
            (profile_ref.at[x], profile_v.at[x]),
            (flow_ref.at[:, x], flow_v.at[:, x]),
            (field_ref.at[:, x], field_v.at[:, x]),
        )
        return [pltpu.make_async_copy(a, b, plane_sem.at[n, x]) for n, (a, b) in enumerate(pairs)]

    table_load = pltpu.make_async_copy(strengths_ref, strengths_v, table_sem.at[0])
    table_load.start()
    for x in range(sx):
        start_all(loads(x))
    table_load.wait()
    table = lane_table(strengths_v)

    def body(x, carry):
        wait_all(loads(x))
        fluid = 1.0 - wall_v[x].astype(jnp.float32)
        bcell = gather_strength(table, magnet_v[x]) * profile_v[x]
        fluid_ref[x] = fluid
        bcell_ref[x] = bcell
        f = [flow_v[i, x] for i in range(NF)]
        g = [field_v[k, x] for k in range(NG)]
        for i, value in collide(f, g, fluid, bcell, range(NP)).items():
            post_ref[i, x] = value
        return carry

    lax.fori_loop(0, sx, body, 0)


def collide_call(flow, field, profile, strengths, wall, magnet):
    sx, sy, sz = profile.shape
    cells = pltpu.VMEM((sx, sy, sz), jnp.float32)
    names = pltpu.VMEM((sx, sy, sz), jnp.int32)
    return pl.pallas_call(
        collide_kernel,
        in_specs=[ANY] * 6,
        out_specs=[VMEM] * 5,
        out_shape=[
            pltpu.VMEM((NP, sx, sy, sz), jnp.float32),
            cells,
            cells,
            cells,
            names,
        ],
        scratch_shapes=[
            pltpu.VMEM(flow.shape, jnp.float32),
            pltpu.VMEM(field.shape, jnp.float32),
            names,
            pltpu.VMEM(strengths.shape, jnp.float32),
            pltpu.SemaphoreType.DMA((5, sx)),
            pltpu.SemaphoreType.DMA((1,)),
        ],
        compiler_params=pltpu.CompilerParams(vmem_limit_bytes=COLLIDE_VMEM),
        cost_estimate=pl.CostEstimate(
            flops=300 * sx * sy * sz, bytes_accessed=12 * NP * sx * sy * sz, transcendentals=0
        ),
        name="collide",
    )(flow, field, profile, strengths, wall, magnet)


CORNER_RIGHT = ((0, 7, 0, 8), (1, 9, 1, 10))
CORNER_LEFT = ((0, 10, 0, 9), (1, 8, 1, 7))


def corner_slots(side, post, adj):
    posts, adjs = (UP, DOWN) if side == 0 else (DOWN, UP)
    return posts.index(post), 6 + adjs.index(adj), MASK


def corner_kernel(first_ref, second_ref, after_ref, right_ref, left_ref):
    del after_ref
    odd = lax.rem(lax.axis_index("gy"), 2) == 1
    sx = first_ref.shape[1]

    def row(side, slot, x):
        a, b = first_ref[slot, x : x + 1, :], second_ref[slot, x : x + 1, :]
        return jnp.where(odd, a, b) if side == 0 else jnp.where(odd, b, a)

    for out, table, x in ((right_ref, CORNER_RIGHT, sx - 1), (left_ref, CORNER_LEFT, 0)):
        out[...] = jnp.zeros_like(out)
        for side, post, _, adj in table:
            for n, slot in enumerate(corner_slots(side, post, adj)):
                out[2 * n + side : 2 * n + side + 1, :] = row(side, slot, x)


def corner_call(first, second, after):
    sz = first.shape[2]
    out = pltpu.VMEM((8, sz), jnp.float32)
    return pl.pallas_call(
        corner_kernel,
        in_specs=[VMEM, VMEM, ANY],
        out_specs=[VMEM, VMEM],
        out_shape=[out, out],
        compiler_params=pltpu.CompilerParams(vmem_limit_bytes=2 << 20),
        name="corners",
    )(first, second, after)


def plane_step(
    x_index, post, post_row, adj, adj_row, mask, mask_row, fluid, bcell, profile, magnet,
    near_ref, new_ref, out_ref, sums_ref, count, new_done, out_done,
):
    sy, sz = fluid.shape
    yi = lax.broadcasted_iota(jnp.int32, (sy, sz), 0)
    zi = lax.broadcasted_iota(jnp.int32, (sy, sz), 1)
    top, bottom = yi == sy - 1, yi == 0
    zlast, zfirst = zi == sz - 1, zi == 0

    def shift(value, row, dy, dz):
        if dy == -1:
            value = jnp.where(bottom, row(), pltpu.roll(value, 1, 0))
        elif dy == 1:
            value = jnp.where(top, row(), pltpu.roll(value, sy - 1, 0))
        if dz == -1:
            value = pltpu.roll(value, 1, 1)
        elif dz == 1:
            value = pltpu.roll(value, sz - 1, 1)
        return value

    def moved(get, get_row, i, sign):
        dx, dy, dz = (sign * c for c in LATTICE[i if i < NF else i - NF])
        return shift(get(i, dx), lambda: get_row(i, dx, dy), dy, dz)

    def near_of(i, sign):
        dx, dy, dz = (sign * c for c in LATTICE[i])
        value = shift(mask(dx), lambda: mask_row(dx, dy), dy, dz)
        if dz == -1:
            value = jnp.where(zfirst, 0.0, value)
        elif dz == 1:
            value = jnp.where(zlast, 0.0, value)
        return value

    for n, i in enumerate(FIRST):
        near_ref[2 * n] = near_of(i, -1)
        near_ref[2 * n + 1] = near_of(i, 1)

    def near(n):
        return near_ref[2 * n] > 0.5, near_ref[2 * n + 1] > 0.5

    def pull(i, n):
        minus, plus = near(n)
        a = fluid * jnp.where(minus, moved(post, post_row, i, -1), post(i + 1, 0))
        b = fluid * jnp.where(plus, moved(post, post_row, i + 1, -1), post(i, 0))
        new_ref[i, x_index] = a
        new_ref[i + 1, x_index] = b
        return a, b

    f0 = fluid * post(0, 0)
    new_ref[0, x_index] = f0
    rho = f0 + (1.0 - fluid)
    momx = momy = momz = shear0 = 0.0
    for n, i in enumerate(FIRST):
        a, b = pull(i, n)
        s, d = a + b, a - b
        rho = rho + s
        cx, cy, cz = LATTICE[i]
        if cx:
            momx = momx + d
        if cy:
            momy = momy + d if cy > 0 else momy - d
        if cz:
            momz = momz + d if cz > 0 else momz - d
        if cx and cy:
            shear0 = shear0 + s if cx * cy > 0 else shear0 - s
    g0 = fluid * post(NF, 0)
    new_ref[NF, x_index] = g0
    bval = g0
    gy = None
    for n, k in enumerate((1, 3, 5)):
        a, b = pull(NF + k, n)
        bval = bval + (a + b)
        if k == 3:
            gy = a - b
    new_done()
    inv = 1.0 / rho
    ux, uy, uz = momx * inv, momy * inv, momz * inv
    current = gy - bval * uy
    shear = shear0 - momx * uy
    force = (COUPLE * bcell) * current
    vx = ux + TAU_PLUS * force * inv

    def push(i, n):
        minus, plus = near(n)
        a = fluid * jnp.where(plus, moved(adj, adj_row, i, 1), adj(i + 1, 0))
        b = fluid * jnp.where(minus, moved(adj, adj_row, i + 1, 1), adj(i, 0))
        return a, b

    l0 = fluid * adj(0, 0)
    out_ref[0, x_index] = (1.0 - 2.0 * PLUS) * l0
    total = (2.0 * PLUS * W0) * l0
    m1 = [0.0, 0.0, 0.0]
    m2 = {}
    for n, i in enumerate(FIRST):
        a, b = push(i, n)
        s, d = a + b, a - b
        de = (0.5 - PLUS) * s
        do = (0.5 - MINUS) * d
        out_ref[i, x_index] = de + do
        out_ref[i + 1, x_index] = de - do
        w = weight(i)
        s = (2.0 * PLUS * w) * s
        d = (2.0 * MINUS * w) * d
        total = total + s
        c = LATTICE[i]
        for axis in range(3):
            if c[axis]:
                m1[axis] = m1[axis] + d if c[axis] > 0 else m1[axis] - d
            for other in range(axis, 3):
                sign = c[axis] * c[other]
                if sign:
                    old = m2.get((axis, other))
                    if old is None:
                        m2[axis, other] = s if sign > 0 else -s
                    else:
                        m2[axis, other] = old + s if sign > 0 else old - s
    h0 = fluid * adj(NF, 0)
    hsum = V0 * h0
    h1 = []
    hs = None
    for n, k in enumerate((1, 3, 5)):
        a, b = push(NF + k, n)
        hs = a + b if hs is None else hs + (a + b)
        h1.append(V1 * (a - b))
    hsum = hsum + V1 * hs

    base = 1.0 - 1.5 * (vx * vx + uy * uy + uz * uz)
    tx = m2[0, 0] * vx + m2[0, 1] * uy + m2[0, 2] * uz
    ty = m2[0, 1] * vx + m2[1, 1] * uy + m2[1, 2] * uz
    tz = m2[0, 2] * vx + m2[1, 2] * uy + m2[2, 2] * uz
    rhobar = (
        total * base
        + 4.5 * (vx * tx + uy * ty + uz * tz)
        + 3.0 * (m1[0] * vx + m1[1] * uy + m1[2] * uz)
    )
    total3 = 3.0 * total
    vxbar = rho * (9.0 * tx + 3.0 * m1[0] - total3 * vx)
    uybar = rho * (9.0 * ty + 3.0 * m1[1] - total3 * uy)
    uzbar = rho * (9.0 * tz + 3.0 * m1[2] - total3 * uz)
    slope = 4.0 * bval
    forcebar = (TAU_PLUS * vxbar) * inv
    rhobar = rhobar - forcebar * force * inv
    currentbar = (COUPLE * bcell) * forcebar
    shearbar = (SOURCE * bcell) * hsum
    dcell = COUPLE * current * forcebar + SOURCE * shear * hsum
    uxbar = vxbar + slope * h1[0]
    uybar = uybar + slope * h1[1] - bval * currentbar - momx * shearbar
    uzbar = uzbar + slope * h1[2]
    bbar = hsum + 4.0 * (h1[0] * ux + h1[1] * uy + h1[2] * uz) - uy * currentbar
    mxbar = uxbar * inv - uy * shearbar
    mybar = uybar * inv
    mzbar = uzbar * inv
    rhobar = rhobar - (ux * uxbar + uy * uybar + uz * uzbar) * inv

    out_ref[0, x_index] = out_ref[0, x_index] + rhobar
    for i in FIRST:
        cm = along(i, mxbar, mybar, mzbar)
        cx, cy, _ = LATTICE[i]
        common = rhobar
        if cx and cy:
            common = rhobar + shearbar if cx * cy > 0 else rhobar - shearbar
        out_ref[i, x_index] = out_ref[i, x_index] + (common + cm)
        out_ref[i + 1, x_index] = out_ref[i + 1, x_index] + (common - cm)
    for k in range(NG):
        value = bbar
        if k == 3:
            value = bbar + currentbar
        elif k == 4:
            value = bbar - currentbar
        out_ref[NF + k, x_index] = value

    out_done()

    share = dcell * profile
    for m in range(count):
        hit = jnp.where(magnet == m, share, 0.0)
        part = hit[:, 0:128]
        for z in range(128, sz, 128):
            part = part + hit[:, z : z + 128]
        sums_ref[m] = sums_ref[m] + part


def halo_slot(kind, i, dy):
    names = (UP, DOWN) if (dy == -1) == (kind == 0) else (DOWN, UP)
    return names[0].index(i) + 6 * kind


def face_slot(kind, i, dx):
    names = RIGHT if (dx == -1) == (kind == 0) else LEFT
    return names.index(i) + 6 * kind


def adj_plane(adjf_ref, adjg_ref, i, x):
    return adjf_ref[i, x] if i < NF else adjg_ref[i - NF, x]


def load_halo(first_ref, second_ref, halo_ref):
    odd = lax.rem(lax.axis_index("gy"), 2)
    halo_ref[1 - odd] = first_ref[...]
    halo_ref[odd] = second_ref[...]
    here = lax.axis_index("gy")
    keep_low = jnp.where(here == 0, 0.0, 1.0)
    keep_high = jnp.where(here == lax.axis_size("gy") - 1, 0.0, 1.0)
    halo_ref[0, MASK] = halo_ref[0, MASK] * keep_low
    halo_ref[1, MASK] = halo_ref[1, MASK] * keep_high
    return keep_low, keep_high


def plane_stores(n, x, new_v, out_v, newf_ref, newg_ref, outf_ref, outg_ref, sem):
    pairs = (
        (new_v.at[pl.ds(0, NF), n], newf_ref.at[:, x]),
        (new_v.at[pl.ds(NF, NG), n], newg_ref.at[:, x]),
        (out_v.at[pl.ds(0, NF), n], outf_ref.at[:, x]),
        (out_v.at[pl.ds(NF, NG), n], outg_ref.at[:, x]),
    )
    return [pltpu.make_async_copy(a, b, sem.at[k, n]) for k, (a, b) in enumerate(pairs)]


def inner_kernel(
    post_ref, adjf_ref, adjg_ref, fluid_ref, bcell_ref, first_ref, second_ref, profile_ref,
    magnet_ref,
    newf_ref, newg_ref, outf_ref, outg_ref, sums_ref,
    new_v, out_v, halo_v, near_v, store_sem,
):
    sx = fluid_ref.shape[0]
    count = sums_ref.shape[0]

    def stores(x):
        return plane_stores(
            x, x, new_v, out_v, newf_ref, newg_ref, outf_ref, outg_ref, store_sem
        )

    sums_ref[...] = jnp.zeros_like(sums_ref)
    load_halo(first_ref, second_ref, halo_v)

    def body(x, carry):
        def row_of(slot, dx, dy):
            return halo_v[0 if dy == -1 else 1, slot, pl.ds(x + dx, 1), :]

        plane_step(
            x,
            lambda i, dx: post_ref[i, x + dx],
            lambda i, dx, dy: row_of(halo_slot(0, i, dy), dx, dy),
            lambda i, dx: adj_plane(adjf_ref, adjg_ref, i, x + dx),
            lambda i, dx, dy: row_of(halo_slot(1, i, dy), dx, dy),
            lambda dx: fluid_ref[x + dx],
            lambda dx, dy: row_of(MASK, dx, dy),
            fluid_ref[x],
            bcell_ref[x],
            profile_ref[x],
            magnet_ref[x],
            near_v,
            new_v,
            out_v,
            sums_ref,
            count,
            lambda: start_all(stores(x)[:2]),
            lambda: start_all(stores(x)[2:]),
        )
        return carry

    lax.fori_loop(1, sx - 1, body, 0)
    for x in range(1, sx - 1):
        wait_all(stores(x))


def inner_call(post, adjf, adjg, fluid, bcell, first, second, profile, magnet, count):
    sx, sy, sz = profile.shape
    full = pltpu.VMEM((NP, sx, sy, sz), jnp.float32)
    flow = jax.ShapeDtypeStruct((NF, sx, sy, sz), jnp.float32)
    field = jax.ShapeDtypeStruct((NG, sx, sy, sz), jnp.float32)
    return pl.pallas_call(
        inner_kernel,
        in_specs=[VMEM] * 9,
        out_specs=[ANY, ANY, ANY, ANY, VMEM],
        out_shape=[flow, field, flow, field, pltpu.VMEM((count, 8, 128), jnp.float32)],
        scratch_shapes=[
            full,
            full,
            pltpu.VMEM((2, SLOTS, sx, sz), jnp.float32),
            pltpu.VMEM((18, sy, sz), jnp.float32),
            pltpu.SemaphoreType.DMA((4, sx)),
        ],
        compiler_params=pltpu.CompilerParams(vmem_limit_bytes=INNER_VMEM),
        cost_estimate=pl.CostEstimate(
            flops=700 * sx * sy * sz, bytes_accessed=16 * NP * sx * sy * sz, transcendentals=0
        ),
        name="inner",
    )(post, adjf, adjg, fluid, bcell, first, second, profile, magnet)


def outer_kernel(
    scale, post_ref, adjf_ref, adjg_ref, fluid_ref, bcell_ref, first_ref, second_ref, fromleft_ref, fromright_ref,
    cornerleft_ref, cornerright_ref, profile_ref, magnet_ref,
    partial_ref, newf_in, newg_in, outf_in, outg_in,
    newf_ref, newg_ref, outf_ref, outg_ref, share_ref,
    new_v, out_v, halo_v, near_v, sums_v, store_sem,
):
    del newf_in, newg_in, outf_in, outg_in
    sx = fluid_ref.shape[0]
    count = sums_v.shape[0]
    sums_v[...] = partial_ref[...]
    keep_low, keep_high = load_halo(first_ref, second_ref, halo_v)
    stores = []
    for n, (x, away) in enumerate(((0, -1), (sx - 1, 1))):
        these = plane_stores(
            n, x, new_v, out_v, newf_ref, newg_ref, outf_ref, outg_ref, store_sem
        )
        stores += these
        face_ref, corner_ref = (
            (fromleft_ref, cornerleft_ref) if away == -1 else (fromright_ref, cornerright_ref)
        )

        def get(kind, i, dx, x=x, away=away, face_ref=face_ref):
            if dx == away:
                return face_ref[face_slot(kind, i, dx)]
            if kind == 1:
                return adj_plane(adjf_ref, adjg_ref, i, x + dx)
            return post_ref[i, x + dx]

        def row(kind, i, dx, dy, x=x, away=away, corner_ref=corner_ref):
            side = 0 if dy == -1 else 1
            if dx == away:
                line = corner_ref[2 * kind + side : 2 * kind + side + 1, :]
                if kind == 2:
                    line = line * (keep_low if side == 0 else keep_high)
                return line
            slot = MASK if kind == 2 else halo_slot(kind, i, dy)
            return halo_v[side, slot, x + dx : x + dx + 1, :]

        def mask(dx, x=x, away=away, face_ref=face_ref):
            return face_ref[MASK] if dx == away else fluid_ref[x + dx]

        plane_step(
            n,
            lambda i, dx, get=get: get(0, i, dx),
            lambda i, dx, dy, row=row: row(0, i, dx, dy),
            lambda i, dx, get=get: get(1, i, dx),
            lambda i, dx, dy, row=row: row(1, i, dx, dy),
            mask,
            lambda dx, dy, row=row: row(2, 0, dx, dy),
            fluid_ref[x],
            bcell_ref[x],
            profile_ref[x],
            magnet_ref[x],
            near_v,
            new_v,
            out_v,
            sums_v,
            count,
            lambda these=these: start_all(these[:2]),
            lambda these=these: start_all(these[2:]),
        )
    rows = jnp.concatenate(
        [jnp.sum(sums_v[m], axis=0, keepdims=True) for m in range(count)], axis=0
    )
    share_ref[...] = lax.dot_general(
        jnp.ones((share_ref.shape[0], 128), jnp.float32),
        rows * scale,
        (((1,), (1,)), ((), ())),
        precision=lax.Precision.HIGHEST,
        preferred_element_type=jnp.float32,
    )
    wait_all(stores)


def outer_call(
    post, adjf, adjg, fluid, bcell, first, second, fromleft, fromright, cornerleft, cornerright,
    profile, magnet, partial, newf, newg, outf, outg, scale,
):
    sx, sy, sz = profile.shape
    count = partial.shape[0]
    flow = jax.ShapeDtypeStruct(newf.shape, jnp.float32)
    field = jax.ShapeDtypeStruct(newg.shape, jnp.float32)
    return pl.pallas_call(
        functools.partial(outer_kernel, scale),
        in_specs=[VMEM] * 14 + [ANY] * 4,
        out_specs=[ANY] * 4 + [VMEM],
        out_shape=[
            flow,
            field,
            flow,
            field,
            jax.ShapeDtypeStruct((lax.axis_size(("gx", "gy")), count), jnp.float32),
        ],
        input_output_aliases={14: 0, 15: 1, 16: 2, 17: 3},
        scratch_shapes=[
            pltpu.VMEM((NP, 2, sy, sz), jnp.float32),
            pltpu.VMEM((NP, 2, sy, sz), jnp.float32),
            pltpu.VMEM((2, SLOTS, sx, sz), jnp.float32),
            pltpu.VMEM((18, sy, sz), jnp.float32),
            pltpu.VMEM((count, 8, 128), jnp.float32),
            pltpu.SemaphoreType.DMA((4, 2)),
        ],
        compiler_params=pltpu.CompilerParams(vmem_limit_bytes=OUTER_VMEM),
        name="outer",
    )(
        post, adjf, adjg, fluid, bcell, first, second, fromleft, fromright, cornerleft, cornerright,
        profile, magnet, partial, newf, newg, outf, outg,
    )


def ring(count, step):
    return [(i, (i + step) % count) for i in range(count)]


def on_device(flow, field, adj_flow_in, adj_field_in, profile, strengths, wall, magnet):
    across, around = lax.axis_size("gy"), lax.axis_size("gx")
    count = strengths.shape[0]
    table = strengths.reshape(1, count)
    arrays = (flow, field, adj_flow_in, adj_field_in, profile, table, wall, magnet)
    mine1, mine2, right, left = rim_call(*arrays)
    inside = [(i, i ^ 1) for i in range(across)]
    between = [(i, (((i + 1) ^ 1) - 1) % across) for i in range(across)]
    second = lax.ppermute(mine2, "gy", between)
    first = lax.ppermute(mine1, "gy", inside)
    fromleft = lax.ppermute(right, "gx", ring(around, 1))
    fromright = lax.ppermute(left, "gx", ring(around, -1))
    post, fluid, bcell, profile, magnet = collide_call(flow, field, profile, table, wall, magnet)
    corner_r, corner_l = corner_call(first, second, bcell)
    cornerleft = lax.ppermute(corner_r, "gx", ring(around, 1))
    cornerright = lax.ppermute(corner_l, "gx", ring(around, -1))
    newf, newg, outf, outg, partial = inner_call(
        post, adj_flow_in, adj_field_in, fluid, bcell, first, second, profile, magnet, count
    )
    cells = flow.shape[1] * around * flow.shape[2] * across * flow.shape[3]
    newf, newg, outf, outg, share = outer_call(
        post, adj_flow_in, adj_field_in, fluid, bcell, first, second, fromleft, fromright, cornerleft, cornerright,
        profile, magnet, partial, newf, newg, outf, outg, 1.0 / math.sqrt(cells / count),
    )
    totals = jnp.sum(lax.all_to_all(share, ("gx", "gy"), 0, 0, tiled=True), axis=0)
    return (newf, newg, outf, outg, totals)


def solution(mesh):
    stack = P(None, "gx", "gy", None)
    cell = P("gx", "gy", None)
    return jax.shard_map(
        on_device,
        mesh=mesh,
        in_specs=(stack, stack, stack, stack, cell, P(), cell, cell),
        out_specs=(stack, stack, stack, stack, P()),
        check_vma=False,
    )
```

```python
import functools
import math

import jax
import jax.numpy as jnp
from jax import lax
from jax.experimental import pallas as pl
from jax.experimental.pallas import tpu as pltpu
from jax.sharding import PartitionSpec as P

LATTICE = [
    (0, 0, 0),
    (1, 0, 0),
    (-1, 0, 0),
    (0, 1, 0),
    (0, -1, 0),
    (0, 0, 1),
    (0, 0, -1),
    (1, 1, 0),
    (-1, -1, 0),
    (1, -1, 0),
    (-1, 1, 0),
    (1, 0, 1),
    (-1, 0, -1),
    (1, 0, -1),
    (-1, 0, 1),
    (0, 1, 1),
    (0, -1, -1),
    (0, 1, -1),
    (0, -1, 1),
]
NF, NG = 19, 7
NP = NF + NG
FIRST = [1, 3, 5, 7, 9, 11, 13, 15, 17]
W0, W1, W2 = 1.0 / 3.0, 1.0 / 18.0, 1.0 / 36.0
V0, V1 = 0.25, 0.125
PLUS = 0.625
MINUS = 0.5 / 1.125
TAU_PLUS = 0.8
COUPLE = 2.0
SOURCE = 2.0

UP = [3, 7, 10, 15, 17, NF + 3]
DOWN = [4, 8, 9, 16, 18, NF + 4]
RIGHT = [1, 7, 9, 11, 13, NF + 1]
LEFT = [2, 8, 10, 12, 14, NF + 2]
SLOTS = 13
MASK = 12

RIM_VMEM = 58 << 20
COLLIDE_VMEM = 4 << 20
INNER_VMEM = 12 << 20
OUTER_VMEM = 8 << 20


def weight(i):
    return W1 if i <= 6 else W2


def gather_strength(table, magnet):
    parts = [
        jnp.take_along_axis(table, magnet[:, z : z + 128], axis=1, mode="promise_in_bounds")
        for z in range(0, magnet.shape[1], 128)
    ]
    return jnp.concatenate(parts, axis=1)


def lane_table(strengths_ref):
    row = strengths_ref[...]
    rest = 128 - row.shape[1]
    if rest:
        row = jnp.concatenate([row, jnp.zeros((1, rest), jnp.float32)], axis=1)
    return jnp.broadcast_to(row, (8, 128))


def vector_sums(pair):
    x = pair[1] + pair[7] + pair[9] + pair[11] + pair[13]
    y = pair[3] + pair[7] - pair[9] + pair[15] + pair[17]
    z = pair[5] + pair[11] - pair[13] + pair[15] - pair[17]
    return x, y, z


def along(i, vx, vy, vz):
    out = None
    for c, v in zip(LATTICE[i], (vx, vy, vz)):
        if c:
            if out is None:
                out = v if c > 0 else -v
            else:
                out = out + v if c > 0 else out - v
    return out


def start_all(copies):
    for c in copies:
        c.start()


def wait_all(copies):
    for c in copies:
        c.wait()


def collide(f, g, fluid, bcell, wanted):
    even = {i: f[i] + f[i + 1] for i in FIRST}
    diff = {i: f[i] - f[i + 1] for i in FIRST}
    rho = f[0] + (1.0 - fluid)
    for i in FIRST:
        rho = rho + even[i]
    momx, momy, momz = vector_sums(diff)
    inv = 1.0 / rho
    ux, uy, uz = momx * inv, momy * inv, momz * inv
    bval = g[0] + g[1] + g[2] + g[3] + g[4] + g[5] + g[6]
    current = (g[3] - g[4]) - bval * uy
    shear = (even[7] - even[9]) - momx * uy
    force = (COUPLE * bcell) * current
    vx = ux + TAU_PLUS * force * inv
    base = 1.0 - 1.5 * (vx * vx + uy * uy + uz * uz)
    post = {}
    if 0 in wanted:
        post[0] = f[0] - 2.0 * PLUS * (f[0] - (W0 * rho) * base)
    rho1, rho2 = W1 * rho, W2 * rho
    for i in FIRST:
        if i not in wanted and i + 1 not in wanted:
            continue
        wr = rho1 if i <= 6 else rho2
        a = along(i, vx, uy, uz)
        ne = PLUS * (even[i] - (2.0 * wr) * (base + 4.5 * a * a))
        no = MINUS * (diff[i] - (6.0 * wr) * a)
        if i in wanted:
            post[i] = f[i] - ne - no
        if i + 1 in wanted:
            post[i + 1] = f[i + 1] - ne + no
    common = bval + (SOURCE * bcell) * shear
    slope = 4.0 * bval
    if NF in wanted:
        post[NF] = V0 * common
    for k, u in ((1, ux), (3, uy), (5, uz)):
        if NF + k in wanted:
            post[NF + k] = V1 * (common + slope * u)
        if NF + k + 1 in wanted:
            post[NF + k + 1] = V1 * (common - slope * u)
    return post


def rim_kernel(
    flow_ref, field_ref, adjf_ref, adjg_ref, profile_ref, strengths_ref, wall_ref, magnet_ref,
    first_ref, second_ref, right_ref, left_ref,
    rows_v, faces_v, profile_v, wall_v, magnet_v, strengths_v, message_v, cell_sem, rows_sem,
    faces_sem, adj_sem,
):
    sx, sy = profile_v.shape[:2]
    odd = lax.rem(lax.axis_index("gy"), 2)
    ends = (sy - 1, 0)
    sides = (0, sx - 1)

    def adj_at(i, where):
        return adjf_ref.at[(i, *where)] if i < NF else adjg_ref.at[(i - NF, *where)]

    rows = []
    for n, y in enumerate(ends):
        rows += [
            pltpu.make_async_copy(
                flow_ref.at[:, :, y], rows_v.at[n, pl.ds(0, NF)], rows_sem.at[n, 0]
            ),
            pltpu.make_async_copy(
                field_ref.at[:, :, y], rows_v.at[n, pl.ds(NF, NG)], rows_sem.at[n, 1]
            ),
        ]
    cells = [
        pltpu.make_async_copy(a, b, cell_sem.at[n])
        for n, (a, b) in enumerate(
            (
                (wall_ref, wall_v),
                (magnet_ref, magnet_v),
                (strengths_ref, strengths_v),
                (profile_ref, profile_v),
            )
        )
    ]
    faces = []
    for n, x in enumerate(sides):
        faces += [
            pltpu.make_async_copy(
                flow_ref.at[:, x], faces_v.at[n, pl.ds(0, NF)], faces_sem.at[n, 0]
            ),
            pltpu.make_async_copy(
                field_ref.at[:, x], faces_v.at[n, pl.ds(NF, NG)], faces_sem.at[n, 1]
            ),
        ]
    adjs = []
    for s in range(6):
        for n, (i, where, out) in enumerate(
            (
                (DOWN[s], (slice(None), ends[0]), message_v.at[0]),
                (UP[s], (slice(None), ends[1]), message_v.at[1]),
                (RIGHT[s], (sides[0],), left_ref),
                (LEFT[s], (sides[1],), right_ref),
            )
        ):
            adjs.append(pltpu.make_async_copy(adj_at(i, where), out.at[6 + s], adj_sem.at[n, s]))
    start_all(rows[:2])
    start_all(cells)
    start_all(rows[2:])
    start_all(faces)
    start_all(adjs)
    wait_all(cells)
    table = lane_table(strengths_v)
    for n, (y, wanted) in enumerate(zip(ends, (UP, DOWN))):
        wait_all(rows[2 * n : 2 * n + 2])
        fluid = 1.0 - wall_v[:, y, :].astype(jnp.float32)
        bcell = gather_strength(table, magnet_v[:, y, :]) * profile_v[:, y, :]
        post = collide(
            [rows_v[n, i] for i in range(NF)],
            [rows_v[n, NF + k] for k in range(NG)],
            fluid,
            bcell,
            wanted,
        )
        for s in range(6):
            message_v[n, s] = post[wanted[s]]
        message_v[n, MASK] = fluid
    for n, (x, wanted, out) in enumerate(
        ((sides[0], LEFT, left_ref), (sides[1], RIGHT, right_ref))
    ):
        wait_all(faces[2 * n : 2 * n + 2])
        fluid = 1.0 - wall_v[x].astype(jnp.float32)
        bcell = gather_strength(table, magnet_v[x]) * profile_v[x]
        post = collide(
            [faces_v[n, i] for i in range(NF)],
            [faces_v[n, NF + k] for k in range(NG)],
            fluid,
            bcell,
            wanted,
        )
        for s in range(6):
            out[s] = post[wanted[s]]
        out[MASK] = fluid
    wait_all(adjs)
    first_ref[...] = message_v[odd]
    second_ref[...] = message_v[1 - odd]


ANY = pl.BlockSpec(memory_space=pl.ANY)
VMEM = pl.BlockSpec(memory_space=pltpu.VMEM)


def rim_call(flow, field, adjf, adjg, profile, strengths, wall, magnet):
    sx, sy, sz = profile.shape
    cells = pltpu.VMEM((sx, sy, sz), jnp.float32)
    names = pltpu.VMEM((sx, sy, sz), jnp.int32)
    rows = pltpu.VMEM((SLOTS, sx, sz), jnp.float32)
    faces = pltpu.VMEM((SLOTS, sy, sz), jnp.float32)
    dma = pltpu.SemaphoreType.DMA
    return pl.pallas_call(
        rim_kernel,
        in_specs=[ANY] * 8,
        out_specs=[VMEM] * 4,
        out_shape=[rows, rows, faces, faces],
        scratch_shapes=[
            pltpu.VMEM((2, NP, sx, sz), jnp.float32),
            pltpu.VMEM((2, NP, sy, sz), jnp.float32),
            cells,
            names,
            names,
            pltpu.VMEM(strengths.shape, jnp.float32),
            pltpu.VMEM((2, SLOTS, sx, sz), jnp.float32),
            dma((4,)),
            dma((2, 2)),
            dma((2, 2)),
            dma((4, 6)),
        ],
        compiler_params=pltpu.CompilerParams(vmem_limit_bytes=RIM_VMEM),
        name="rims",
    )(flow, field, adjf, adjg, profile, strengths, wall, magnet)


def collide_kernel(
    flow_ref, field_ref, profile_ref, strengths_ref, wall_ref, magnet_ref,
    post_ref, fluid_ref, bcell_ref,
):
    table = lane_table(strengths_ref)

    def body(x, carry):
        fluid = 1.0 - wall_ref[x].astype(jnp.float32)
        bcell = gather_strength(table, magnet_ref[x]) * profile_ref[x]
        fluid_ref[x] = fluid
        bcell_ref[x] = bcell
        f = [flow_ref[i, x] for i in range(NF)]
        g = [field_ref[k, x] for k in range(NG)]
        for i, value in collide(f, g, fluid, bcell, range(NP)).items():
            post_ref[i, x] = value
        return carry

    lax.fori_loop(0, fluid_ref.shape[0], body, 0)


def collide_call(flow, field, profile, strengths, wall, magnet):
    sx, sy, sz = profile.shape
    full = pltpu.VMEM((NP, sx, sy, sz), jnp.float32)
    cells = pltpu.VMEM((sx, sy, sz), jnp.float32)
    return pl.pallas_call(
        collide_kernel,
        in_specs=[VMEM] * 6,
        out_specs=[VMEM] * 3,
        out_shape=[full, cells, cells],
        compiler_params=pltpu.CompilerParams(vmem_limit_bytes=COLLIDE_VMEM),
        cost_estimate=pl.CostEstimate(
            flops=300 * sx * sy * sz, bytes_accessed=12 * NP * sx * sy * sz, transcendentals=0
        ),
        name="collide",
    )(flow, field, profile, strengths, wall, magnet)


CORNER_RIGHT = ((0, 7, 0, 8), (1, 9, 1, 10))
CORNER_LEFT = ((0, 10, 0, 9), (1, 8, 1, 7))


def corner_slots(side, post, adj):
    posts, adjs = (UP, DOWN) if side == 0 else (DOWN, UP)
    return posts.index(post), 6 + adjs.index(adj), MASK


def corner_kernel(first_ref, second_ref, after_ref, right_ref, left_ref):
    del after_ref
    odd = lax.rem(lax.axis_index("gy"), 2) == 1
    sx = first_ref.shape[1]

    def row(side, slot, x):
        a, b = first_ref[slot, x : x + 1, :], second_ref[slot, x : x + 1, :]
        return jnp.where(odd, a, b) if side == 0 else jnp.where(odd, b, a)

    for out, table, x in ((right_ref, CORNER_RIGHT, sx - 1), (left_ref, CORNER_LEFT, 0)):
        out[...] = jnp.zeros_like(out)
        for side, post, _, adj in table:
            for n, slot in enumerate(corner_slots(side, post, adj)):
                out[2 * n + side : 2 * n + side + 1, :] = row(side, slot, x)


def corner_call(first, second, after):
    sz = first.shape[2]
    out = pltpu.VMEM((8, sz), jnp.float32)
    return pl.pallas_call(
        corner_kernel,
        in_specs=[VMEM, VMEM, ANY],
        out_specs=[VMEM, VMEM],
        out_shape=[out, out],
        compiler_params=pltpu.CompilerParams(vmem_limit_bytes=2 << 20),
        name="corners",
    )(first, second, after)


def plane_step(
    x_index, post, post_row, adj, adj_row, mask, mask_row, fluid, bcell, profile, magnet,
    near_ref, new_ref, out_ref, sums_ref, count,
):
    sy, sz = fluid.shape
    yi = lax.broadcasted_iota(jnp.int32, (sy, sz), 0)
    zi = lax.broadcasted_iota(jnp.int32, (sy, sz), 1)
    top, bottom = yi == sy - 1, yi == 0
    zlast, zfirst = zi == sz - 1, zi == 0

    def shift(value, row, dy, dz):
        if dy == -1:
            value = jnp.where(bottom, row(), pltpu.roll(value, 1, 0))
        elif dy == 1:
            value = jnp.where(top, row(), pltpu.roll(value, sy - 1, 0))
        if dz == -1:
            value = pltpu.roll(value, 1, 1)
        elif dz == 1:
            value = pltpu.roll(value, sz - 1, 1)
        return value

    def moved(get, get_row, i, sign):
        dx, dy, dz = (sign * c for c in LATTICE[i if i < NF else i - NF])
        return shift(get(i, dx), lambda: get_row(i, dx, dy), dy, dz)

    def near_of(i, sign):
        dx, dy, dz = (sign * c for c in LATTICE[i])
        value = shift(mask(dx), lambda: mask_row(dx, dy), dy, dz)
        if dz == -1:
            value = jnp.where(zfirst, 0.0, value)
        elif dz == 1:
            value = jnp.where(zlast, 0.0, value)
        return value

    for n, i in enumerate(FIRST):
        near_ref[2 * n] = near_of(i, -1)
        near_ref[2 * n + 1] = near_of(i, 1)

    def near(n):
        return near_ref[2 * n] > 0.5, near_ref[2 * n + 1] > 0.5

    def pull(i, n):
        minus, plus = near(n)
        a = fluid * jnp.where(minus, moved(post, post_row, i, -1), post(i + 1, 0))
        b = fluid * jnp.where(plus, moved(post, post_row, i + 1, -1), post(i, 0))
        new_ref[i, x_index] = a
        new_ref[i + 1, x_index] = b
        return a, b

    f0 = fluid * post(0, 0)
    new_ref[0, x_index] = f0
    rho = f0 + (1.0 - fluid)
    momx = momy = momz = shear0 = 0.0
    for n, i in enumerate(FIRST):
        a, b = pull(i, n)
        s, d = a + b, a - b
        rho = rho + s
        cx, cy, cz = LATTICE[i]
        if cx:
            momx = momx + d
        if cy:
            momy = momy + d if cy > 0 else momy - d
        if cz:
            momz = momz + d if cz > 0 else momz - d
        if cx and cy:
            shear0 = shear0 + s if cx * cy > 0 else shear0 - s
    g0 = fluid * post(NF, 0)
    new_ref[NF, x_index] = g0
    bval = g0
    gy = None
    for n, k in enumerate((1, 3, 5)):
        a, b = pull(NF + k, n)
        bval = bval + (a + b)
        if k == 3:
            gy = a - b
    inv = 1.0 / rho
    ux, uy, uz = momx * inv, momy * inv, momz * inv
    current = gy - bval * uy
    shear = shear0 - momx * uy
    force = (COUPLE * bcell) * current
    vx = ux + TAU_PLUS * force * inv

    def push(i, n):
        minus, plus = near(n)
        a = fluid * jnp.where(plus, moved(adj, adj_row, i, 1), adj(i + 1, 0))
        b = fluid * jnp.where(minus, moved(adj, adj_row, i + 1, 1), adj(i, 0))
        return a, b

    l0 = fluid * adj(0, 0)
    out_ref[0, x_index] = (1.0 - 2.0 * PLUS) * l0
    total = (2.0 * PLUS * W0) * l0
    m1 = [0.0, 0.0, 0.0]
    m2 = {}
    for n, i in enumerate(FIRST):
        a, b = push(i, n)
        s, d = a + b, a - b
        de = (0.5 - PLUS) * s
        do = (0.5 - MINUS) * d
        out_ref[i, x_index] = de + do
        out_ref[i + 1, x_index] = de - do
        w = weight(i)
        s = (2.0 * PLUS * w) * s
        d = (2.0 * MINUS * w) * d
        total = total + s
        c = LATTICE[i]
        for axis in range(3):
            if c[axis]:
                m1[axis] = m1[axis] + d if c[axis] > 0 else m1[axis] - d
            for other in range(axis, 3):
                sign = c[axis] * c[other]
                if sign:
                    old = m2.get((axis, other))
                    if old is None:
                        m2[axis, other] = s if sign > 0 else -s
                    else:
                        m2[axis, other] = old + s if sign > 0 else old - s
    h0 = fluid * adj(NF, 0)
    hsum = V0 * h0
    h1 = []
    hs = None
    for n, k in enumerate((1, 3, 5)):
        a, b = push(NF + k, n)
        hs = a + b if hs is None else hs + (a + b)
        h1.append(V1 * (a - b))
    hsum = hsum + V1 * hs

    base = 1.0 - 1.5 * (vx * vx + uy * uy + uz * uz)
    tx = m2[0, 0] * vx + m2[0, 1] * uy + m2[0, 2] * uz
    ty = m2[0, 1] * vx + m2[1, 1] * uy + m2[1, 2] * uz
    tz = m2[0, 2] * vx + m2[1, 2] * uy + m2[2, 2] * uz
    rhobar = (
        total * base
        + 4.5 * (vx * tx + uy * ty + uz * tz)
        + 3.0 * (m1[0] * vx + m1[1] * uy + m1[2] * uz)
    )
    total3 = 3.0 * total
    vxbar = rho * (9.0 * tx + 3.0 * m1[0] - total3 * vx)
    uybar = rho * (9.0 * ty + 3.0 * m1[1] - total3 * uy)
    uzbar = rho * (9.0 * tz + 3.0 * m1[2] - total3 * uz)
    slope = 4.0 * bval
    forcebar = (TAU_PLUS * vxbar) * inv
    rhobar = rhobar - forcebar * force * inv
    currentbar = (COUPLE * bcell) * forcebar
    shearbar = (SOURCE * bcell) * hsum
    dcell = COUPLE * current * forcebar + SOURCE * shear * hsum
    uxbar = vxbar + slope * h1[0]
    uybar = uybar + slope * h1[1] - bval * currentbar - momx * shearbar
    uzbar = uzbar + slope * h1[2]
    bbar = hsum + 4.0 * (h1[0] * ux + h1[1] * uy + h1[2] * uz) - uy * currentbar
    mxbar = uxbar * inv - uy * shearbar
    mybar = uybar * inv
    mzbar = uzbar * inv
    rhobar = rhobar - (ux * uxbar + uy * uybar + uz * uzbar) * inv

    out_ref[0, x_index] = out_ref[0, x_index] + rhobar
    for i in FIRST:
        cm = along(i, mxbar, mybar, mzbar)
        cx, cy, _ = LATTICE[i]
        common = rhobar
        if cx and cy:
            common = rhobar + shearbar if cx * cy > 0 else rhobar - shearbar
        out_ref[i, x_index] = out_ref[i, x_index] + (common + cm)
        out_ref[i + 1, x_index] = out_ref[i + 1, x_index] + (common - cm)
    for k in range(NG):
        value = bbar
        if k == 3:
            value = bbar + currentbar
        elif k == 4:
            value = bbar - currentbar
        out_ref[NF + k, x_index] = value

    share = dcell * profile
    for m in range(count):
        hit = jnp.where(magnet == m, share, 0.0)
        part = hit[:, 0:128]
        for z in range(128, sz, 128):
            part = part + hit[:, z : z + 128]
        sums_ref[m] = sums_ref[m] + part


def halo_slot(kind, i, dy):
    names = (UP, DOWN) if (dy == -1) == (kind == 0) else (DOWN, UP)
    return names[0].index(i) + 6 * kind


def face_slot(kind, i, dx):
    names = RIGHT if (dx == -1) == (kind == 0) else LEFT
    return names.index(i) + 6 * kind


def adj_plane(adjf_ref, adjg_ref, i, x):
    return adjf_ref[i, x] if i < NF else adjg_ref[i - NF, x]


def load_halo(first_ref, second_ref, halo_ref):
    odd = lax.rem(lax.axis_index("gy"), 2)
    halo_ref[1 - odd] = first_ref[...]
    halo_ref[odd] = second_ref[...]
    here = lax.axis_index("gy")
    keep_low = jnp.where(here == 0, 0.0, 1.0)
    keep_high = jnp.where(here == lax.axis_size("gy") - 1, 0.0, 1.0)
    halo_ref[0, MASK] = halo_ref[0, MASK] * keep_low
    halo_ref[1, MASK] = halo_ref[1, MASK] * keep_high
    return keep_low, keep_high


def plane_stores(n, x, new_v, out_v, newf_ref, newg_ref, outf_ref, outg_ref, sem):
    pairs = (
        (new_v.at[pl.ds(0, NF), n], newf_ref.at[:, x]),
        (new_v.at[pl.ds(NF, NG), n], newg_ref.at[:, x]),
        (out_v.at[pl.ds(0, NF), n], outf_ref.at[:, x]),
        (out_v.at[pl.ds(NF, NG), n], outg_ref.at[:, x]),
    )
    return [pltpu.make_async_copy(a, b, sem.at[k, n]) for k, (a, b) in enumerate(pairs)]


def inner_kernel(
    post_ref, adjf_ref, adjg_ref, fluid_ref, bcell_ref, first_ref, second_ref, profile_ref,
    magnet_ref,
    newf_ref, newg_ref, outf_ref, outg_ref, sums_ref,
    new_v, out_v, halo_v, near_v, store_sem,
):
    sx = fluid_ref.shape[0]
    count = sums_ref.shape[0]

    def stores(x):
        return plane_stores(
            x, x, new_v, out_v, newf_ref, newg_ref, outf_ref, outg_ref, store_sem
        )

    sums_ref[...] = jnp.zeros_like(sums_ref)
    load_halo(first_ref, second_ref, halo_v)

    def body(x, carry):
        def row_of(slot, dx, dy):
            return halo_v[0 if dy == -1 else 1, slot, pl.ds(x + dx, 1), :]

        plane_step(
            x,
            lambda i, dx: post_ref[i, x + dx],
            lambda i, dx, dy: row_of(halo_slot(0, i, dy), dx, dy),
            lambda i, dx: adj_plane(adjf_ref, adjg_ref, i, x + dx),
            lambda i, dx, dy: row_of(halo_slot(1, i, dy), dx, dy),
            lambda dx: fluid_ref[x + dx],
            lambda dx, dy: row_of(MASK, dx, dy),
            fluid_ref[x],
            bcell_ref[x],
            profile_ref[x],
            magnet_ref[x],
            near_v,
            new_v,
            out_v,
            sums_ref,
            count,
        )
        start_all(stores(x))
        return carry

    lax.fori_loop(1, sx - 1, body, 0)
    for x in range(1, sx - 1):
        wait_all(stores(x))


def inner_call(post, adjf, adjg, fluid, bcell, first, second, profile, magnet, count):
    sx, sy, sz = profile.shape
    full = pltpu.VMEM((NP, sx, sy, sz), jnp.float32)
    flow = jax.ShapeDtypeStruct((NF, sx, sy, sz), jnp.float32)
    field = jax.ShapeDtypeStruct((NG, sx, sy, sz), jnp.float32)
    return pl.pallas_call(
        inner_kernel,
        in_specs=[VMEM] * 9,
        out_specs=[ANY, ANY, ANY, ANY, VMEM],
        out_shape=[flow, field, flow, field, pltpu.VMEM((count, 8, 128), jnp.float32)],
        scratch_shapes=[
            full,
            full,
            pltpu.VMEM((2, SLOTS, sx, sz), jnp.float32),
            pltpu.VMEM((18, sy, sz), jnp.float32),
            pltpu.SemaphoreType.DMA((4, sx)),
        ],
        compiler_params=pltpu.CompilerParams(vmem_limit_bytes=INNER_VMEM),
        cost_estimate=pl.CostEstimate(
            flops=700 * sx * sy * sz, bytes_accessed=16 * NP * sx * sy * sz, transcendentals=0
        ),
        name="inner",
    )(post, adjf, adjg, fluid, bcell, first, second, profile, magnet)


def outer_kernel(
    scale, second_ref, fromleft_ref, fromright_ref, first_ref, post_ref, adjf_ref, adjg_ref,
    fluid_ref, bcell_ref,
    cornerleft_ref, cornerright_ref, profile_ref, magnet_ref,
    partial_ref, newf_in, newg_in, outf_in, outg_in,
    newf_ref, newg_ref, outf_ref, outg_ref, share_ref,
    new_v, out_v, halo_v, near_v, sums_v, store_sem,
):
    del newf_in, newg_in, outf_in, outg_in
    sx = fluid_ref.shape[0]
    count = sums_v.shape[0]
    sums_v[...] = partial_ref[...]
    keep_low, keep_high = load_halo(first_ref, second_ref, halo_v)
    stores = []
    for n, (x, away) in enumerate(((0, -1), (sx - 1, 1))):
        face_ref, corner_ref = (
            (fromleft_ref, cornerleft_ref) if away == -1 else (fromright_ref, cornerright_ref)
        )

        def get(kind, i, dx, x=x, away=away, face_ref=face_ref):
            if dx == away:
                return face_ref[face_slot(kind, i, dx)]
            if kind == 1:
                return adj_plane(adjf_ref, adjg_ref, i, x + dx)
            return post_ref[i, x + dx]

        def row(kind, i, dx, dy, x=x, away=away, corner_ref=corner_ref):
            side = 0 if dy == -1 else 1
            if dx == away:
                line = corner_ref[2 * kind + side : 2 * kind + side + 1, :]
                if kind == 2:
                    line = line * (keep_low if side == 0 else keep_high)
                return line
            slot = MASK if kind == 2 else halo_slot(kind, i, dy)
            return halo_v[side, slot, x + dx : x + dx + 1, :]

        def mask(dx, x=x, away=away, face_ref=face_ref):
            return face_ref[MASK] if dx == away else fluid_ref[x + dx]

        plane_step(
            n,
            lambda i, dx, get=get: get(0, i, dx),
            lambda i, dx, dy, row=row: row(0, i, dx, dy),
            lambda i, dx, get=get: get(1, i, dx),
            lambda i, dx, dy, row=row: row(1, i, dx, dy),
            mask,
            lambda dx, dy, row=row: row(2, 0, dx, dy),
            fluid_ref[x],
            bcell_ref[x],
            profile_ref[x],
            magnet_ref[x],
            near_v,
            new_v,
            out_v,
            sums_v,
            count,
        )
        these = plane_stores(
            n, x, new_v, out_v, newf_ref, newg_ref, outf_ref, outg_ref, store_sem
        )
        start_all(these)
        stores += these
    rows = jnp.concatenate(
        [jnp.sum(sums_v[m], axis=0, keepdims=True) for m in range(count)], axis=0
    )
    share_ref[...] = lax.dot_general(
        jnp.ones((share_ref.shape[0], 128), jnp.float32),
        rows * scale,
        (((1,), (1,)), ((), ())),
        precision=lax.Precision.HIGHEST,
        preferred_element_type=jnp.float32,
    )
    wait_all(stores)


def outer_call(
    post, adjf, adjg, fluid, bcell, first, second, fromleft, fromright, cornerleft, cornerright,
    profile, magnet, partial, newf, newg, outf, outg, scale,
):
    sx, sy, sz = profile.shape
    count = partial.shape[0]
    flow = jax.ShapeDtypeStruct(newf.shape, jnp.float32)
    field = jax.ShapeDtypeStruct(newg.shape, jnp.float32)
    return pl.pallas_call(
        functools.partial(outer_kernel, scale),
        in_specs=[VMEM] * 14 + [ANY] * 4,
        out_specs=[ANY] * 4 + [VMEM],
        out_shape=[
            flow,
            field,
            flow,
            field,
            jax.ShapeDtypeStruct((lax.axis_size(("gx", "gy")), count), jnp.float32),
        ],
        input_output_aliases={14: 0, 15: 1, 16: 2, 17: 3},
        scratch_shapes=[
            pltpu.VMEM((NP, 2, sy, sz), jnp.float32),
            pltpu.VMEM((NP, 2, sy, sz), jnp.float32),
            pltpu.VMEM((2, SLOTS, sx, sz), jnp.float32),
            pltpu.VMEM((18, sy, sz), jnp.float32),
            pltpu.VMEM((count, 8, 128), jnp.float32),
            pltpu.SemaphoreType.DMA((4, 2)),
        ],
        compiler_params=pltpu.CompilerParams(vmem_limit_bytes=OUTER_VMEM),
        name="outer",
    )(
        second, fromleft, fromright, first, post, adjf, adjg, fluid, bcell, cornerleft,
        cornerright, profile, magnet, partial, newf, newg, outf, outg,
    )


def ring(count, step):
    return [(i, (i + step) % count) for i in range(count)]


def on_device(flow, field, adj_flow_in, adj_field_in, profile, strengths, wall, magnet):
    across, around = lax.axis_size("gy"), lax.axis_size("gx")
    count = strengths.shape[0]
    table = strengths.reshape(1, count)
    arrays = (flow, field, adj_flow_in, adj_field_in, profile, table, wall, magnet)
    mine1, mine2, right, left = rim_call(*arrays)
    inside = [(i, i ^ 1) for i in range(across)]
    between = [(i, (((i + 1) ^ 1) - 1) % across) for i in range(across)]
    second = lax.ppermute(mine2, "gy", between)
    first = lax.ppermute(mine1, "gy", inside)
    fromleft = lax.ppermute(right, "gx", ring(around, 1))
    fromright = lax.ppermute(left, "gx", ring(around, -1))
    post, fluid, bcell = collide_call(flow, field, profile, table, wall, magnet)
    corner_r, corner_l = corner_call(first, second, bcell)
    cornerleft = lax.ppermute(corner_r, "gx", ring(around, 1))
    cornerright = lax.ppermute(corner_l, "gx", ring(around, -1))
    newf, newg, outf, outg, partial = inner_call(
        post, adj_flow_in, adj_field_in, fluid, bcell, first, second, profile, magnet, count
    )
    cells = flow.shape[1] * around * flow.shape[2] * across * flow.shape[3]
    newf, newg, outf, outg, share = outer_call(
        post, adj_flow_in, adj_field_in, fluid, bcell, first, second, fromleft, fromright, cornerleft, cornerright,
        profile, magnet, partial, newf, newg, outf, outg, 1.0 / math.sqrt(cells / count),
    )
    totals = jnp.sum(lax.all_to_all(share, ("gx", "gy"), 0, 0, tiled=True), axis=0)
    return (newf, newg, outf, outg, totals)


def solution(mesh):
    stack = P(None, "gx", "gy", None)
    cell = P("gx", "gy", None)
    return jax.shard_map(
        on_device,
        mesh=mesh,
        in_specs=(stack, stack, stack, stack, cell, P(), cell, cell),
        out_specs=(stack, stack, stack, stack, P()),
        check_vma=False,
    )
```

```python
import functools
import math

import jax
import jax.numpy as jnp
from jax import lax
from jax.experimental import pallas as pl
from jax.experimental.pallas import tpu as pltpu
from jax.sharding import PartitionSpec as P

LATTICE = [
    (0, 0, 0),
    (1, 0, 0),
    (-1, 0, 0),
    (0, 1, 0),
    (0, -1, 0),
    (0, 0, 1),
    (0, 0, -1),
    (1, 1, 0),
    (-1, -1, 0),
    (1, -1, 0),
    (-1, 1, 0),
    (1, 0, 1),
    (-1, 0, -1),
    (1, 0, -1),
    (-1, 0, 1),
    (0, 1, 1),
    (0, -1, -1),
    (0, 1, -1),
    (0, -1, 1),
]
NF, NG = 19, 7
NP = NF + NG
FIRST = [1, 3, 5, 7, 9, 11, 13, 15, 17]
W0, W1, W2 = 1.0 / 3.0, 1.0 / 18.0, 1.0 / 36.0
V0, V1 = 0.25, 0.125
PLUS = 0.625
MINUS = 0.5 / 1.125
TAU_PLUS = 0.8
COUPLE = 2.0
SOURCE = 2.0

UP = [3, 7, 10, 15, 17, NF + 3]
DOWN = [4, 8, 9, 16, 18, NF + 4]
RIGHT = [1, 7, 9, 11, 13, NF + 1]
LEFT = [2, 8, 10, 12, 14, NF + 2]
SLOTS = 13
MASK = 12

RIM_VMEM = 58 << 20
COLLIDE_VMEM = 4 << 20
INNER_VMEM = 12 << 20
OUTER_VMEM = 8 << 20


def weight(i):
    return W1 if i <= 6 else W2


def gather_strength(table, magnet):
    parts = [
        jnp.take_along_axis(table, magnet[:, z : z + 128], axis=1, mode="promise_in_bounds")
        for z in range(0, magnet.shape[1], 128)
    ]
    return jnp.concatenate(parts, axis=1)


def lane_table(strengths_ref):
    row = strengths_ref[...]
    rest = 128 - row.shape[1]
    if rest:
        row = jnp.concatenate([row, jnp.zeros((1, rest), jnp.float32)], axis=1)
    return jnp.broadcast_to(row, (8, 128))


def vector_sums(pair):
    x = pair[1] + pair[7] + pair[9] + pair[11] + pair[13]
    y = pair[3] + pair[7] - pair[9] + pair[15] + pair[17]
    z = pair[5] + pair[11] - pair[13] + pair[15] - pair[17]
    return x, y, z


def along(i, vx, vy, vz):
    out = None
    for c, v in zip(LATTICE[i], (vx, vy, vz)):
        if c:
            if out is None:
                out = v if c > 0 else -v
            else:
                out = out + v if c > 0 else out - v
    return out


def start_all(copies):
    for c in copies:
        c.start()


def wait_all(copies):
    for c in copies:
        c.wait()


def collide(f, g, fluid, bcell, wanted):
    even = {i: f[i] + f[i + 1] for i in FIRST}
    diff = {i: f[i] - f[i + 1] for i in FIRST}
    rho = f[0] + (1.0 - fluid)
    for i in FIRST:
        rho = rho + even[i]
    momx, momy, momz = vector_sums(diff)
    inv = 1.0 / rho
    ux, uy, uz = momx * inv, momy * inv, momz * inv
    bval = g[0] + g[1] + g[2] + g[3] + g[4] + g[5] + g[6]
    current = (g[3] - g[4]) - bval * uy
    shear = (even[7] - even[9]) - momx * uy
    force = (COUPLE * bcell) * current
    vx = ux + TAU_PLUS * force * inv
    base = 1.0 - 1.5 * (vx * vx + uy * uy + uz * uz)
    post = {}
    if 0 in wanted:
        post[0] = f[0] - 2.0 * PLUS * (f[0] - (W0 * rho) * base)
    rho1, rho2 = W1 * rho, W2 * rho
    for i in FIRST:
        if i not in wanted and i + 1 not in wanted:
            continue
        wr = rho1 if i <= 6 else rho2
        a = along(i, vx, uy, uz)
        ne = PLUS * (even[i] - (2.0 * wr) * (base + 4.5 * a * a))
        no = MINUS * (diff[i] - (6.0 * wr) * a)
        if i in wanted:
            post[i] = f[i] - ne - no
        if i + 1 in wanted:
            post[i + 1] = f[i + 1] - ne + no
    common = bval + (SOURCE * bcell) * shear
    slope = 4.0 * bval
    if NF in wanted:
        post[NF] = V0 * common
    for k, u in ((1, ux), (3, uy), (5, uz)):
        if NF + k in wanted:
            post[NF + k] = V1 * (common + slope * u)
        if NF + k + 1 in wanted:
            post[NF + k + 1] = V1 * (common - slope * u)
    return post


def rim_kernel(
    flow_ref, field_ref, adjf_ref, adjg_ref, profile_ref, strengths_ref, wall_ref, magnet_ref,
    first_ref, second_ref, right_ref, left_ref,
    rows_v, faces_v, profile_v, wall_v, magnet_v, strengths_v, message_v, cell_sem, rows_sem,
    faces_sem, adj_sem,
):
    sx, sy = profile_v.shape[:2]
    odd = lax.rem(lax.axis_index("gy"), 2)
    ends = (sy - 1, 0)
    sides = (0, sx - 1)

    def adj_at(i, where):
        return adjf_ref.at[(i, *where)] if i < NF else adjg_ref.at[(i - NF, *where)]

    rows = []
    for n, y in enumerate(ends):
        rows += [
            pltpu.make_async_copy(
                flow_ref.at[:, :, y], rows_v.at[n, pl.ds(0, NF)], rows_sem.at[n, 0]
            ),
            pltpu.make_async_copy(
                field_ref.at[:, :, y], rows_v.at[n, pl.ds(NF, NG)], rows_sem.at[n, 1]
            ),
        ]
    cells = [
        pltpu.make_async_copy(a, b, cell_sem.at[n])
        for n, (a, b) in enumerate(
            (
                (wall_ref, wall_v),
                (magnet_ref, magnet_v),
                (strengths_ref, strengths_v),
                (profile_ref, profile_v),
            )
        )
    ]
    faces = []
    for n, x in enumerate(sides):
        faces += [
            pltpu.make_async_copy(
                flow_ref.at[:, x], faces_v.at[n, pl.ds(0, NF)], faces_sem.at[n, 0]
            ),
            pltpu.make_async_copy(
                field_ref.at[:, x], faces_v.at[n, pl.ds(NF, NG)], faces_sem.at[n, 1]
            ),
        ]
    adjs = []
    for s in range(6):
        for n, (i, where, out) in enumerate(
            (
                (DOWN[s], (slice(None), ends[0]), message_v.at[0]),
                (UP[s], (slice(None), ends[1]), message_v.at[1]),
                (RIGHT[s], (sides[0],), left_ref),
                (LEFT[s], (sides[1],), right_ref),
            )
        ):
            adjs.append(pltpu.make_async_copy(adj_at(i, where), out.at[6 + s], adj_sem.at[n, s]))
    start_all(rows[:2])
    start_all(cells)
    start_all(rows[2:])
    start_all(faces)
    start_all(adjs)
    wait_all(cells)
    table = lane_table(strengths_v)
    for n, (y, wanted) in enumerate(zip(ends, (UP, DOWN))):
        wait_all(rows[2 * n : 2 * n + 2])
        fluid = 1.0 - wall_v[:, y, :].astype(jnp.float32)
        bcell = gather_strength(table, magnet_v[:, y, :]) * profile_v[:, y, :]
        post = collide(
            [rows_v[n, i] for i in range(NF)],
            [rows_v[n, NF + k] for k in range(NG)],
            fluid,
            bcell,
            wanted,
        )
        for s in range(6):
            message_v[n, s] = post[wanted[s]]
        message_v[n, MASK] = fluid
    for n, (x, wanted, out) in enumerate(
        ((sides[0], LEFT, left_ref), (sides[1], RIGHT, right_ref))
    ):
        wait_all(faces[2 * n : 2 * n + 2])
        fluid = 1.0 - wall_v[x].astype(jnp.float32)
        bcell = gather_strength(table, magnet_v[x]) * profile_v[x]
        post = collide(
            [faces_v[n, i] for i in range(NF)],
            [faces_v[n, NF + k] for k in range(NG)],
            fluid,
            bcell,
            wanted,
        )
        for s in range(6):
            out[s] = post[wanted[s]]
        out[MASK] = fluid
    wait_all(adjs)
    first_ref[...] = message_v[odd]
    second_ref[...] = message_v[1 - odd]


ANY = pl.BlockSpec(memory_space=pl.ANY)
VMEM = pl.BlockSpec(memory_space=pltpu.VMEM)


def rim_call(flow, field, adjf, adjg, profile, strengths, wall, magnet):
    sx, sy, sz = profile.shape
    cells = pltpu.VMEM((sx, sy, sz), jnp.float32)
    names = pltpu.VMEM((sx, sy, sz), jnp.int32)
    rows = pltpu.VMEM((SLOTS, sx, sz), jnp.float32)
    faces = pltpu.VMEM((SLOTS, sy, sz), jnp.float32)
    dma = pltpu.SemaphoreType.DMA
    return pl.pallas_call(
        rim_kernel,
        in_specs=[ANY] * 8,
        out_specs=[VMEM] * 4,
        out_shape=[rows, rows, faces, faces],
        scratch_shapes=[
            pltpu.VMEM((2, NP, sx, sz), jnp.float32),
            pltpu.VMEM((2, NP, sy, sz), jnp.float32),
            cells,
            names,
            names,
            pltpu.VMEM(strengths.shape, jnp.float32),
            pltpu.VMEM((2, SLOTS, sx, sz), jnp.float32),
            dma((4,)),
            dma((2, 2)),
            dma((2, 2)),
            dma((4, 6)),
        ],
        compiler_params=pltpu.CompilerParams(vmem_limit_bytes=RIM_VMEM),
        name="rims",
    )(flow, field, adjf, adjg, profile, strengths, wall, magnet)


def collide_kernel(
    flow_ref, field_ref, profile_ref, strengths_ref, wall_ref, magnet_ref,
    post_ref, fluid_ref, bcell_ref,
):
    table = lane_table(strengths_ref)

    def body(x, carry):
        fluid = 1.0 - wall_ref[x].astype(jnp.float32)
        bcell = gather_strength(table, magnet_ref[x]) * profile_ref[x]
        fluid_ref[x] = fluid
        bcell_ref[x] = bcell
        f = [flow_ref[i, x] for i in range(NF)]
        g = [field_ref[k, x] for k in range(NG)]
        for i, value in collide(f, g, fluid, bcell, range(NP)).items():
            post_ref[i, x] = value
        return carry

    lax.fori_loop(0, fluid_ref.shape[0], body, 0)


def collide_call(flow, field, profile, strengths, wall, magnet):
    sx, sy, sz = profile.shape
    full = pltpu.VMEM((NP, sx, sy, sz), jnp.float32)
    cells = pltpu.VMEM((sx, sy, sz), jnp.float32)
    return pl.pallas_call(
        collide_kernel,
        in_specs=[VMEM] * 6,
        out_specs=[VMEM] * 3,
        out_shape=[full, cells, cells],
        compiler_params=pltpu.CompilerParams(vmem_limit_bytes=COLLIDE_VMEM),
        cost_estimate=pl.CostEstimate(
            flops=300 * sx * sy * sz, bytes_accessed=12 * NP * sx * sy * sz, transcendentals=0
        ),
        name="collide",
    )(flow, field, profile, strengths, wall, magnet)


CORNER_RIGHT = ((0, 7, 0, 8), (1, 9, 1, 10))
CORNER_LEFT = ((0, 10, 0, 9), (1, 8, 1, 7))


def corner_slots(side, post, adj):
    posts, adjs = (UP, DOWN) if side == 0 else (DOWN, UP)
    return posts.index(post), 6 + adjs.index(adj), MASK


def corner_kernel(table, x, first_ref, second_ref, after_ref, out_ref):
    del after_ref
    odd = lax.rem(lax.axis_index("gy"), 2) == 1

    def row(side, slot):
        a, b = first_ref[slot, x : x + 1, :], second_ref[slot, x : x + 1, :]
        return jnp.where(odd, a, b) if side == 0 else jnp.where(odd, b, a)

    out_ref[...] = jnp.zeros_like(out_ref)
    for side, post, _, adj in table:
        for n, slot in enumerate(corner_slots(side, post, adj)):
            out_ref[2 * n + side : 2 * n + side + 1, :] = row(side, slot)


def corner_call(table, x, first, second, after):
    return pl.pallas_call(
        functools.partial(corner_kernel, table, x),
        in_specs=[VMEM, VMEM, ANY],
        out_specs=VMEM,
        out_shape=pltpu.VMEM((8, first.shape[2]), jnp.float32),
        compiler_params=pltpu.CompilerParams(vmem_limit_bytes=2 << 20),
        name="corners",
    )(first, second, after)


def plane_step(
    x_index, post, post_row, adj, adj_row, mask, mask_row, fluid, bcell, profile, magnet,
    near_ref, new_ref, out_ref, sums_ref, count,
):
    sy, sz = fluid.shape
    yi = lax.broadcasted_iota(jnp.int32, (sy, sz), 0)
    zi = lax.broadcasted_iota(jnp.int32, (sy, sz), 1)
    top, bottom = yi == sy - 1, yi == 0
    zlast, zfirst = zi == sz - 1, zi == 0

    def shift(value, row, dy, dz):
        if dy == -1:
            value = jnp.where(bottom, row(), pltpu.roll(value, 1, 0))
        elif dy == 1:
            value = jnp.where(top, row(), pltpu.roll(value, sy - 1, 0))
        if dz == -1:
            value = pltpu.roll(value, 1, 1)
        elif dz == 1:
            value = pltpu.roll(value, sz - 1, 1)
        return value

    def moved(get, get_row, i, sign):
        dx, dy, dz = (sign * c for c in LATTICE[i if i < NF else i - NF])
        return shift(get(i, dx), lambda: get_row(i, dx, dy), dy, dz)

    def near_of(i, sign):
        dx, dy, dz = (sign * c for c in LATTICE[i])
        value = shift(mask(dx), lambda: mask_row(dx, dy), dy, dz)
        if dz == -1:
            value = jnp.where(zfirst, 0.0, value)
        elif dz == 1:
            value = jnp.where(zlast, 0.0, value)
        return value

    for n, i in enumerate(FIRST):
        near_ref[2 * n] = near_of(i, -1)
        near_ref[2 * n + 1] = near_of(i, 1)

    def near(n):
        return near_ref[2 * n] > 0.5, near_ref[2 * n + 1] > 0.5

    def pull(i, n):
        minus, plus = near(n)
        a = fluid * jnp.where(minus, moved(post, post_row, i, -1), post(i + 1, 0))
        b = fluid * jnp.where(plus, moved(post, post_row, i + 1, -1), post(i, 0))
        new_ref[i, x_index] = a
        new_ref[i + 1, x_index] = b
        return a, b

    f0 = fluid * post(0, 0)
    new_ref[0, x_index] = f0
    rho = f0 + (1.0 - fluid)
    momx = momy = momz = shear0 = 0.0
    for n, i in enumerate(FIRST):
        a, b = pull(i, n)
        s, d = a + b, a - b
        rho = rho + s
        cx, cy, cz = LATTICE[i]
        if cx:
            momx = momx + d
        if cy:
            momy = momy + d if cy > 0 else momy - d
        if cz:
            momz = momz + d if cz > 0 else momz - d
        if cx and cy:
            shear0 = shear0 + s if cx * cy > 0 else shear0 - s
    g0 = fluid * post(NF, 0)
    new_ref[NF, x_index] = g0
    bval = g0
    gy = None
    for n, k in enumerate((1, 3, 5)):
        a, b = pull(NF + k, n)
        bval = bval + (a + b)
        if k == 3:
            gy = a - b
    inv = 1.0 / rho
    ux, uy, uz = momx * inv, momy * inv, momz * inv
    current = gy - bval * uy
    shear = shear0 - momx * uy
    force = (COUPLE * bcell) * current
    vx = ux + TAU_PLUS * force * inv

    def push(i, n):
        minus, plus = near(n)
        a = fluid * jnp.where(plus, moved(adj, adj_row, i, 1), adj(i + 1, 0))
        b = fluid * jnp.where(minus, moved(adj, adj_row, i + 1, 1), adj(i, 0))
        return a, b

    l0 = fluid * adj(0, 0)
    out_ref[0, x_index] = (1.0 - 2.0 * PLUS) * l0
    total = (2.0 * PLUS * W0) * l0
    m1 = [0.0, 0.0, 0.0]
    m2 = {}
    for n, i in enumerate(FIRST):
        a, b = push(i, n)
        s, d = a + b, a - b
        de = (0.5 - PLUS) * s
        do = (0.5 - MINUS) * d
        out_ref[i, x_index] = de + do
        out_ref[i + 1, x_index] = de - do
        w = weight(i)
        s = (2.0 * PLUS * w) * s
        d = (2.0 * MINUS * w) * d
        total = total + s
        c = LATTICE[i]
        for axis in range(3):
            if c[axis]:
                m1[axis] = m1[axis] + d if c[axis] > 0 else m1[axis] - d
            for other in range(axis, 3):
                sign = c[axis] * c[other]
                if sign:
                    old = m2.get((axis, other))
                    if old is None:
                        m2[axis, other] = s if sign > 0 else -s
                    else:
                        m2[axis, other] = old + s if sign > 0 else old - s
    h0 = fluid * adj(NF, 0)
    hsum = V0 * h0
    h1 = []
    hs = None
    for n, k in enumerate((1, 3, 5)):
        a, b = push(NF + k, n)
        hs = a + b if hs is None else hs + (a + b)
        h1.append(V1 * (a - b))
    hsum = hsum + V1 * hs

    base = 1.0 - 1.5 * (vx * vx + uy * uy + uz * uz)
    tx = m2[0, 0] * vx + m2[0, 1] * uy + m2[0, 2] * uz
    ty = m2[0, 1] * vx + m2[1, 1] * uy + m2[1, 2] * uz
    tz = m2[0, 2] * vx + m2[1, 2] * uy + m2[2, 2] * uz
    rhobar = (
        total * base
        + 4.5 * (vx * tx + uy * ty + uz * tz)
        + 3.0 * (m1[0] * vx + m1[1] * uy + m1[2] * uz)
    )
    total3 = 3.0 * total
    vxbar = rho * (9.0 * tx + 3.0 * m1[0] - total3 * vx)
    uybar = rho * (9.0 * ty + 3.0 * m1[1] - total3 * uy)
    uzbar = rho * (9.0 * tz + 3.0 * m1[2] - total3 * uz)
    slope = 4.0 * bval
    forcebar = (TAU_PLUS * vxbar) * inv
    rhobar = rhobar - forcebar * force * inv
    currentbar = (COUPLE * bcell) * forcebar
    shearbar = (SOURCE * bcell) * hsum
    dcell = COUPLE * current * forcebar + SOURCE * shear * hsum
    uxbar = vxbar + slope * h1[0]
    uybar = uybar + slope * h1[1] - bval * currentbar - momx * shearbar
    uzbar = uzbar + slope * h1[2]
    bbar = hsum + 4.0 * (h1[0] * ux + h1[1] * uy + h1[2] * uz) - uy * currentbar
    mxbar = uxbar * inv - uy * shearbar
    mybar = uybar * inv
    mzbar = uzbar * inv
    rhobar = rhobar - (ux * uxbar + uy * uybar + uz * uzbar) * inv

    out_ref[0, x_index] = out_ref[0, x_index] + rhobar
    for i in FIRST:
        cm = along(i, mxbar, mybar, mzbar)
        cx, cy, _ = LATTICE[i]
        common = rhobar
        if cx and cy:
            common = rhobar + shearbar if cx * cy > 0 else rhobar - shearbar
        out_ref[i, x_index] = out_ref[i, x_index] + (common + cm)
        out_ref[i + 1, x_index] = out_ref[i + 1, x_index] + (common - cm)
    for k in range(NG):
        value = bbar
        if k == 3:
            value = bbar + currentbar
        elif k == 4:
            value = bbar - currentbar
        out_ref[NF + k, x_index] = value

    share = dcell * profile
    for m in range(count):
        hit = jnp.where(magnet == m, share, 0.0)
        part = hit[:, 0:128]
        for z in range(128, sz, 128):
            part = part + hit[:, z : z + 128]
        sums_ref[m] = sums_ref[m] + part


def halo_slot(kind, i, dy):
    names = (UP, DOWN) if (dy == -1) == (kind == 0) else (DOWN, UP)
    return names[0].index(i) + 6 * kind


def face_slot(kind, i, dx):
    names = RIGHT if (dx == -1) == (kind == 0) else LEFT
    return names.index(i) + 6 * kind


def adj_plane(adjf_ref, adjg_ref, i, x):
    return adjf_ref[i, x] if i < NF else adjg_ref[i - NF, x]


def load_halo(first_ref, second_ref, halo_ref):
    odd = lax.rem(lax.axis_index("gy"), 2)
    halo_ref[1 - odd] = first_ref[...]
    halo_ref[odd] = second_ref[...]
    here = lax.axis_index("gy")
    keep_low = jnp.where(here == 0, 0.0, 1.0)
    keep_high = jnp.where(here == lax.axis_size("gy") - 1, 0.0, 1.0)
    halo_ref[0, MASK] = halo_ref[0, MASK] * keep_low
    halo_ref[1, MASK] = halo_ref[1, MASK] * keep_high
    return keep_low, keep_high


def plane_stores(n, x, new_v, out_v, newf_ref, newg_ref, outf_ref, outg_ref, sem):
    pairs = (
        (new_v.at[pl.ds(0, NF), n], newf_ref.at[:, x]),
        (new_v.at[pl.ds(NF, NG), n], newg_ref.at[:, x]),
        (out_v.at[pl.ds(0, NF), n], outf_ref.at[:, x]),
        (out_v.at[pl.ds(NF, NG), n], outg_ref.at[:, x]),
    )
    return [pltpu.make_async_copy(a, b, sem.at[k, n]) for k, (a, b) in enumerate(pairs)]


def inner_planes(
    start, stop, base, done, post_ref, adjf_ref, adjg_ref, fluid_ref, bcell_ref, profile_ref,
    magnet_ref, new_v, out_v, halo_v, near_v, sums_ref,
):
    def body(x, carry):
        def row_of(slot, dx, dy):
            return halo_v[0 if dy == -1 else 1, slot, pl.ds(x + dx, 1), :]

        plane_step(
            x - base,
            lambda i, dx: post_ref[i, x + dx],
            lambda i, dx, dy: row_of(halo_slot(0, i, dy), dx, dy),
            lambda i, dx: adj_plane(adjf_ref, adjg_ref, i, x + dx),
            lambda i, dx, dy: row_of(halo_slot(1, i, dy), dx, dy),
            lambda dx: fluid_ref[x + dx],
            lambda dx, dy: row_of(MASK, dx, dy),
            fluid_ref[x],
            bcell_ref[x],
            profile_ref[x],
            magnet_ref[x],
            near_v,
            new_v,
            out_v,
            sums_ref,
            sums_ref.shape[0],
        )
        done(x)
        return carry

    lax.fori_loop(start, stop, body, 0)


def inner_kernel(
    post_ref, adjf_ref, adjg_ref, fluid_ref, bcell_ref, first_ref, second_ref, profile_ref,
    magnet_ref,
    new_ref, out_ref, sums_ref, halo_ref,
    near_v,
):
    sums_ref[...] = jnp.zeros_like(sums_ref)
    load_halo(first_ref, second_ref, halo_ref)
    inner_planes(
        1, 1 + new_ref.shape[1], 1, lambda x: None, post_ref, adjf_ref, adjg_ref, fluid_ref,
        bcell_ref, profile_ref, magnet_ref, new_ref, out_ref, halo_ref, near_v, sums_ref,
    )


def inner_call(post, adjf, adjg, fluid, bcell, first, second, profile, magnet, count):
    sx, sy, sz = profile.shape
    part = pltpu.VMEM((NP, (sx - 2) // 2, sy, sz), jnp.float32)
    return pl.pallas_call(
        inner_kernel,
        in_specs=[VMEM] * 9,
        out_specs=[VMEM] * 4,
        out_shape=[
            part,
            part,
            pltpu.VMEM((count, 8, 128), jnp.float32),
            pltpu.VMEM((2, SLOTS, sx, sz), jnp.float32),
        ],
        scratch_shapes=[pltpu.VMEM((18, sy, sz), jnp.float32)],
        compiler_params=pltpu.CompilerParams(vmem_limit_bytes=OUTER_VMEM),
        cost_estimate=pl.CostEstimate(
            flops=350 * sx * sy * sz, bytes_accessed=8 * NP * sx * sy * sz, transcendentals=0
        ),
        name="inner",
    )(post, adjf, adjg, fluid, bcell, first, second, profile, magnet)


def rest_kernel(
    post_ref, adjf_ref, adjg_ref, fluid_ref, bcell_ref, halo_ref, profile_ref, magnet_ref,
    new_ref, out_ref, partial_ref, after_ref,
    newf_ref, newg_ref, outf_ref, outg_ref, sums_ref,
    new_v, out_v, near_v, store_sem,
):
    del after_ref
    sx = fluid_ref.shape[0]
    middle = 1 + new_ref.shape[1]

    def stores(x):
        pairs = (
            (new_v.at[pl.ds(0, NF), x - middle], newf_ref.at[:, x]),
            (new_v.at[pl.ds(NF, NG), x - middle], newg_ref.at[:, x]),
            (out_v.at[pl.ds(0, NF), x - middle], outf_ref.at[:, x]),
            (out_v.at[pl.ds(NF, NG), x - middle], outg_ref.at[:, x]),
        )
        return [pltpu.make_async_copy(a, b, store_sem.at[k, x]) for k, (a, b) in enumerate(pairs)]

    early = []
    for x in range(1, middle):
        pairs = (
            (new_ref.at[pl.ds(0, NF), x - 1], newf_ref.at[:, x]),
            (new_ref.at[pl.ds(NF, NG), x - 1], newg_ref.at[:, x]),
            (out_ref.at[pl.ds(0, NF), x - 1], outf_ref.at[:, x]),
            (out_ref.at[pl.ds(NF, NG), x - 1], outg_ref.at[:, x]),
        )
        early += [pltpu.make_async_copy(a, b, store_sem.at[k, x]) for k, (a, b) in enumerate(pairs)]
    start_all(early)
    sums_ref[...] = partial_ref[...]
    inner_planes(
        middle, sx - 1, middle, lambda x: start_all(stores(x)), post_ref, adjf_ref, adjg_ref,
        fluid_ref, bcell_ref, profile_ref, magnet_ref, new_v, out_v, halo_ref, near_v, sums_ref,
    )
    wait_all(early)
    for x in range(middle, sx - 1):
        wait_all(stores(x))


def rest_call(
    post, adjf, adjg, fluid, bcell, halo, profile, magnet, new, out, partial, after
):
    sx, sy, sz = profile.shape
    part = pltpu.VMEM((NP, sx - 2 - new.shape[1], sy, sz), jnp.float32)
    flow = jax.ShapeDtypeStruct((NF, sx, sy, sz), jnp.float32)
    field = jax.ShapeDtypeStruct((NG, sx, sy, sz), jnp.float32)
    return pl.pallas_call(
        rest_kernel,
        in_specs=[VMEM] * 11 + [ANY],
        out_specs=[ANY, ANY, ANY, ANY, VMEM],
        out_shape=[flow, field, flow, field, pltpu.VMEM(partial.shape, jnp.float32)],
        scratch_shapes=[
            part,
            part,
            pltpu.VMEM((18, sy, sz), jnp.float32),
            pltpu.SemaphoreType.DMA((4, sx)),
        ],
        compiler_params=pltpu.CompilerParams(vmem_limit_bytes=OUTER_VMEM),
        cost_estimate=pl.CostEstimate(
            flops=350 * sx * sy * sz, bytes_accessed=8 * NP * sx * sy * sz, transcendentals=0
        ),
        name="rest",
    )(post, adjf, adjg, fluid, bcell, halo, profile, magnet, new, out, partial, after)


def outer_kernel(
    scale, second_ref, fromleft_ref, fromright_ref, first_ref, post_ref, adjf_ref, adjg_ref,
    fluid_ref, bcell_ref,
    cornerleft_ref, cornerright_ref, profile_ref, magnet_ref,
    partial_ref, newf_in, newg_in, outf_in, outg_in,
    newf_ref, newg_ref, outf_ref, outg_ref, share_ref,
    new_v, out_v, halo_v, near_v, sums_v, store_sem,
):
    del newf_in, newg_in, outf_in, outg_in
    sx = fluid_ref.shape[0]
    count = sums_v.shape[0]
    sums_v[...] = partial_ref[...]
    keep_low, keep_high = load_halo(first_ref, second_ref, halo_v)
    stores = []
    for n, (x, away) in enumerate(((0, -1), (sx - 1, 1))):
        face_ref, corner_ref = (
            (fromleft_ref, cornerleft_ref) if away == -1 else (fromright_ref, cornerright_ref)
        )

        def get(kind, i, dx, x=x, away=away, face_ref=face_ref):
            if dx == away:
                return face_ref[face_slot(kind, i, dx)]
            if kind == 1:
                return adj_plane(adjf_ref, adjg_ref, i, x + dx)
            return post_ref[i, x + dx]

        def row(kind, i, dx, dy, x=x, away=away, corner_ref=corner_ref):
            side = 0 if dy == -1 else 1
            if dx == away:
                line = corner_ref[2 * kind + side : 2 * kind + side + 1, :]
                if kind == 2:
                    line = line * (keep_low if side == 0 else keep_high)
                return line
            slot = MASK if kind == 2 else halo_slot(kind, i, dy)
            return halo_v[side, slot, x + dx : x + dx + 1, :]

        def mask(dx, x=x, away=away, face_ref=face_ref):
            return face_ref[MASK] if dx == away else fluid_ref[x + dx]

        plane_step(
            n,
            lambda i, dx, get=get: get(0, i, dx),
            lambda i, dx, dy, row=row: row(0, i, dx, dy),
            lambda i, dx, get=get: get(1, i, dx),
            lambda i, dx, dy, row=row: row(1, i, dx, dy),
            mask,
            lambda dx, dy, row=row: row(2, 0, dx, dy),
            fluid_ref[x],
            bcell_ref[x],
            profile_ref[x],
            magnet_ref[x],
            near_v,
            new_v,
            out_v,
            sums_v,
            count,
        )
        these = plane_stores(
            n, x, new_v, out_v, newf_ref, newg_ref, outf_ref, outg_ref, store_sem
        )
        start_all(these)
        stores += these
    rows = jnp.concatenate(
        [jnp.sum(sums_v[m], axis=0, keepdims=True) for m in range(count)], axis=0
    )
    share_ref[...] = lax.dot_general(
        jnp.ones((share_ref.shape[0], 128), jnp.float32),
        rows * scale,
        (((1,), (1,)), ((), ())),
        precision=lax.Precision.HIGHEST,
        preferred_element_type=jnp.float32,
    )
    wait_all(stores)


def outer_call(
    post, adjf, adjg, fluid, bcell, first, second, fromleft, fromright, cornerleft, cornerright,
    profile, magnet, partial, newf, newg, outf, outg, scale,
):
    sx, sy, sz = profile.shape
    count = partial.shape[0]
    flow = jax.ShapeDtypeStruct(newf.shape, jnp.float32)
    field = jax.ShapeDtypeStruct(newg.shape, jnp.float32)
    return pl.pallas_call(
        functools.partial(outer_kernel, scale),
        in_specs=[VMEM] * 14 + [ANY] * 4,
        out_specs=[ANY] * 4 + [VMEM],
        out_shape=[
            flow,
            field,
            flow,
            field,
            jax.ShapeDtypeStruct((lax.axis_size(("gx", "gy")), count), jnp.float32),
        ],
        input_output_aliases={14: 0, 15: 1, 16: 2, 17: 3},
        scratch_shapes=[
            pltpu.VMEM((NP, 2, sy, sz), jnp.float32),
            pltpu.VMEM((NP, 2, sy, sz), jnp.float32),
            pltpu.VMEM((2, SLOTS, sx, sz), jnp.float32),
            pltpu.VMEM((18, sy, sz), jnp.float32),
            pltpu.VMEM((count, 8, 128), jnp.float32),
            pltpu.SemaphoreType.DMA((4, 2)),
        ],
        compiler_params=pltpu.CompilerParams(vmem_limit_bytes=OUTER_VMEM),
        name="outer",
    )(
        second, fromleft, fromright, first, post, adjf, adjg, fluid, bcell, cornerleft,
        cornerright, profile, magnet, partial, newf, newg, outf, outg,
    )


def ring(count, step):
    return [(i, (i + step) % count) for i in range(count)]


def on_device(flow, field, adj_flow_in, adj_field_in, profile, strengths, wall, magnet):
    across, around = lax.axis_size("gy"), lax.axis_size("gx")
    count = strengths.shape[0]
    table = strengths.reshape(1, count)
    arrays = (flow, field, adj_flow_in, adj_field_in, profile, table, wall, magnet)
    mine1, mine2, right, left = rim_call(*arrays)
    inside = [(i, i ^ 1) for i in range(across)]
    between = [(i, (((i + 1) ^ 1) - 1) % across) for i in range(across)]
    second = lax.ppermute(mine2, "gy", between)
    first = lax.ppermute(mine1, "gy", inside)
    fromleft = lax.ppermute(right, "gx", ring(around, 1))
    fromright = lax.ppermute(left, "gx", ring(around, -1))
    post, fluid, bcell = collide_call(flow, field, profile, table, wall, magnet)
    corner_r = corner_call(CORNER_RIGHT, flow.shape[1] - 1, first, second, bcell)
    cornerleft = lax.ppermute(corner_r, "gx", ring(around, 1))
    new, out, partial, halo = inner_call(
        post, adj_flow_in, adj_field_in, fluid, bcell, first, second, profile, magnet, count
    )
    corner_l = corner_call(CORNER_LEFT, 0, first, second, partial)
    cornerright = lax.ppermute(corner_l, "gx", ring(around, -1))
    newf, newg, outf, outg, partial = rest_call(
        post, adj_flow_in, adj_field_in, fluid, bcell, halo, profile, magnet, new, out, partial,
        corner_l,
    )
    cells = flow.shape[1] * around * flow.shape[2] * across * flow.shape[3]
    newf, newg, outf, outg, share = outer_call(
        post, adj_flow_in, adj_field_in, fluid, bcell, first, second, fromleft, fromright, cornerleft, cornerright,
        profile, magnet, partial, newf, newg, outf, outg, 1.0 / math.sqrt(cells / count),
    )
    totals = jnp.sum(lax.all_to_all(share, ("gx", "gy"), 0, 0, tiled=True), axis=0)
    return (newf, newg, outf, outg, totals)


def solution(mesh):
    stack = P(None, "gx", "gy", None)
    cell = P("gx", "gy", None)
    return jax.shard_map(
        on_device,
        mesh=mesh,
        in_specs=(stack, stack, stack, stack, cell, P(), cell, cell),
        out_specs=(stack, stack, stack, stack, P()),
        check_vma=False,
    )
```

```python
import functools
import math

import jax
import jax.numpy as jnp
from jax import lax
from jax.experimental import pallas as pl
from jax.experimental.pallas import tpu as pltpu
from jax.sharding import PartitionSpec as P

LATTICE = [
    (0, 0, 0),
    (1, 0, 0),
    (-1, 0, 0),
    (0, 1, 0),
    (0, -1, 0),
    (0, 0, 1),
    (0, 0, -1),
    (1, 1, 0),
    (-1, -1, 0),
    (1, -1, 0),
    (-1, 1, 0),
    (1, 0, 1),
    (-1, 0, -1),
    (1, 0, -1),
    (-1, 0, 1),
    (0, 1, 1),
    (0, -1, -1),
    (0, 1, -1),
    (0, -1, 1),
]
NF, NG = 19, 7
NP = NF + NG
FIRST = [1, 3, 5, 7, 9, 11, 13, 15, 17]
W0, W1, W2 = 1.0 / 3.0, 1.0 / 18.0, 1.0 / 36.0
V0, V1 = 0.25, 0.125
PLUS = 0.625
MINUS = 0.5 / 1.125
TAU_PLUS = 0.8
COUPLE = 2.0
SOURCE = 2.0

UP = [3, 7, 10, 15, 17, NF + 3]
DOWN = [4, 8, 9, 16, 18, NF + 4]
RIGHT = [1, 7, 9, 11, 13, NF + 1]
LEFT = [2, 8, 10, 12, 14, NF + 2]
SLOTS = 13
MASK = 12

RIM_VMEM = 58 << 20
COLLIDE_VMEM = 4 << 20
INNER_VMEM = 12 << 20
OUTER_VMEM = 8 << 20


def weight(i):
    return W1 if i <= 6 else W2


def gather_strength(table, magnet):
    parts = [
        jnp.take_along_axis(table, magnet[:, z : z + 128], axis=1, mode="promise_in_bounds")
        for z in range(0, magnet.shape[1], 128)
    ]
    return jnp.concatenate(parts, axis=1)


def lane_table(strengths_ref):
    row = strengths_ref[...]
    rest = 128 - row.shape[1]
    if rest:
        row = jnp.concatenate([row, jnp.zeros((1, rest), jnp.float32)], axis=1)
    return jnp.broadcast_to(row, (8, 128))


def vector_sums(pair):
    x = pair[1] + pair[7] + pair[9] + pair[11] + pair[13]
    y = pair[3] + pair[7] - pair[9] + pair[15] + pair[17]
    z = pair[5] + pair[11] - pair[13] + pair[15] - pair[17]
    return x, y, z


def along(i, vx, vy, vz):
    out = None
    for c, v in zip(LATTICE[i], (vx, vy, vz)):
        if c:
            if out is None:
                out = v if c > 0 else -v
            else:
                out = out + v if c > 0 else out - v
    return out


def start_all(copies):
    for c in copies:
        c.start()


def wait_all(copies):
    for c in copies:
        c.wait()


def collide(f, g, fluid, bcell, wanted):
    even = {i: f[i] + f[i + 1] for i in FIRST}
    diff = {i: f[i] - f[i + 1] for i in FIRST}
    rho = f[0] + (1.0 - fluid)
    for i in FIRST:
        rho = rho + even[i]
    momx, momy, momz = vector_sums(diff)
    inv = 1.0 / rho
    ux, uy, uz = momx * inv, momy * inv, momz * inv
    bval = g[0] + g[1] + g[2] + g[3] + g[4] + g[5] + g[6]
    current = (g[3] - g[4]) - bval * uy
    shear = (even[7] - even[9]) - momx * uy
    force = (COUPLE * bcell) * current
    vx = ux + TAU_PLUS * force * inv
    base = 1.0 - 1.5 * (vx * vx + uy * uy + uz * uz)
    post = {}
    if 0 in wanted:
        post[0] = f[0] - 2.0 * PLUS * (f[0] - (W0 * rho) * base)
    rho1, rho2 = W1 * rho, W2 * rho
    for i in FIRST:
        if i not in wanted and i + 1 not in wanted:
            continue
        wr = rho1 if i <= 6 else rho2
        a = along(i, vx, uy, uz)
        ne = PLUS * (even[i] - (2.0 * wr) * (base + 4.5 * a * a))
        no = MINUS * (diff[i] - (6.0 * wr) * a)
        if i in wanted:
            post[i] = f[i] - ne - no
        if i + 1 in wanted:
            post[i + 1] = f[i + 1] - ne + no
    common = bval + (SOURCE * bcell) * shear
    slope = 4.0 * bval
    if NF in wanted:
        post[NF] = V0 * common
    for k, u in ((1, ux), (3, uy), (5, uz)):
        if NF + k in wanted:
            post[NF + k] = V1 * (common + slope * u)
        if NF + k + 1 in wanted:
            post[NF + k + 1] = V1 * (common - slope * u)
    return post


def rim_kernel(
    flow_ref, field_ref, adjf_ref, adjg_ref, profile_ref, strengths_ref, wall_ref, magnet_ref,
    first_ref, second_ref, right_ref, left_ref,
    rows_v, faces_v, profile_v, wall_v, magnet_v, strengths_v, message_v, cell_sem, rows_sem,
    faces_sem, adj_sem,
):
    sx, sy = profile_v.shape[:2]
    odd = lax.rem(lax.axis_index("gy"), 2)
    ends = (sy - 1, 0)
    sides = (0, sx - 1)

    def adj_at(i, where):
        return adjf_ref.at[(i, *where)] if i < NF else adjg_ref.at[(i - NF, *where)]

    rows = []
    for n, y in enumerate(ends):
        rows += [
            pltpu.make_async_copy(
                flow_ref.at[:, :, y], rows_v.at[n, pl.ds(0, NF)], rows_sem.at[n, 0]
            ),
            pltpu.make_async_copy(
                field_ref.at[:, :, y], rows_v.at[n, pl.ds(NF, NG)], rows_sem.at[n, 1]
            ),
        ]
    cells = [
        pltpu.make_async_copy(a, b, cell_sem.at[n])
        for n, (a, b) in enumerate(
            (
                (wall_ref, wall_v),
                (magnet_ref, magnet_v),
                (strengths_ref, strengths_v),
                (profile_ref, profile_v),
            )
        )
    ]
    faces = []
    for n, x in enumerate(sides):
        faces += [
            pltpu.make_async_copy(
                flow_ref.at[:, x], faces_v.at[n, pl.ds(0, NF)], faces_sem.at[n, 0]
            ),
            pltpu.make_async_copy(
                field_ref.at[:, x], faces_v.at[n, pl.ds(NF, NG)], faces_sem.at[n, 1]
            ),
        ]
    adjs = []
    for s in range(6):
        for n, (i, where, out) in enumerate(
            (
                (DOWN[s], (slice(None), ends[0]), message_v.at[0]),
                (UP[s], (slice(None), ends[1]), message_v.at[1]),
                (RIGHT[s], (sides[0],), left_ref),
                (LEFT[s], (sides[1],), right_ref),
            )
        ):
            adjs.append(pltpu.make_async_copy(adj_at(i, where), out.at[6 + s], adj_sem.at[n, s]))
    start_all(rows[:2])
    start_all(cells)
    start_all(rows[2:])
    start_all(faces)
    start_all(adjs)
    wait_all(cells)
    table = lane_table(strengths_v)
    for n, (y, wanted) in enumerate(zip(ends, (UP, DOWN))):
        wait_all(rows[2 * n : 2 * n + 2])
        fluid = 1.0 - wall_v[:, y, :].astype(jnp.float32)
        bcell = gather_strength(table, magnet_v[:, y, :]) * profile_v[:, y, :]
        post = collide(
            [rows_v[n, i] for i in range(NF)],
            [rows_v[n, NF + k] for k in range(NG)],
            fluid,
            bcell,
            wanted,
        )
        for s in range(6):
            message_v[n, s] = post[wanted[s]]
        message_v[n, MASK] = fluid
    for n, (x, wanted, out) in enumerate(
        ((sides[0], LEFT, left_ref), (sides[1], RIGHT, right_ref))
    ):
        wait_all(faces[2 * n : 2 * n + 2])
        fluid = 1.0 - wall_v[x].astype(jnp.float32)
        bcell = gather_strength(table, magnet_v[x]) * profile_v[x]
        post = collide(
            [faces_v[n, i] for i in range(NF)],
            [faces_v[n, NF + k] for k in range(NG)],
            fluid,
            bcell,
            wanted,
        )
        for s in range(6):
            out[s] = post[wanted[s]]
        out[MASK] = fluid
    wait_all(adjs)
    first_ref[...] = message_v[odd]
    second_ref[...] = message_v[1 - odd]


ANY = pl.BlockSpec(memory_space=pl.ANY)
VMEM = pl.BlockSpec(memory_space=pltpu.VMEM)


def rim_call(flow, field, adjf, adjg, profile, strengths, wall, magnet):
    sx, sy, sz = profile.shape
    cells = pltpu.VMEM((sx, sy, sz), jnp.float32)
    names = pltpu.VMEM((sx, sy, sz), jnp.int32)
    rows = pltpu.VMEM((SLOTS, sx, sz), jnp.float32)
    faces = pltpu.VMEM((SLOTS, sy, sz), jnp.float32)
    dma = pltpu.SemaphoreType.DMA
    return pl.pallas_call(
        rim_kernel,
        in_specs=[ANY] * 8,
        out_specs=[VMEM] * 4,
        out_shape=[rows, rows, faces, faces],
        scratch_shapes=[
            pltpu.VMEM((2, NP, sx, sz), jnp.float32),
            pltpu.VMEM((2, NP, sy, sz), jnp.float32),
            cells,
            names,
            names,
            pltpu.VMEM(strengths.shape, jnp.float32),
            pltpu.VMEM((2, SLOTS, sx, sz), jnp.float32),
            dma((4,)),
            dma((2, 2)),
            dma((2, 2)),
            dma((4, 6)),
        ],
        compiler_params=pltpu.CompilerParams(vmem_limit_bytes=RIM_VMEM),
        name="rims",
    )(flow, field, adjf, adjg, profile, strengths, wall, magnet)


def collide_kernel(
    flow_ref, field_ref, profile_ref, strengths_ref, wall_ref, magnet_ref,
    post_ref, fluid_ref, bcell_ref,
):
    table = lane_table(strengths_ref)

    def body(x, carry):
        fluid = 1.0 - wall_ref[x].astype(jnp.float32)
        bcell = gather_strength(table, magnet_ref[x]) * profile_ref[x]
        fluid_ref[x] = fluid
        bcell_ref[x] = bcell
        f = [flow_ref[i, x] for i in range(NF)]
        g = [field_ref[k, x] for k in range(NG)]
        for i, value in collide(f, g, fluid, bcell, range(NP)).items():
            post_ref[i, x] = value
        return carry

    lax.fori_loop(0, fluid_ref.shape[0], body, 0)


def collide_call(flow, field, profile, strengths, wall, magnet):
    sx, sy, sz = profile.shape
    full = pltpu.VMEM((NP, sx, sy, sz), jnp.float32)
    cells = pltpu.VMEM((sx, sy, sz), jnp.float32)
    return pl.pallas_call(
        collide_kernel,
        in_specs=[VMEM] * 6,
        out_specs=[VMEM] * 3,
        out_shape=[full, cells, cells],
        compiler_params=pltpu.CompilerParams(vmem_limit_bytes=COLLIDE_VMEM),
        cost_estimate=pl.CostEstimate(
            flops=300 * sx * sy * sz, bytes_accessed=12 * NP * sx * sy * sz, transcendentals=0
        ),
        name="collide",
    )(flow, field, profile, strengths, wall, magnet)


CORNER_RIGHT = ((0, 7, 0, 8), (1, 9, 1, 10))
CORNER_LEFT = ((0, 10, 0, 9), (1, 8, 1, 7))


def corner_slots(side, post, adj):
    posts, adjs = (UP, DOWN) if side == 0 else (DOWN, UP)
    return posts.index(post), 6 + adjs.index(adj), MASK


def corner_kernel(first_ref, second_ref, after_ref, right_ref, left_ref):
    del after_ref
    odd = lax.rem(lax.axis_index("gy"), 2) == 1
    sx = first_ref.shape[1]

    def row(side, slot, x):
        a, b = first_ref[slot, x : x + 1, :], second_ref[slot, x : x + 1, :]
        return jnp.where(odd, a, b) if side == 0 else jnp.where(odd, b, a)

    for out, table, x in ((right_ref, CORNER_RIGHT, sx - 1), (left_ref, CORNER_LEFT, 0)):
        out[...] = jnp.zeros_like(out)
        for side, post, _, adj in table:
            for n, slot in enumerate(corner_slots(side, post, adj)):
                out[2 * n + side : 2 * n + side + 1, :] = row(side, slot, x)


def corner_call(first, second, after):
    sz = first.shape[2]
    out = pltpu.VMEM((8, sz), jnp.float32)
    return pl.pallas_call(
        corner_kernel,
        in_specs=[VMEM, VMEM, ANY],
        out_specs=[VMEM, VMEM],
        out_shape=[out, out],
        compiler_params=pltpu.CompilerParams(vmem_limit_bytes=2 << 20),
        name="corners",
    )(first, second, after)


def plane_step(
    x_index, post, post_row, adj, adj_row, mask, mask_row, fluid, bcell, profile, magnet,
    near_ref, new_ref, out_ref, sums_ref, count,
):
    sy, sz = fluid.shape
    yi = lax.broadcasted_iota(jnp.int32, (sy, sz), 0)
    zi = lax.broadcasted_iota(jnp.int32, (sy, sz), 1)
    top, bottom = yi == sy - 1, yi == 0
    zlast, zfirst = zi == sz - 1, zi == 0

    def shift(value, row, dy, dz):
        if dy == -1:
            value = jnp.where(bottom, row(), pltpu.roll(value, 1, 0))
        elif dy == 1:
            value = jnp.where(top, row(), pltpu.roll(value, sy - 1, 0))
        if dz == -1:
            value = pltpu.roll(value, 1, 1)
        elif dz == 1:
            value = pltpu.roll(value, sz - 1, 1)
        return value

    def moved(get, get_row, i, sign):
        dx, dy, dz = (sign * c for c in LATTICE[i if i < NF else i - NF])
        return shift(get(i, dx), lambda: get_row(i, dx, dy), dy, dz)

    def near_of(i, sign):
        dx, dy, dz = (sign * c for c in LATTICE[i])
        value = shift(mask(dx), lambda: mask_row(dx, dy), dy, dz)
        if dz == -1:
            value = jnp.where(zfirst, 0.0, value)
        elif dz == 1:
            value = jnp.where(zlast, 0.0, value)
        return value

    for n, i in enumerate(FIRST):
        near_ref[2 * n] = near_of(i, -1)
        near_ref[2 * n + 1] = near_of(i, 1)

    def near(n):
        return near_ref[2 * n] > 0.5, near_ref[2 * n + 1] > 0.5

    def pull(i, n):
        minus, plus = near(n)
        a = fluid * jnp.where(minus, moved(post, post_row, i, -1), post(i + 1, 0))
        b = fluid * jnp.where(plus, moved(post, post_row, i + 1, -1), post(i, 0))
        new_ref[i, x_index] = a
        new_ref[i + 1, x_index] = b
        return a, b

    f0 = fluid * post(0, 0)
    new_ref[0, x_index] = f0
    rho = f0 + (1.0 - fluid)
    momx = momy = momz = shear0 = 0.0
    for n, i in enumerate(FIRST):
        a, b = pull(i, n)
        s, d = a + b, a - b
        rho = rho + s
        cx, cy, cz = LATTICE[i]
        if cx:
            momx = momx + d
        if cy:
            momy = momy + d if cy > 0 else momy - d
        if cz:
            momz = momz + d if cz > 0 else momz - d
        if cx and cy:
            shear0 = shear0 + s if cx * cy > 0 else shear0 - s
    g0 = fluid * post(NF, 0)
    new_ref[NF, x_index] = g0
    bval = g0
    gy = None
    for n, k in enumerate((1, 3, 5)):
        a, b = pull(NF + k, n)
        bval = bval + (a + b)
        if k == 3:
            gy = a - b
    inv = 1.0 / rho
    ux, uy, uz = momx * inv, momy * inv, momz * inv
    current = gy - bval * uy
    shear = shear0 - momx * uy
    force = (COUPLE * bcell) * current
    vx = ux + TAU_PLUS * force * inv

    def push(i, n):
        minus, plus = near(n)
        a = fluid * jnp.where(plus, moved(adj, adj_row, i, 1), adj(i + 1, 0))
        b = fluid * jnp.where(minus, moved(adj, adj_row, i + 1, 1), adj(i, 0))
        return a, b

    l0 = fluid * adj(0, 0)
    out_ref[0, x_index] = (1.0 - 2.0 * PLUS) * l0
    total = (2.0 * PLUS * W0) * l0
    m1 = [0.0, 0.0, 0.0]
    m2 = {}
    for n, i in enumerate(FIRST):
        a, b = push(i, n)
        s, d = a + b, a - b
        de = (0.5 - PLUS) * s
        do = (0.5 - MINUS) * d
        out_ref[i, x_index] = de + do
        out_ref[i + 1, x_index] = de - do
        w = weight(i)
        s = (2.0 * PLUS * w) * s
        d = (2.0 * MINUS * w) * d
        total = total + s
        c = LATTICE[i]
        for axis in range(3):
            if c[axis]:
                m1[axis] = m1[axis] + d if c[axis] > 0 else m1[axis] - d
            for other in range(axis, 3):
                sign = c[axis] * c[other]
                if sign:
                    old = m2.get((axis, other))
                    if old is None:
                        m2[axis, other] = s if sign > 0 else -s
                    else:
                        m2[axis, other] = old + s if sign > 0 else old - s
    h0 = fluid * adj(NF, 0)
    hsum = V0 * h0
    h1 = []
    hs = None
    for n, k in enumerate((1, 3, 5)):
        a, b = push(NF + k, n)
        hs = a + b if hs is None else hs + (a + b)
        h1.append(V1 * (a - b))
    hsum = hsum + V1 * hs

    base = 1.0 - 1.5 * (vx * vx + uy * uy + uz * uz)
    tx = m2[0, 0] * vx + m2[0, 1] * uy + m2[0, 2] * uz
    ty = m2[0, 1] * vx + m2[1, 1] * uy + m2[1, 2] * uz
    tz = m2[0, 2] * vx + m2[1, 2] * uy + m2[2, 2] * uz
    rhobar = (
        total * base
        + 4.5 * (vx * tx + uy * ty + uz * tz)
        + 3.0 * (m1[0] * vx + m1[1] * uy + m1[2] * uz)
    )
    total3 = 3.0 * total
    vxbar = rho * (9.0 * tx + 3.0 * m1[0] - total3 * vx)
    uybar = rho * (9.0 * ty + 3.0 * m1[1] - total3 * uy)
    uzbar = rho * (9.0 * tz + 3.0 * m1[2] - total3 * uz)
    slope = 4.0 * bval
    forcebar = (TAU_PLUS * vxbar) * inv
    rhobar = rhobar - forcebar * force * inv
    currentbar = (COUPLE * bcell) * forcebar
    shearbar = (SOURCE * bcell) * hsum
    dcell = COUPLE * current * forcebar + SOURCE * shear * hsum
    uxbar = vxbar + slope * h1[0]
    uybar = uybar + slope * h1[1] - bval * currentbar - momx * shearbar
    uzbar = uzbar + slope * h1[2]
    bbar = hsum + 4.0 * (h1[0] * ux + h1[1] * uy + h1[2] * uz) - uy * currentbar
    mxbar = uxbar * inv - uy * shearbar
    mybar = uybar * inv
    mzbar = uzbar * inv
    rhobar = rhobar - (ux * uxbar + uy * uybar + uz * uzbar) * inv

    out_ref[0, x_index] = out_ref[0, x_index] + rhobar
    for i in FIRST:
        cm = along(i, mxbar, mybar, mzbar)
        cx, cy, _ = LATTICE[i]
        common = rhobar
        if cx and cy:
            common = rhobar + shearbar if cx * cy > 0 else rhobar - shearbar
        out_ref[i, x_index] = out_ref[i, x_index] + (common + cm)
        out_ref[i + 1, x_index] = out_ref[i + 1, x_index] + (common - cm)
    for k in range(NG):
        value = bbar
        if k == 3:
            value = bbar + currentbar
        elif k == 4:
            value = bbar - currentbar
        out_ref[NF + k, x_index] = value

    share = dcell * profile
    for m in range(count):
        hit = jnp.where(magnet == m, share, 0.0)
        part = hit[:, 0:128]
        for z in range(128, sz, 128):
            part = part + hit[:, z : z + 128]
        sums_ref[m] = sums_ref[m] + part


def halo_slot(kind, i, dy):
    names = (UP, DOWN) if (dy == -1) == (kind == 0) else (DOWN, UP)
    return names[0].index(i) + 6 * kind


def face_slot(kind, i, dx):
    names = RIGHT if (dx == -1) == (kind == 0) else LEFT
    return names.index(i) + 6 * kind


def adj_plane(adjf_ref, adjg_ref, i, x):
    return adjf_ref[i, x] if i < NF else adjg_ref[i - NF, x]


def load_halo(first_ref, second_ref, halo_ref):
    odd = lax.rem(lax.axis_index("gy"), 2)
    halo_ref[1 - odd] = first_ref[...]
    halo_ref[odd] = second_ref[...]
    here = lax.axis_index("gy")
    keep_low = jnp.where(here == 0, 0.0, 1.0)
    keep_high = jnp.where(here == lax.axis_size("gy") - 1, 0.0, 1.0)
    halo_ref[0, MASK] = halo_ref[0, MASK] * keep_low
    halo_ref[1, MASK] = halo_ref[1, MASK] * keep_high
    return keep_low, keep_high


def plane_stores(n, x, new_v, out_v, newf_ref, newg_ref, outf_ref, outg_ref, sem):
    pairs = (
        (new_v.at[pl.ds(0, NF), n], newf_ref.at[:, x]),
        (new_v.at[pl.ds(NF, NG), n], newg_ref.at[:, x]),
        (out_v.at[pl.ds(0, NF), n], outf_ref.at[:, x]),
        (out_v.at[pl.ds(NF, NG), n], outg_ref.at[:, x]),
    )
    return [pltpu.make_async_copy(a, b, sem.at[k, n]) for k, (a, b) in enumerate(pairs)]


def inner_kernel(
    post_ref, adjf_ref, adjg_ref, fluid_ref, bcell_ref, first_ref, second_ref, profile_ref,
    magnet_ref,
    newf_ref, newg_ref, outf_ref, outg_ref, sums_ref,
    new_v, out_v, halo_v, near_v, store_sem,
):
    sx = fluid_ref.shape[0]
    count = sums_ref.shape[0]

    def stores(x):
        return plane_stores(
            x, x, new_v, out_v, newf_ref, newg_ref, outf_ref, outg_ref, store_sem
        )

    sums_ref[...] = jnp.zeros_like(sums_ref)
    load_halo(first_ref, second_ref, halo_v)

    def body(x, carry):
        def row_of(slot, dx, dy):
            return halo_v[0 if dy == -1 else 1, slot, pl.ds(x + dx, 1), :]

        plane_step(
            x,
            lambda i, dx: post_ref[i, x + dx],
            lambda i, dx, dy: row_of(halo_slot(0, i, dy), dx, dy),
            lambda i, dx: adj_plane(adjf_ref, adjg_ref, i, x + dx),
            lambda i, dx, dy: row_of(halo_slot(1, i, dy), dx, dy),
            lambda dx: fluid_ref[x + dx],
            lambda dx, dy: row_of(MASK, dx, dy),
            fluid_ref[x],
            bcell_ref[x],
            profile_ref[x],
            magnet_ref[x],
            near_v,
            new_v,
            out_v,
            sums_ref,
            count,
        )
        start_all(stores(x))
        return carry

    lax.fori_loop(1, sx - 1, body, 0)
    for x in range(1, sx - 1):
        wait_all(stores(x))


def inner_call(post, adjf, adjg, fluid, bcell, first, second, profile, magnet, count):
    sx, sy, sz = profile.shape
    full = pltpu.VMEM((NP, sx, sy, sz), jnp.float32)
    flow = jax.ShapeDtypeStruct((NF, sx, sy, sz), jnp.float32)
    field = jax.ShapeDtypeStruct((NG, sx, sy, sz), jnp.float32)
    return pl.pallas_call(
        inner_kernel,
        in_specs=[VMEM] * 9,
        out_specs=[ANY, ANY, ANY, ANY, VMEM],
        out_shape=[flow, field, flow, field, pltpu.VMEM((count, 8, 128), jnp.float32)],
        scratch_shapes=[
            full,
            full,
            pltpu.VMEM((2, SLOTS, sx, sz), jnp.float32),
            pltpu.VMEM((18, sy, sz), jnp.float32),
            pltpu.SemaphoreType.DMA((4, sx)),
        ],
        compiler_params=pltpu.CompilerParams(vmem_limit_bytes=INNER_VMEM),
        cost_estimate=pl.CostEstimate(
            flops=700 * sx * sy * sz, bytes_accessed=16 * NP * sx * sy * sz, transcendentals=0
        ),
        name="inner",
    )(post, adjf, adjg, fluid, bcell, first, second, profile, magnet)


def outer_kernel(
    scale, second_ref, fromleft_ref, fromright_ref, first_ref, post_ref, adjf_ref, adjg_ref,
    fluid_ref, bcell_ref,
    cornerright_ref, cornerleft_ref, profile_ref, magnet_ref,
    partial_ref, newf_in, newg_in, outf_in, outg_in,
    newf_ref, newg_ref, outf_ref, outg_ref, share_ref,
    new_v, out_v, halo_v, near_v, sums_v, store_sem,
):
    del newf_in, newg_in, outf_in, outg_in
    sx = fluid_ref.shape[0]
    count = sums_v.shape[0]
    sums_v[...] = partial_ref[...]
    keep_low, keep_high = load_halo(first_ref, second_ref, halo_v)
    stores = []
    for n, (x, away) in enumerate(((0, -1), (sx - 1, 1))):
        face_ref, corner_ref = (
            (fromleft_ref, cornerleft_ref) if away == -1 else (fromright_ref, cornerright_ref)
        )

        def get(kind, i, dx, x=x, away=away, face_ref=face_ref):
            if dx == away:
                return face_ref[face_slot(kind, i, dx)]
            if kind == 1:
                return adj_plane(adjf_ref, adjg_ref, i, x + dx)
            return post_ref[i, x + dx]

        def row(kind, i, dx, dy, x=x, away=away, corner_ref=corner_ref):
            side = 0 if dy == -1 else 1
            if dx == away:
                line = corner_ref[2 * kind + side : 2 * kind + side + 1, :]
                if kind == 2:
                    line = line * (keep_low if side == 0 else keep_high)
                return line
            slot = MASK if kind == 2 else halo_slot(kind, i, dy)
            return halo_v[side, slot, x + dx : x + dx + 1, :]

        def mask(dx, x=x, away=away, face_ref=face_ref):
            return face_ref[MASK] if dx == away else fluid_ref[x + dx]

        plane_step(
            n,
            lambda i, dx, get=get: get(0, i, dx),
            lambda i, dx, dy, row=row: row(0, i, dx, dy),
            lambda i, dx, get=get: get(1, i, dx),
            lambda i, dx, dy, row=row: row(1, i, dx, dy),
            mask,
            lambda dx, dy, row=row: row(2, 0, dx, dy),
            fluid_ref[x],
            bcell_ref[x],
            profile_ref[x],
            magnet_ref[x],
            near_v,
            new_v,
            out_v,
            sums_v,
            count,
        )
        these = plane_stores(
            n, x, new_v, out_v, newf_ref, newg_ref, outf_ref, outg_ref, store_sem
        )
        start_all(these)
        stores += these
    rows = jnp.concatenate(
        [jnp.sum(sums_v[m], axis=0, keepdims=True) for m in range(count)], axis=0
    )
    share_ref[...] = lax.dot_general(
        jnp.ones((share_ref.shape[0], 128), jnp.float32),
        rows * scale,
        (((1,), (1,)), ((), ())),
        precision=lax.Precision.HIGHEST,
        preferred_element_type=jnp.float32,
    )
    wait_all(stores)


def outer_call(
    post, adjf, adjg, fluid, bcell, first, second, fromleft, fromright, cornerleft, cornerright,
    profile, magnet, partial, newf, newg, outf, outg, scale,
):
    sx, sy, sz = profile.shape
    count = partial.shape[0]
    flow = jax.ShapeDtypeStruct(newf.shape, jnp.float32)
    field = jax.ShapeDtypeStruct(newg.shape, jnp.float32)
    return pl.pallas_call(
        functools.partial(outer_kernel, scale),
        in_specs=[VMEM] * 14 + [ANY] * 4,
        out_specs=[ANY] * 4 + [VMEM],
        out_shape=[
            flow,
            field,
            flow,
            field,
            jax.ShapeDtypeStruct((lax.axis_size(("gx", "gy")), count), jnp.float32),
        ],
        input_output_aliases={14: 0, 15: 1, 16: 2, 17: 3},
        scratch_shapes=[
            pltpu.VMEM((NP, 2, sy, sz), jnp.float32),
            pltpu.VMEM((NP, 2, sy, sz), jnp.float32),
            pltpu.VMEM((2, SLOTS, sx, sz), jnp.float32),
            pltpu.VMEM((18, sy, sz), jnp.float32),
            pltpu.VMEM((count, 8, 128), jnp.float32),
            pltpu.SemaphoreType.DMA((4, 2)),
        ],
        compiler_params=pltpu.CompilerParams(vmem_limit_bytes=OUTER_VMEM),
        name="outer",
    )(
        second, fromleft, fromright, first, post, adjf, adjg, fluid, bcell, cornerright,
        cornerleft, profile, magnet, partial, newf, newg, outf, outg,
    )


def ring(count, step):
    return [(i, (i + step) % count) for i in range(count)]


def on_device(flow, field, adj_flow_in, adj_field_in, profile, strengths, wall, magnet):
    across, around = lax.axis_size("gy"), lax.axis_size("gx")
    count = strengths.shape[0]
    table = strengths.reshape(1, count)
    arrays = (flow, field, adj_flow_in, adj_field_in, profile, table, wall, magnet)
    mine1, mine2, right, left = rim_call(*arrays)
    inside = [(i, i ^ 1) for i in range(across)]
    between = [(i, (((i + 1) ^ 1) - 1) % across) for i in range(across)]
    second = lax.ppermute(mine2, "gy", between)
    first = lax.ppermute(mine1, "gy", inside)
    fromleft = lax.ppermute(right, "gx", ring(around, 1))
    fromright = lax.ppermute(left, "gx", ring(around, -1))
    post, fluid, bcell = collide_call(flow, field, profile, table, wall, magnet)
    corner_r, corner_l = corner_call(first, second, bcell)
    cornerleft = lax.ppermute(corner_r, "gx", ring(around, 1))
    cornerright = lax.ppermute(corner_l, "gx", ring(around, -1))
    newf, newg, outf, outg, partial = inner_call(
        post, adj_flow_in, adj_field_in, fluid, bcell, first, second, profile, magnet, count
    )
    cells = flow.shape[1] * around * flow.shape[2] * across * flow.shape[3]
    newf, newg, outf, outg, share = outer_call(
        post, adj_flow_in, adj_field_in, fluid, bcell, first, second, fromleft, fromright, cornerleft, cornerright,
        profile, magnet, partial, newf, newg, outf, outg, 1.0 / math.sqrt(cells / count),
    )
    totals = jnp.sum(lax.all_to_all(share, ("gx", "gy"), 0, 0, tiled=True), axis=0)
    return (newf, newg, outf, outg, totals)


def solution(mesh):
    stack = P(None, "gx", "gy", None)
    cell = P("gx", "gy", None)
    return jax.shard_map(
        on_device,
        mesh=mesh,
        in_specs=(stack, stack, stack, stack, cell, P(), cell, cell),
        out_specs=(stack, stack, stack, stack, P()),
        check_vma=False,
    )
```

```python
import functools
import math

import jax
import jax.numpy as jnp
from jax import lax
from jax.experimental import pallas as pl
from jax.experimental.pallas import tpu as pltpu
from jax.sharding import PartitionSpec as P

LATTICE = [
    (0, 0, 0),
    (1, 0, 0),
    (-1, 0, 0),
    (0, 1, 0),
    (0, -1, 0),
    (0, 0, 1),
    (0, 0, -1),
    (1, 1, 0),
    (-1, -1, 0),
    (1, -1, 0),
    (-1, 1, 0),
    (1, 0, 1),
    (-1, 0, -1),
    (1, 0, -1),
    (-1, 0, 1),
    (0, 1, 1),
    (0, -1, -1),
    (0, 1, -1),
    (0, -1, 1),
]
NF, NG = 19, 7
NP = NF + NG
FIRST = [1, 3, 5, 7, 9, 11, 13, 15, 17]
W0, W1, W2 = 1.0 / 3.0, 1.0 / 18.0, 1.0 / 36.0
V0, V1 = 0.25, 0.125
PLUS = 0.625
MINUS = 0.5 / 1.125
TAU_PLUS = 0.8
COUPLE = 2.0
SOURCE = 2.0

UP = [3, 7, 10, 15, 17, NF + 3]
DOWN = [4, 8, 9, 16, 18, NF + 4]
RIGHT = [1, 7, 9, 11, 13, NF + 1]
LEFT = [2, 8, 10, 12, 14, NF + 2]
SLOTS = 13
MASK = 12
TURNED = [5, 6, 11, 12, 13, 14, NF + 5, NF + 6]

RIM_VMEM = 58 << 20
COLLIDE_VMEM = 4 << 20
INNER_VMEM = 12 << 20
OUTER_VMEM = 8 << 20


def weight(i):
    return W1 if i <= 6 else W2


def gather_strength(table, magnet):
    parts = [
        jnp.take_along_axis(table, magnet[:, z : z + 128], axis=1, mode="promise_in_bounds")
        for z in range(0, magnet.shape[1], 128)
    ]
    return jnp.concatenate(parts, axis=1)


def lane_table(strengths_ref):
    row = strengths_ref[...]
    rest = 128 - row.shape[1]
    if rest:
        row = jnp.concatenate([row, jnp.zeros((1, rest), jnp.float32)], axis=1)
    return jnp.broadcast_to(row, (8, 128))


def vector_sums(pair):
    x = pair[1] + pair[7] + pair[9] + pair[11] + pair[13]
    y = pair[3] + pair[7] - pair[9] + pair[15] + pair[17]
    z = pair[5] + pair[11] - pair[13] + pair[15] - pair[17]
    return x, y, z


def along(i, vx, vy, vz):
    out = None
    for c, v in zip(LATTICE[i], (vx, vy, vz)):
        if c:
            if out is None:
                out = v if c > 0 else -v
            else:
                out = out + v if c > 0 else out - v
    return out


def start_all(copies):
    for c in copies:
        c.start()


def wait_all(copies):
    for c in copies:
        c.wait()


def collide(f, g, fluid, bcell, wanted):
    even = {i: f[i] + f[i + 1] for i in FIRST}
    diff = {i: f[i] - f[i + 1] for i in FIRST}
    rho = f[0] + (1.0 - fluid)
    for i in FIRST:
        rho = rho + even[i]
    momx, momy, momz = vector_sums(diff)
    inv = 1.0 / rho
    ux, uy, uz = momx * inv, momy * inv, momz * inv
    bval = g[0] + g[1] + g[2] + g[3] + g[4] + g[5] + g[6]
    current = (g[3] - g[4]) - bval * uy
    shear = (even[7] - even[9]) - momx * uy
    force = (COUPLE * bcell) * current
    vx = ux + TAU_PLUS * force * inv
    base = 1.0 - 1.5 * (vx * vx + uy * uy + uz * uz)
    post = {}
    if 0 in wanted:
        post[0] = f[0] - 2.0 * PLUS * (f[0] - (W0 * rho) * base)
    rho1, rho2 = W1 * rho, W2 * rho
    for i in FIRST:
        if i not in wanted and i + 1 not in wanted:
            continue
        wr = rho1 if i <= 6 else rho2
        a = along(i, vx, uy, uz)
        ne = PLUS * (even[i] - (2.0 * wr) * (base + 4.5 * a * a))
        no = MINUS * (diff[i] - (6.0 * wr) * a)
        if i in wanted:
            post[i] = f[i] - ne - no
        if i + 1 in wanted:
            post[i + 1] = f[i + 1] - ne + no
    common = bval + (SOURCE * bcell) * shear
    slope = 4.0 * bval
    if NF in wanted:
        post[NF] = V0 * common
    for k, u in ((1, ux), (3, uy), (5, uz)):
        if NF + k in wanted:
            post[NF + k] = V1 * (common + slope * u)
        if NF + k + 1 in wanted:
            post[NF + k + 1] = V1 * (common - slope * u)
    return post


def rim_kernel(
    flow_ref, field_ref, adjf_ref, adjg_ref, profile_ref, strengths_ref, wall_ref, magnet_ref,
    first_ref, second_ref, right_ref, left_ref,
    rows_v, faces_v, profile_v, wall_v, magnet_v, strengths_v, message_v, cell_sem, rows_sem,
    faces_sem, adj_sem,
):
    sx, sy = profile_v.shape[:2]
    odd = lax.rem(lax.axis_index("gy"), 2)
    ends = (sy - 1, 0)
    sides = (0, sx - 1)

    def adj_at(i, where):
        return adjf_ref.at[(i, *where)] if i < NF else adjg_ref.at[(i - NF, *where)]

    rows = []
    for n, y in enumerate(ends):
        rows += [
            pltpu.make_async_copy(
                flow_ref.at[:, :, y], rows_v.at[n, pl.ds(0, NF)], rows_sem.at[n, 0]
            ),
            pltpu.make_async_copy(
                field_ref.at[:, :, y], rows_v.at[n, pl.ds(NF, NG)], rows_sem.at[n, 1]
            ),
        ]
    cells = [
        pltpu.make_async_copy(a, b, cell_sem.at[n])
        for n, (a, b) in enumerate(
            (
                (wall_ref, wall_v),
                (magnet_ref, magnet_v),
                (strengths_ref, strengths_v),
                (profile_ref, profile_v),
            )
        )
    ]
    faces = []
    for n, x in enumerate(sides):
        faces += [
            pltpu.make_async_copy(
                flow_ref.at[:, x], faces_v.at[n, pl.ds(0, NF)], faces_sem.at[n, 0]
            ),
            pltpu.make_async_copy(
                field_ref.at[:, x], faces_v.at[n, pl.ds(NF, NG)], faces_sem.at[n, 1]
            ),
        ]
    adjs = []
    for s in range(6):
        for n, (i, where, out) in enumerate(
            (
                (DOWN[s], (slice(None), ends[0]), message_v.at[0]),
                (UP[s], (slice(None), ends[1]), message_v.at[1]),
                (RIGHT[s], (sides[0],), left_ref),
                (LEFT[s], (sides[1],), right_ref),
            )
        ):
            adjs.append(pltpu.make_async_copy(adj_at(i, where), out.at[6 + s], adj_sem.at[n, s]))
    start_all(rows[:2])
    start_all(cells)
    start_all(rows[2:])
    start_all(faces)
    start_all(adjs)
    wait_all(cells)
    table = lane_table(strengths_v)
    for n, (y, wanted) in enumerate(zip(ends, (UP, DOWN))):
        wait_all(rows[2 * n : 2 * n + 2])
        fluid = 1.0 - wall_v[:, y, :].astype(jnp.float32)
        bcell = gather_strength(table, magnet_v[:, y, :]) * profile_v[:, y, :]
        post = collide(
            [rows_v[n, i] for i in range(NF)],
            [rows_v[n, NF + k] for k in range(NG)],
            fluid,
            bcell,
            wanted,
        )
        for s in range(6):
            message_v[n, s] = post[wanted[s]]
        message_v[n, MASK] = fluid
    for n, (x, wanted, out) in enumerate(
        ((sides[0], LEFT, left_ref), (sides[1], RIGHT, right_ref))
    ):
        wait_all(faces[2 * n : 2 * n + 2])
        fluid = 1.0 - wall_v[x].astype(jnp.float32)
        bcell = gather_strength(table, magnet_v[x]) * profile_v[x]
        post = collide(
            [faces_v[n, i] for i in range(NF)],
            [faces_v[n, NF + k] for k in range(NG)],
            fluid,
            bcell,
            wanted,
        )
        for s in range(6):
            out[s] = post[wanted[s]]
        out[MASK] = fluid
    wait_all(adjs)
    first_ref[...] = message_v[odd]
    second_ref[...] = message_v[1 - odd]


ANY = pl.BlockSpec(memory_space=pl.ANY)
VMEM = pl.BlockSpec(memory_space=pltpu.VMEM)


def rim_call(flow, field, adjf, adjg, profile, strengths, wall, magnet):
    sx, sy, sz = profile.shape
    cells = pltpu.VMEM((sx, sy, sz), jnp.float32)
    names = pltpu.VMEM((sx, sy, sz), jnp.int32)
    rows = pltpu.VMEM((SLOTS, sx, sz), jnp.float32)
    faces = pltpu.VMEM((SLOTS, sy, sz), jnp.float32)
    dma = pltpu.SemaphoreType.DMA
    return pl.pallas_call(
        rim_kernel,
        in_specs=[ANY] * 8,
        out_specs=[VMEM] * 4,
        out_shape=[rows, rows, faces, faces],
        scratch_shapes=[
            pltpu.VMEM((2, NP, sx, sz), jnp.float32),
            pltpu.VMEM((2, NP, sy, sz), jnp.float32),
            cells,
            names,
            names,
            pltpu.VMEM(strengths.shape, jnp.float32),
            pltpu.VMEM((2, SLOTS, sx, sz), jnp.float32),
            dma((4,)),
            dma((2, 2)),
            dma((2, 2)),
            dma((4, 6)),
        ],
        compiler_params=pltpu.CompilerParams(vmem_limit_bytes=RIM_VMEM),
        name="rims",
    )(flow, field, adjf, adjg, profile, strengths, wall, magnet)


def collide_kernel(
    flow_ref, field_ref, profile_ref, strengths_ref, wall_ref, magnet_ref,
    adjf_ref, adjg_ref,
    post_ref, fluid_ref, bcell_ref, turned_ref, zfluid_ref,
):
    table = lane_table(strengths_ref)

    def body(x, carry):
        fluid = 1.0 - wall_ref[x].astype(jnp.float32)
        bcell = gather_strength(table, magnet_ref[x]) * profile_ref[x]
        fluid_ref[x] = fluid
        bcell_ref[x] = bcell
        f = [flow_ref[i, x] for i in range(NF)]
        g = [field_ref[k, x] for k in range(NG)]
        post = collide(f, g, fluid, bcell, range(NP))
        for i, value in post.items():
            post_ref[i, x] = value
        sz = fluid.shape[1]
        for n, i in enumerate(TURNED):
            up = LATTICE[i if i < NF else i - NF][2] > 0
            turned_ref[n, x] = pltpu.roll(post[i], 1 if up else sz - 1, 1)
            value = adj_plane(adjf_ref, adjg_ref, i, x)
            turned_ref[len(TURNED) + n, x] = pltpu.roll(value, sz - 1 if up else 1, 1)
        zi = lax.broadcasted_iota(jnp.int32, fluid.shape, 1)
        zfluid_ref[0, x] = jnp.where(zi == 0, 0.0, pltpu.roll(fluid, 1, 1))
        zfluid_ref[1, x] = jnp.where(zi == sz - 1, 0.0, pltpu.roll(fluid, sz - 1, 1))
        return carry

    lax.fori_loop(0, fluid_ref.shape[0], body, 0)


def collide_call(flow, field, profile, strengths, wall, magnet, adjf, adjg):
    sx, sy, sz = profile.shape
    full = pltpu.VMEM((NP, sx, sy, sz), jnp.float32)
    cells = pltpu.VMEM((sx, sy, sz), jnp.float32)
    return pl.pallas_call(
        collide_kernel,
        in_specs=[VMEM] * 8,
        out_specs=[VMEM] * 5,
        out_shape=[
            full,
            cells,
            cells,
            pltpu.VMEM((2 * len(TURNED), sx, sy, sz), jnp.float32),
            pltpu.VMEM((2, sx, sy, sz), jnp.float32),
        ],
        compiler_params=pltpu.CompilerParams(vmem_limit_bytes=COLLIDE_VMEM),
        cost_estimate=pl.CostEstimate(
            flops=300 * sx * sy * sz, bytes_accessed=12 * NP * sx * sy * sz, transcendentals=0
        ),
        name="collide",
    )(flow, field, profile, strengths, wall, magnet, adjf, adjg)


CORNER_RIGHT = ((0, 7, 0, 8), (1, 9, 1, 10))
CORNER_LEFT = ((0, 10, 0, 9), (1, 8, 1, 7))


def corner_slots(side, post, adj):
    posts, adjs = (UP, DOWN) if side == 0 else (DOWN, UP)
    return posts.index(post), 6 + adjs.index(adj), MASK


def corner_kernel(first_ref, second_ref, after_ref, right_ref, left_ref):
    del after_ref
    odd = lax.rem(lax.axis_index("gy"), 2) == 1
    sx = first_ref.shape[1]

    def row(side, slot, x):
        a, b = first_ref[slot, x : x + 1, :], second_ref[slot, x : x + 1, :]
        return jnp.where(odd, a, b) if side == 0 else jnp.where(odd, b, a)

    for out, table, x in ((right_ref, CORNER_RIGHT, sx - 1), (left_ref, CORNER_LEFT, 0)):
        out[...] = jnp.zeros_like(out)
        for side, post, _, adj in table:
            for n, slot in enumerate(corner_slots(side, post, adj)):
                out[2 * n + side : 2 * n + side + 1, :] = row(side, slot, x)


def corner_call(first, second, after):
    sz = first.shape[2]
    out = pltpu.VMEM((8, sz), jnp.float32)
    return pl.pallas_call(
        corner_kernel,
        in_specs=[VMEM, VMEM, ANY],
        out_specs=[VMEM, VMEM],
        out_shape=[out, out],
        compiler_params=pltpu.CompilerParams(vmem_limit_bytes=2 << 20),
        name="corners",
    )(first, second, after)


def plane_step(
    x_index, post, post_row, adj, adj_row, mask, mask_row, fluid, bcell, profile, magnet,
    near_ref, new_ref, out_ref, sums_ref, count, turned, zmask,
):
    sy, sz = fluid.shape
    yi = lax.broadcasted_iota(jnp.int32, (sy, sz), 0)
    zi = lax.broadcasted_iota(jnp.int32, (sy, sz), 1)
    top, bottom = yi == sy - 1, yi == 0
    zlast, zfirst = zi == sz - 1, zi == 0

    def shift(value, row, dy, dz):
        if dy == -1:
            value = jnp.where(bottom, row(), pltpu.roll(value, 1, 0))
        elif dy == 1:
            value = jnp.where(top, row(), pltpu.roll(value, sy - 1, 0))
        if dz == -1:
            value = pltpu.roll(value, 1, 1)
        elif dz == 1:
            value = pltpu.roll(value, sz - 1, 1)
        return value

    def moved(get, get_row, i, sign):
        dx, dy, dz = (sign * c for c in LATTICE[i if i < NF else i - NF])
        if dz and not dy:
            value = turned(0 if sign == -1 else 1, i, dx)
            if value is not None:
                return value
        return shift(get(i, dx), lambda: get_row(i, dx, dy), dy, dz)

    def near_of(i, sign):
        dx, dy, dz = (sign * c for c in LATTICE[i])
        if dz and not dy:
            value = zmask(dx, dz)
            if value is not None:
                return value
        value = shift(mask(dx), lambda: mask_row(dx, dy), dy, dz)
        if dz == -1:
            value = jnp.where(zfirst, 0.0, value)
        elif dz == 1:
            value = jnp.where(zlast, 0.0, value)
        return value

    for n, i in enumerate(FIRST):
        near_ref[2 * n] = near_of(i, -1)
        near_ref[2 * n + 1] = near_of(i, 1)

    def near(n):
        return near_ref[2 * n] > 0.5, near_ref[2 * n + 1] > 0.5

    def pull(i, n):
        minus, plus = near(n)
        a = fluid * jnp.where(minus, moved(post, post_row, i, -1), post(i + 1, 0))
        b = fluid * jnp.where(plus, moved(post, post_row, i + 1, -1), post(i, 0))
        new_ref[i, x_index] = a
        new_ref[i + 1, x_index] = b
        return a, b

    f0 = fluid * post(0, 0)
    new_ref[0, x_index] = f0
    rho = f0 + (1.0 - fluid)
    momx = momy = momz = shear0 = 0.0
    for n, i in enumerate(FIRST):
        a, b = pull(i, n)
        s, d = a + b, a - b
        rho = rho + s
        cx, cy, cz = LATTICE[i]
        if cx:
            momx = momx + d
        if cy:
            momy = momy + d if cy > 0 else momy - d
        if cz:
            momz = momz + d if cz > 0 else momz - d
        if cx and cy:
            shear0 = shear0 + s if cx * cy > 0 else shear0 - s
    g0 = fluid * post(NF, 0)
    new_ref[NF, x_index] = g0
    bval = g0
    gy = None
    for n, k in enumerate((1, 3, 5)):
        a, b = pull(NF + k, n)
        bval = bval + (a + b)
        if k == 3:
            gy = a - b
    inv = 1.0 / rho
    ux, uy, uz = momx * inv, momy * inv, momz * inv
    current = gy - bval * uy
    shear = shear0 - momx * uy
    force = (COUPLE * bcell) * current
    vx = ux + TAU_PLUS * force * inv

    def push(i, n):
        minus, plus = near(n)
        a = fluid * jnp.where(plus, moved(adj, adj_row, i, 1), adj(i + 1, 0))
        b = fluid * jnp.where(minus, moved(adj, adj_row, i + 1, 1), adj(i, 0))
        return a, b

    l0 = fluid * adj(0, 0)
    out_ref[0, x_index] = (1.0 - 2.0 * PLUS) * l0
    total = (2.0 * PLUS * W0) * l0
    m1 = [0.0, 0.0, 0.0]
    m2 = {}
    for n, i in enumerate(FIRST):
        a, b = push(i, n)
        s, d = a + b, a - b
        de = (0.5 - PLUS) * s
        do = (0.5 - MINUS) * d
        out_ref[i, x_index] = de + do
        out_ref[i + 1, x_index] = de - do
        w = weight(i)
        s = (2.0 * PLUS * w) * s
        d = (2.0 * MINUS * w) * d
        total = total + s
        c = LATTICE[i]
        for axis in range(3):
            if c[axis]:
                m1[axis] = m1[axis] + d if c[axis] > 0 else m1[axis] - d
            for other in range(axis, 3):
                sign = c[axis] * c[other]
                if sign:
                    old = m2.get((axis, other))
                    if old is None:
                        m2[axis, other] = s if sign > 0 else -s
                    else:
                        m2[axis, other] = old + s if sign > 0 else old - s
    h0 = fluid * adj(NF, 0)
    hsum = V0 * h0
    h1 = []
    hs = None
    for n, k in enumerate((1, 3, 5)):
        a, b = push(NF + k, n)
        hs = a + b if hs is None else hs + (a + b)
        h1.append(V1 * (a - b))
    hsum = hsum + V1 * hs

    base = 1.0 - 1.5 * (vx * vx + uy * uy + uz * uz)
    tx = m2[0, 0] * vx + m2[0, 1] * uy + m2[0, 2] * uz
    ty = m2[0, 1] * vx + m2[1, 1] * uy + m2[1, 2] * uz
    tz = m2[0, 2] * vx + m2[1, 2] * uy + m2[2, 2] * uz
    rhobar = (
        total * base
        + 4.5 * (vx * tx + uy * ty + uz * tz)
        + 3.0 * (m1[0] * vx + m1[1] * uy + m1[2] * uz)
    )
    total3 = 3.0 * total
    vxbar = rho * (9.0 * tx + 3.0 * m1[0] - total3 * vx)
    uybar = rho * (9.0 * ty + 3.0 * m1[1] - total3 * uy)
    uzbar = rho * (9.0 * tz + 3.0 * m1[2] - total3 * uz)
    slope = 4.0 * bval
    forcebar = (TAU_PLUS * vxbar) * inv
    rhobar = rhobar - forcebar * force * inv
    currentbar = (COUPLE * bcell) * forcebar
    shearbar = (SOURCE * bcell) * hsum
    dcell = COUPLE * current * forcebar + SOURCE * shear * hsum
    uxbar = vxbar + slope * h1[0]
    uybar = uybar + slope * h1[1] - bval * currentbar - momx * shearbar
    uzbar = uzbar + slope * h1[2]
    bbar = hsum + 4.0 * (h1[0] * ux + h1[1] * uy + h1[2] * uz) - uy * currentbar
    mxbar = uxbar * inv - uy * shearbar
    mybar = uybar * inv
    mzbar = uzbar * inv
    rhobar = rhobar - (ux * uxbar + uy * uybar + uz * uzbar) * inv

    out_ref[0, x_index] = out_ref[0, x_index] + rhobar
    for i in FIRST:
        cm = along(i, mxbar, mybar, mzbar)
        cx, cy, _ = LATTICE[i]
        common = rhobar
        if cx and cy:
            common = rhobar + shearbar if cx * cy > 0 else rhobar - shearbar
        out_ref[i, x_index] = out_ref[i, x_index] + (common + cm)
        out_ref[i + 1, x_index] = out_ref[i + 1, x_index] + (common - cm)
    for k in range(NG):
        value = bbar
        if k == 3:
            value = bbar + currentbar
        elif k == 4:
            value = bbar - currentbar
        out_ref[NF + k, x_index] = value

    share = dcell * profile
    for m in range(count):
        hit = jnp.where(magnet == m, share, 0.0)
        part = hit[:, 0:128]
        for z in range(128, sz, 128):
            part = part + hit[:, z : z + 128]
        sums_ref[m] = sums_ref[m] + part


def halo_slot(kind, i, dy):
    names = (UP, DOWN) if (dy == -1) == (kind == 0) else (DOWN, UP)
    return names[0].index(i) + 6 * kind


def face_slot(kind, i, dx):
    names = RIGHT if (dx == -1) == (kind == 0) else LEFT
    return names.index(i) + 6 * kind


def adj_plane(adjf_ref, adjg_ref, i, x):
    return adjf_ref[i, x] if i < NF else adjg_ref[i - NF, x]


def load_halo(first_ref, second_ref, halo_ref):
    odd = lax.rem(lax.axis_index("gy"), 2)
    halo_ref[1 - odd] = first_ref[...]
    halo_ref[odd] = second_ref[...]
    here = lax.axis_index("gy")
    keep_low = jnp.where(here == 0, 0.0, 1.0)
    keep_high = jnp.where(here == lax.axis_size("gy") - 1, 0.0, 1.0)
    halo_ref[0, MASK] = halo_ref[0, MASK] * keep_low
    halo_ref[1, MASK] = halo_ref[1, MASK] * keep_high
    return keep_low, keep_high


def plane_stores(n, x, new_v, out_v, newf_ref, newg_ref, outf_ref, outg_ref, sem):
    pairs = (
        (new_v.at[pl.ds(0, NF), n], newf_ref.at[:, x]),
        (new_v.at[pl.ds(NF, NG), n], newg_ref.at[:, x]),
        (out_v.at[pl.ds(0, NF), n], outf_ref.at[:, x]),
        (out_v.at[pl.ds(NF, NG), n], outg_ref.at[:, x]),
    )
    return [pltpu.make_async_copy(a, b, sem.at[k, n]) for k, (a, b) in enumerate(pairs)]


def inner_kernel(
    post_ref, adjf_ref, adjg_ref, fluid_ref, bcell_ref, first_ref, second_ref, profile_ref,
    magnet_ref, turned_ref, zfluid_ref,
    newf_ref, newg_ref, outf_ref, outg_ref, sums_ref,
    new_v, out_v, halo_v, near_v, store_sem,
):
    sx = fluid_ref.shape[0]
    count = sums_ref.shape[0]

    def stores(x):
        return plane_stores(
            x, x, new_v, out_v, newf_ref, newg_ref, outf_ref, outg_ref, store_sem
        )

    sums_ref[...] = jnp.zeros_like(sums_ref)
    load_halo(first_ref, second_ref, halo_v)

    def body(x, carry):
        def row_of(slot, dx, dy):
            return halo_v[0 if dy == -1 else 1, slot, pl.ds(x + dx, 1), :]

        plane_step(
            x,
            lambda i, dx: post_ref[i, x + dx],
            lambda i, dx, dy: row_of(halo_slot(0, i, dy), dx, dy),
            lambda i, dx: adj_plane(adjf_ref, adjg_ref, i, x + dx),
            lambda i, dx, dy: row_of(halo_slot(1, i, dy), dx, dy),
            lambda dx: fluid_ref[x + dx],
            lambda dx, dy: row_of(MASK, dx, dy),
            fluid_ref[x],
            bcell_ref[x],
            profile_ref[x],
            magnet_ref[x],
            near_v,
            new_v,
            out_v,
            sums_ref,
            count,
            lambda kind, i, dx: turned_ref[len(TURNED) * kind + TURNED.index(i), x + dx],
            lambda dx, dz: zfluid_ref[0 if dz == -1 else 1, x + dx],
        )
        start_all(stores(x))
        return carry

    lax.fori_loop(1, sx - 1, body, 0)
    for x in range(1, sx - 1):
        wait_all(stores(x))


def inner_call(post, adjf, adjg, fluid, bcell, first, second, profile, magnet, turned, zfluid, count):
    sx, sy, sz = profile.shape
    full = pltpu.VMEM((NP, sx, sy, sz), jnp.float32)
    flow = jax.ShapeDtypeStruct((NF, sx, sy, sz), jnp.float32)
    field = jax.ShapeDtypeStruct((NG, sx, sy, sz), jnp.float32)
    return pl.pallas_call(
        inner_kernel,
        in_specs=[VMEM] * 11,
        out_specs=[ANY, ANY, ANY, ANY, VMEM],
        out_shape=[flow, field, flow, field, pltpu.VMEM((count, 8, 128), jnp.float32)],
        scratch_shapes=[
            full,
            full,
            pltpu.VMEM((2, SLOTS, sx, sz), jnp.float32),
            pltpu.VMEM((18, sy, sz), jnp.float32),
            pltpu.SemaphoreType.DMA((4, sx)),
        ],
        compiler_params=pltpu.CompilerParams(vmem_limit_bytes=INNER_VMEM),
        cost_estimate=pl.CostEstimate(
            flops=700 * sx * sy * sz, bytes_accessed=16 * NP * sx * sy * sz, transcendentals=0
        ),
        name="inner",
    )(post, adjf, adjg, fluid, bcell, first, second, profile, magnet, turned, zfluid)


def outer_kernel(
    scale, second_ref, fromleft_ref, fromright_ref, first_ref, post_ref, adjf_ref, adjg_ref,
    fluid_ref, bcell_ref,
    cornerleft_ref, cornerright_ref, profile_ref, magnet_ref, turned_ref, zfluid_ref,
    partial_ref, newf_in, newg_in, outf_in, outg_in,
    newf_ref, newg_ref, outf_ref, outg_ref, share_ref,
    new_v, out_v, halo_v, near_v, sums_v, store_sem,
):
    del newf_in, newg_in, outf_in, outg_in
    sx = fluid_ref.shape[0]
    count = sums_v.shape[0]
    sums_v[...] = partial_ref[...]
    keep_low, keep_high = load_halo(first_ref, second_ref, halo_v)
    stores = []
    for n, (x, away) in enumerate(((0, -1), (sx - 1, 1))):
        face_ref, corner_ref = (
            (fromleft_ref, cornerleft_ref) if away == -1 else (fromright_ref, cornerright_ref)
        )

        def get(kind, i, dx, x=x, away=away, face_ref=face_ref):
            if dx == away:
                return face_ref[face_slot(kind, i, dx)]
            if kind == 1:
                return adj_plane(adjf_ref, adjg_ref, i, x + dx)
            return post_ref[i, x + dx]

        def row(kind, i, dx, dy, x=x, away=away, corner_ref=corner_ref):
            side = 0 if dy == -1 else 1
            if dx == away:
                line = corner_ref[2 * kind + side : 2 * kind + side + 1, :]
                if kind == 2:
                    line = line * (keep_low if side == 0 else keep_high)
                return line
            slot = MASK if kind == 2 else halo_slot(kind, i, dy)
            return halo_v[side, slot, x + dx : x + dx + 1, :]

        def mask(dx, x=x, away=away, face_ref=face_ref):
            return face_ref[MASK] if dx == away else fluid_ref[x + dx]

        plane_step(
            n,
            lambda i, dx, get=get: get(0, i, dx),
            lambda i, dx, dy, row=row: row(0, i, dx, dy),
            lambda i, dx, get=get: get(1, i, dx),
            lambda i, dx, dy, row=row: row(1, i, dx, dy),
            mask,
            lambda dx, dy, row=row: row(2, 0, dx, dy),
            fluid_ref[x],
            bcell_ref[x],
            profile_ref[x],
            magnet_ref[x],
            near_v,
            new_v,
            out_v,
            sums_v,
            count,
            lambda kind, i, dx, x=x, away=away: (
                None if dx == away else turned_ref[len(TURNED) * kind + TURNED.index(i), x + dx]
            ),
            lambda dx, dz, x=x, away=away: (
                None if dx == away else zfluid_ref[0 if dz == -1 else 1, x + dx]
            ),
        )
        these = plane_stores(
            n, x, new_v, out_v, newf_ref, newg_ref, outf_ref, outg_ref, store_sem
        )
        start_all(these)
        stores += these
    rows = jnp.concatenate(
        [jnp.sum(sums_v[m], axis=0, keepdims=True) for m in range(count)], axis=0
    )
    share_ref[...] = lax.dot_general(
        jnp.ones((share_ref.shape[0], 128), jnp.float32),
        rows * scale,
        (((1,), (1,)), ((), ())),
        precision=lax.Precision.HIGHEST,
        preferred_element_type=jnp.float32,
    )
    wait_all(stores)


def outer_call(
    post, adjf, adjg, fluid, bcell, first, second, fromleft, fromright, cornerleft, cornerright,
    profile, magnet, turned, zfluid, partial, newf, newg, outf, outg, scale,
):
    sx, sy, sz = profile.shape
    count = partial.shape[0]
    flow = jax.ShapeDtypeStruct(newf.shape, jnp.float32)
    field = jax.ShapeDtypeStruct(newg.shape, jnp.float32)
    return pl.pallas_call(
        functools.partial(outer_kernel, scale),
        in_specs=[VMEM] * 16 + [ANY] * 4,
        out_specs=[ANY] * 4 + [VMEM],
        out_shape=[
            flow,
            field,
            flow,
            field,
            jax.ShapeDtypeStruct((lax.axis_size(("gx", "gy")), count), jnp.float32),
        ],
        input_output_aliases={16: 0, 17: 1, 18: 2, 19: 3},
        scratch_shapes=[
            pltpu.VMEM((NP, 2, sy, sz), jnp.float32),
            pltpu.VMEM((NP, 2, sy, sz), jnp.float32),
            pltpu.VMEM((2, SLOTS, sx, sz), jnp.float32),
            pltpu.VMEM((18, sy, sz), jnp.float32),
            pltpu.VMEM((count, 8, 128), jnp.float32),
            pltpu.SemaphoreType.DMA((4, 2)),
        ],
        compiler_params=pltpu.CompilerParams(vmem_limit_bytes=OUTER_VMEM),
        name="outer",
    )(
        second, fromleft, fromright, first, post, adjf, adjg, fluid, bcell, cornerleft,
        cornerright, profile, magnet, turned, zfluid, partial, newf, newg, outf, outg,
    )


def ring(count, step):
    return [(i, (i + step) % count) for i in range(count)]


def on_device(flow, field, adj_flow_in, adj_field_in, profile, strengths, wall, magnet):
    across, around = lax.axis_size("gy"), lax.axis_size("gx")
    count = strengths.shape[0]
    table = strengths.reshape(1, count)
    arrays = (flow, field, adj_flow_in, adj_field_in, profile, table, wall, magnet)
    mine1, mine2, right, left = rim_call(*arrays)
    inside = [(i, i ^ 1) for i in range(across)]
    between = [(i, (((i + 1) ^ 1) - 1) % across) for i in range(across)]
    second = lax.ppermute(mine2, "gy", between)
    first = lax.ppermute(mine1, "gy", inside)
    fromleft = lax.ppermute(right, "gx", ring(around, 1))
    fromright = lax.ppermute(left, "gx", ring(around, -1))
    post, fluid, bcell, turned, zfluid = collide_call(
        flow, field, profile, table, wall, magnet, adj_flow_in, adj_field_in
    )
    corner_r, corner_l = corner_call(first, second, bcell)
    cornerleft = lax.ppermute(corner_r, "gx", ring(around, 1))
    cornerright = lax.ppermute(corner_l, "gx", ring(around, -1))
    newf, newg, outf, outg, partial = inner_call(
        post, adj_flow_in, adj_field_in, fluid, bcell, first, second, profile, magnet, turned,
        zfluid, count,
    )
    cells = flow.shape[1] * around * flow.shape[2] * across * flow.shape[3]
    newf, newg, outf, outg, share = outer_call(
        post, adj_flow_in, adj_field_in, fluid, bcell, first, second, fromleft, fromright, cornerleft, cornerright,
        profile, magnet, turned, zfluid, partial, newf, newg, outf, outg, 1.0 / math.sqrt(cells / count),
    )
    totals = jnp.sum(lax.all_to_all(share, ("gx", "gy"), 0, 0, tiled=True), axis=0)
    return (newf, newg, outf, outg, totals)


def solution(mesh):
    stack = P(None, "gx", "gy", None)
    cell = P("gx", "gy", None)
    return jax.shard_map(
        on_device,
        mesh=mesh,
        in_specs=(stack, stack, stack, stack, cell, P(), cell, cell),
        out_specs=(stack, stack, stack, stack, P()),
        check_vma=False,
    )
```

```python
import functools
import math

import jax
import jax.numpy as jnp
from jax import lax
from jax.experimental import pallas as pl
from jax.experimental.pallas import tpu as pltpu
from jax.sharding import PartitionSpec as P

LATTICE = [
    (0, 0, 0),
    (1, 0, 0),
    (-1, 0, 0),
    (0, 1, 0),
    (0, -1, 0),
    (0, 0, 1),
    (0, 0, -1),
    (1, 1, 0),
    (-1, -1, 0),
    (1, -1, 0),
    (-1, 1, 0),
    (1, 0, 1),
    (-1, 0, -1),
    (1, 0, -1),
    (-1, 0, 1),
    (0, 1, 1),
    (0, -1, -1),
    (0, 1, -1),
    (0, -1, 1),
]
NF, NG = 19, 7
NP = NF + NG
FIRST = [1, 3, 5, 7, 9, 11, 13, 15, 17]
W0, W1, W2 = 1.0 / 3.0, 1.0 / 18.0, 1.0 / 36.0
V0, V1 = 0.25, 0.125
PLUS = 0.625
MINUS = 0.5 / 1.125
TAU_PLUS = 0.8
COUPLE = 2.0
SOURCE = 2.0

UP = [3, 7, 10, 15, 17, NF + 3]
DOWN = [4, 8, 9, 16, 18, NF + 4]
RIGHT = [1, 7, 9, 11, 13, NF + 1]
LEFT = [2, 8, 10, 12, 14, NF + 2]
SLOTS = 13
MASK = 12

RIM_VMEM = 63 << 20
COLLIDE_VMEM = 54 << 20
INNER_VMEM = 12 << 20
OUTER_VMEM = 8 << 20


def weight(i):
    return W1 if i <= 6 else W2


def gather_strength(table, magnet):
    parts = [
        jnp.take_along_axis(table, magnet[:, z : z + 128], axis=1, mode="promise_in_bounds")
        for z in range(0, magnet.shape[1], 128)
    ]
    return jnp.concatenate(parts, axis=1)


def lane_table(strengths_v):
    row = strengths_v[...]
    rest = 128 - row.shape[1]
    if rest:
        row = jnp.concatenate([row, jnp.zeros((1, rest), jnp.float32)], axis=1)
    return jnp.broadcast_to(row, (8, 128))


def vector_sums(pair):
    x = pair[1] + pair[7] + pair[9] + pair[11] + pair[13]
    y = pair[3] + pair[7] - pair[9] + pair[15] + pair[17]
    z = pair[5] + pair[11] - pair[13] + pair[15] - pair[17]
    return x, y, z


def along(i, vx, vy, vz):
    out = None
    for c, v in zip(LATTICE[i], (vx, vy, vz)):
        if c:
            if out is None:
                out = v if c > 0 else -v
            else:
                out = out + v if c > 0 else out - v
    return out


def start_all(copies):
    for c in copies:
        c.start()


def wait_all(copies):
    for c in copies:
        c.wait()


def collide(f, g, fluid, bcell, wanted):
    even = {i: f[i] + f[i + 1] for i in FIRST}
    diff = {i: f[i] - f[i + 1] for i in FIRST}
    rho = f[0] + (1.0 - fluid)
    for i in FIRST:
        rho = rho + even[i]
    momx, momy, momz = vector_sums(diff)
    inv = 1.0 / rho
    ux, uy, uz = momx * inv, momy * inv, momz * inv
    bval = g[0] + g[1] + g[2] + g[3] + g[4] + g[5] + g[6]
    current = (g[3] - g[4]) - bval * uy
    shear = (even[7] - even[9]) - momx * uy
    force = (COUPLE * bcell) * current
    vx = ux + TAU_PLUS * force * inv
    base = 1.0 - 1.5 * (vx * vx + uy * uy + uz * uz)
    post = {}
    if 0 in wanted:
        post[0] = f[0] - 2.0 * PLUS * (f[0] - (W0 * rho) * base)
    rho1, rho2 = W1 * rho, W2 * rho
    for i in FIRST:
        if i not in wanted and i + 1 not in wanted:
            continue
        wr = rho1 if i <= 6 else rho2
        a = along(i, vx, uy, uz)
        ne = PLUS * (even[i] - (2.0 * wr) * (base + 4.5 * a * a))
        no = MINUS * (diff[i] - (6.0 * wr) * a)
        if i in wanted:
            post[i] = f[i] - ne - no
        if i + 1 in wanted:
            post[i + 1] = f[i + 1] - ne + no
    common = bval + (SOURCE * bcell) * shear
    slope = 4.0 * bval
    if NF in wanted:
        post[NF] = V0 * common
    for k, u in ((1, ux), (3, uy), (5, uz)):
        if NF + k in wanted:
            post[NF + k] = V1 * (common + slope * u)
        if NF + k + 1 in wanted:
            post[NF + k + 1] = V1 * (common - slope * u)
    return post


def rim_kernel(
    flow_ref, field_ref, adjf_ref, adjg_ref, profile_ref, strengths_ref, wall_ref, magnet_ref,
    first_ref, second_ref, right_ref, left_ref,
    rows_v, faces_v, profile_v, wall_v, magnet_v, strengths_v, message_v, cell_sem, rows_sem,
    faces_sem, adj_sem,
):
    sx, sy = profile_v.shape[:2]
    odd = lax.rem(lax.axis_index("gy"), 2)
    ends = (sy - 1, 0)
    sides = (0, sx - 1)

    def adj_at(i, where):
        return adjf_ref.at[(i, *where)] if i < NF else adjg_ref.at[(i - NF, *where)]

    rows = []
    for n, y in enumerate(ends):
        rows += [
            pltpu.make_async_copy(
                flow_ref.at[:, :, y], rows_v.at[n, pl.ds(0, NF)], rows_sem.at[n, 0]
            ),
            pltpu.make_async_copy(
                field_ref.at[:, :, y], rows_v.at[n, pl.ds(NF, NG)], rows_sem.at[n, 1]
            ),
        ]
    cells = [
        pltpu.make_async_copy(a, b, cell_sem.at[n])
        for n, (a, b) in enumerate(
            (
                (wall_ref, wall_v),
                (magnet_ref, magnet_v),
                (strengths_ref, strengths_v),
                (profile_ref, profile_v),
            )
        )
    ]
    faces = []
    for n, x in enumerate(sides):
        faces += [
            pltpu.make_async_copy(
                flow_ref.at[:, x], faces_v.at[n, pl.ds(0, NF)], faces_sem.at[n, 0]
            ),
            pltpu.make_async_copy(
                field_ref.at[:, x], faces_v.at[n, pl.ds(NF, NG)], faces_sem.at[n, 1]
            ),
        ]
    adjs = []
    for s in range(6):
        for n, (i, where, out) in enumerate(
            (
                (DOWN[s], (slice(None), ends[0]), message_v.at[0]),
                (UP[s], (slice(None), ends[1]), message_v.at[1]),
                (RIGHT[s], (sides[0],), left_ref),
                (LEFT[s], (sides[1],), right_ref),
            )
        ):
            adjs.append(pltpu.make_async_copy(adj_at(i, where), out.at[6 + s], adj_sem.at[n, s]))
    start_all(rows[:2])
    start_all(cells)
    start_all(rows[2:])
    start_all(faces)
    start_all(adjs)
    wait_all(cells)
    table = lane_table(strengths_v)
    for n, (y, wanted) in enumerate(zip(ends, (UP, DOWN))):
        wait_all(rows[2 * n : 2 * n + 2])
        fluid = 1.0 - wall_v[:, y, :].astype(jnp.float32)
        bcell = gather_strength(table, magnet_v[:, y, :]) * profile_v[:, y, :]
        post = collide(
            [rows_v[n, i] for i in range(NF)],
            [rows_v[n, NF + k] for k in range(NG)],
            fluid,
            bcell,
            wanted,
        )
        for s in range(6):
            message_v[n, s] = post[wanted[s]]
        message_v[n, MASK] = fluid
    for n, (x, wanted, out) in enumerate(
        ((sides[0], LEFT, left_ref), (sides[1], RIGHT, right_ref))
    ):
        wait_all(faces[2 * n : 2 * n + 2])
        fluid = 1.0 - wall_v[x].astype(jnp.float32)
        bcell = gather_strength(table, magnet_v[x]) * profile_v[x]
        post = collide(
            [faces_v[n, i] for i in range(NF)],
            [faces_v[n, NF + k] for k in range(NG)],
            fluid,
            bcell,
            wanted,
        )
        for s in range(6):
            out[s] = post[wanted[s]]
        out[MASK] = fluid
    wait_all(adjs)
    first_ref[...] = message_v[odd]
    second_ref[...] = message_v[1 - odd]


ANY = pl.BlockSpec(memory_space=pl.ANY)
VMEM = pl.BlockSpec(memory_space=pltpu.VMEM)


def rim_call(flow, field, adjf, adjg, profile, strengths, wall, magnet):
    sx, sy, sz = profile.shape
    cells = pltpu.VMEM((sx, sy, sz), jnp.float32)
    names = pltpu.VMEM((sx, sy, sz), jnp.int32)
    rows = pltpu.VMEM((SLOTS, sx, sz), jnp.float32)
    faces = pltpu.VMEM((SLOTS, sy, sz), jnp.float32)
    dma = pltpu.SemaphoreType.DMA
    return pl.pallas_call(
        rim_kernel,
        in_specs=[ANY] * 8,
        out_specs=[VMEM] * 4,
        out_shape=[rows, rows, faces, faces],
        scratch_shapes=[
            pltpu.VMEM((2, NP, sx, sz), jnp.float32),
            pltpu.VMEM((2, NP, sy, sz), jnp.float32),
            cells,
            names,
            names,
            pltpu.VMEM(strengths.shape, jnp.float32),
            pltpu.VMEM((2, SLOTS, sx, sz), jnp.float32),
            dma((4,)),
            dma((2, 2)),
            dma((2, 2)),
            dma((4, 6)),
        ],
        compiler_params=pltpu.CompilerParams(vmem_limit_bytes=RIM_VMEM),
        name="rims",
    )(flow, field, adjf, adjg, profile, strengths, wall, magnet)


def collide_kernel(
    flow_ref, field_ref, profile_ref, strengths_ref, wall_ref, magnet_ref,
    post_ref, fluid_ref, bcell_ref, profile_v, magnet_v,
    flow_v, field_v, wall_v, strengths_v, plane_sem, table_sem,
):
    sx = fluid_ref.shape[0]

    def loads(x):
        pairs = (
            (wall_ref.at[x], wall_v.at[x]),
            (magnet_ref.at[x], magnet_v.at[x]),
            (profile_ref.at[x], profile_v.at[x]),
            (flow_ref.at[:, x], flow_v.at[:, x]),
            (field_ref.at[:, x], field_v.at[:, x]),
        )
        return [pltpu.make_async_copy(a, b, plane_sem.at[n, x]) for n, (a, b) in enumerate(pairs)]

    table_load = pltpu.make_async_copy(strengths_ref, strengths_v, table_sem.at[0])
    table_load.start()
    for x in range(sx):
        start_all(loads(x))
    table_load.wait()
    table = lane_table(strengths_v)

    def body(x, carry):
        wait_all(loads(x))
        fluid = 1.0 - wall_v[x].astype(jnp.float32)
        bcell = gather_strength(table, magnet_v[x]) * profile_v[x]
        fluid_ref[x] = fluid
        bcell_ref[x] = bcell
        f = [flow_v[i, x] for i in range(NF)]
        g = [field_v[k, x] for k in range(NG)]
        for i, value in collide(f, g, fluid, bcell, range(NP)).items():
            post_ref[i, x] = value
        return carry

    lax.fori_loop(0, sx, body, 0)


def collide_call(flow, field, profile, strengths, wall, magnet):
    sx, sy, sz = profile.shape
    cells = pltpu.VMEM((sx, sy, sz), jnp.float32)
    names = pltpu.VMEM((sx, sy, sz), jnp.int32)
    return pl.pallas_call(
        collide_kernel,
        in_specs=[ANY] * 6,
        out_specs=[VMEM] * 5,
        out_shape=[
            pltpu.VMEM((NP, sx, sy, sz), jnp.float32),
            cells,
            cells,
            cells,
            names,
        ],
        scratch_shapes=[
            pltpu.VMEM(flow.shape, jnp.float32),
            pltpu.VMEM(field.shape, jnp.float32),
            names,
            pltpu.VMEM(strengths.shape, jnp.float32),
            pltpu.SemaphoreType.DMA((5, sx)),
            pltpu.SemaphoreType.DMA((1,)),
        ],
        compiler_params=pltpu.CompilerParams(vmem_limit_bytes=COLLIDE_VMEM),
        cost_estimate=pl.CostEstimate(
            flops=300 * sx * sy * sz, bytes_accessed=12 * NP * sx * sy * sz, transcendentals=0
        ),
        name="collide",
    )(flow, field, profile, strengths, wall, magnet)


CORNER_RIGHT = ((0, 7, 0, 8), (1, 9, 1, 10))
CORNER_LEFT = ((0, 10, 0, 9), (1, 8, 1, 7))


def corner_slots(side, post, adj):
    posts, adjs = (UP, DOWN) if side == 0 else (DOWN, UP)
    return posts.index(post), 6 + adjs.index(adj), MASK


def corner_kernel(first_ref, second_ref, after_ref, right_ref, left_ref):
    del after_ref
    odd = lax.rem(lax.axis_index("gy"), 2) == 1
    sx = first_ref.shape[1]

    def row(side, slot, x):
        a, b = first_ref[slot, x : x + 1, :], second_ref[slot, x : x + 1, :]
        return jnp.where(odd, a, b) if side == 0 else jnp.where(odd, b, a)

    for out, table, x in ((right_ref, CORNER_RIGHT, sx - 1), (left_ref, CORNER_LEFT, 0)):
        out[...] = jnp.zeros_like(out)
        for side, post, _, adj in table:
            for n, slot in enumerate(corner_slots(side, post, adj)):
                out[2 * n + side : 2 * n + side + 1, :] = row(side, slot, x)


def corner_call(first, second, after):
    sz = first.shape[2]
    out = pltpu.VMEM((8, sz), jnp.float32)
    return pl.pallas_call(
        corner_kernel,
        in_specs=[VMEM, VMEM, ANY],
        out_specs=[VMEM, VMEM],
        out_shape=[out, out],
        compiler_params=pltpu.CompilerParams(vmem_limit_bytes=2 << 20),
        name="corners",
    )(first, second, after)


def plane_step(
    x_index, post, post_row, adj, adj_row, mask, mask_row, fluid, bcell, profile, magnet,
    near_ref, new_ref, out_ref, sums_ref, count, new_done, out_done,
):
    sy, sz = fluid.shape
    yi = lax.broadcasted_iota(jnp.int32, (sy, sz), 0)
    zi = lax.broadcasted_iota(jnp.int32, (sy, sz), 1)
    top, bottom = yi == sy - 1, yi == 0
    zlast, zfirst = zi == sz - 1, zi == 0

    def shift(value, row, dy, dz):
        if dy == -1:
            value = jnp.where(bottom, row(), pltpu.roll(value, 1, 0))
        elif dy == 1:
            value = jnp.where(top, row(), pltpu.roll(value, sy - 1, 0))
        if dz == -1:
            value = pltpu.roll(value, 1, 1)
        elif dz == 1:
            value = pltpu.roll(value, sz - 1, 1)
        return value

    def moved(get, get_row, i, sign):
        dx, dy, dz = (sign * c for c in LATTICE[i if i < NF else i - NF])
        return shift(get(i, dx), lambda: get_row(i, dx, dy), dy, dz)

    def near_of(i, sign):
        dx, dy, dz = (sign * c for c in LATTICE[i])
        value = shift(mask(dx), lambda: mask_row(dx, dy), dy, dz)
        if dz == -1:
            value = jnp.where(zfirst, 0.0, value)
        elif dz == 1:
            value = jnp.where(zlast, 0.0, value)
        return value

    for n, i in enumerate(FIRST):
        near_ref[2 * n] = near_of(i, -1)
        near_ref[2 * n + 1] = near_of(i, 1)

    def near(n):
        return near_ref[2 * n] > 0.5, near_ref[2 * n + 1] > 0.5

    def pull(i, n):
        minus, plus = near(n)
        a = fluid * jnp.where(minus, moved(post, post_row, i, -1), post(i + 1, 0))
        b = fluid * jnp.where(plus, moved(post, post_row, i + 1, -1), post(i, 0))
        new_ref[i, x_index] = a
        new_ref[i + 1, x_index] = b
        return a, b

    f0 = fluid * post(0, 0)
    new_ref[0, x_index] = f0
    rho = f0 + (1.0 - fluid)
    momx = momy = momz = shear0 = 0.0
    for n, i in enumerate(FIRST):
        a, b = pull(i, n)
        s, d = a + b, a - b
        rho = rho + s
        cx, cy, cz = LATTICE[i]
        if cx:
            momx = momx + d
        if cy:
            momy = momy + d if cy > 0 else momy - d
        if cz:
            momz = momz + d if cz > 0 else momz - d
        if cx and cy:
            shear0 = shear0 + s if cx * cy > 0 else shear0 - s
    g0 = fluid * post(NF, 0)
    new_ref[NF, x_index] = g0
    bval = g0
    gy = None
    for n, k in enumerate((1, 3, 5)):
        a, b = pull(NF + k, n)
        bval = bval + (a + b)
        if k == 3:
            gy = a - b
    new_done()
    inv = 1.0 / rho
    ux, uy, uz = momx * inv, momy * inv, momz * inv
    current = gy - bval * uy
    shear = shear0 - momx * uy
    force = (COUPLE * bcell) * current
    vx = ux + TAU_PLUS * force * inv

    def push(i, n):
        minus, plus = near(n)
        a = fluid * jnp.where(plus, moved(adj, adj_row, i, 1), adj(i + 1, 0))
        b = fluid * jnp.where(minus, moved(adj, adj_row, i + 1, 1), adj(i, 0))
        return a, b

    l0 = fluid * adj(0, 0)
    out_ref[0, x_index] = (1.0 - 2.0 * PLUS) * l0
    total = (2.0 * PLUS * W0) * l0
    m1 = [0.0, 0.0, 0.0]
    m2 = {}
    for n, i in enumerate(FIRST):
        a, b = push(i, n)
        s, d = a + b, a - b
        de = (0.5 - PLUS) * s
        do = (0.5 - MINUS) * d
        out_ref[i, x_index] = de + do
        out_ref[i + 1, x_index] = de - do
        w = weight(i)
        s = (2.0 * PLUS * w) * s
        d = (2.0 * MINUS * w) * d
        total = total + s
        c = LATTICE[i]
        for axis in range(3):
            if c[axis]:
                m1[axis] = m1[axis] + d if c[axis] > 0 else m1[axis] - d
            for other in range(axis, 3):
                sign = c[axis] * c[other]
                if sign:
                    old = m2.get((axis, other))
                    if old is None:
                        m2[axis, other] = s if sign > 0 else -s
                    else:
                        m2[axis, other] = old + s if sign > 0 else old - s
    h0 = fluid * adj(NF, 0)
    hsum = V0 * h0
    h1 = []
    hs = None
    for n, k in enumerate((1, 3, 5)):
        a, b = push(NF + k, n)
        hs = a + b if hs is None else hs + (a + b)
        h1.append(V1 * (a - b))
    hsum = hsum + V1 * hs

    base = 1.0 - 1.5 * (vx * vx + uy * uy + uz * uz)
    tx = m2[0, 0] * vx + m2[0, 1] * uy + m2[0, 2] * uz
    ty = m2[0, 1] * vx + m2[1, 1] * uy + m2[1, 2] * uz
    tz = m2[0, 2] * vx + m2[1, 2] * uy + m2[2, 2] * uz
    rhobar = (
        total * base
        + 4.5 * (vx * tx + uy * ty + uz * tz)
        + 3.0 * (m1[0] * vx + m1[1] * uy + m1[2] * uz)
    )
    total3 = 3.0 * total
    vxbar = rho * (9.0 * tx + 3.0 * m1[0] - total3 * vx)
    uybar = rho * (9.0 * ty + 3.0 * m1[1] - total3 * uy)
    uzbar = rho * (9.0 * tz + 3.0 * m1[2] - total3 * uz)
    slope = 4.0 * bval
    forcebar = (TAU_PLUS * vxbar) * inv
    rhobar = rhobar - forcebar * force * inv
    currentbar = (COUPLE * bcell) * forcebar
    shearbar = (SOURCE * bcell) * hsum
    dcell = COUPLE * current * forcebar + SOURCE * shear * hsum
    uxbar = vxbar + slope * h1[0]
    uybar = uybar + slope * h1[1] - bval * currentbar - momx * shearbar
    uzbar = uzbar + slope * h1[2]
    bbar = hsum + 4.0 * (h1[0] * ux + h1[1] * uy + h1[2] * uz) - uy * currentbar
    mxbar = uxbar * inv - uy * shearbar
    mybar = uybar * inv
    mzbar = uzbar * inv
    rhobar = rhobar - (ux * uxbar + uy * uybar + uz * uzbar) * inv

    out_ref[0, x_index] = out_ref[0, x_index] + rhobar
    for i in FIRST:
        cm = along(i, mxbar, mybar, mzbar)
        cx, cy, _ = LATTICE[i]
        common = rhobar
        if cx and cy:
            common = rhobar + shearbar if cx * cy > 0 else rhobar - shearbar
        out_ref[i, x_index] = out_ref[i, x_index] + (common + cm)
        out_ref[i + 1, x_index] = out_ref[i + 1, x_index] + (common - cm)
    for k in range(NG):
        value = bbar
        if k == 3:
            value = bbar + currentbar
        elif k == 4:
            value = bbar - currentbar
        out_ref[NF + k, x_index] = value

    out_done()

    share = dcell * profile
    for m in range(count):
        hit = jnp.where(magnet == m, share, 0.0)
        part = hit[:, 0:128]
        for z in range(128, sz, 128):
            part = part + hit[:, z : z + 128]
        sums_ref[m] = sums_ref[m] + part


def halo_slot(kind, i, dy):
    names = (UP, DOWN) if (dy == -1) == (kind == 0) else (DOWN, UP)
    return names[0].index(i) + 6 * kind


def face_slot(kind, i, dx):
    names = RIGHT if (dx == -1) == (kind == 0) else LEFT
    return names.index(i) + 6 * kind


def adj_plane(adjf_ref, adjg_ref, i, x):
    return adjf_ref[i, x] if i < NF else adjg_ref[i - NF, x]


def load_halo(first_ref, second_ref, halo_ref):
    odd = lax.rem(lax.axis_index("gy"), 2)
    halo_ref[1 - odd] = first_ref[...]
    halo_ref[odd] = second_ref[...]
    here = lax.axis_index("gy")
    keep_low = jnp.where(here == 0, 0.0, 1.0)
    keep_high = jnp.where(here == lax.axis_size("gy") - 1, 0.0, 1.0)
    halo_ref[0, MASK] = halo_ref[0, MASK] * keep_low
    halo_ref[1, MASK] = halo_ref[1, MASK] * keep_high
    return keep_low, keep_high


def plane_stores(n, x, new_v, out_v, newf_ref, newg_ref, outf_ref, outg_ref, sem):
    pairs = (
        (new_v.at[pl.ds(0, NF), n], newf_ref.at[:, x]),
        (new_v.at[pl.ds(NF, NG), n], newg_ref.at[:, x]),
        (out_v.at[pl.ds(0, NF), n], outf_ref.at[:, x]),
        (out_v.at[pl.ds(NF, NG), n], outg_ref.at[:, x]),
    )
    return [pltpu.make_async_copy(a, b, sem.at[k, n]) for k, (a, b) in enumerate(pairs)]


def inner_kernel(
    post_ref, adjf_ref, adjg_ref, fluid_ref, bcell_ref, first_ref, second_ref, profile_ref,
    magnet_ref,
    newf_ref, newg_ref, outf_ref, outg_ref, sums_ref,
    new_v, out_v, halo_v, near_v, store_sem,
):
    sx = fluid_ref.shape[0]
    count = sums_ref.shape[0]

    def stores(x):
        return plane_stores(
            x, x, new_v, out_v, newf_ref, newg_ref, outf_ref, outg_ref, store_sem
        )

    sums_ref[...] = jnp.zeros_like(sums_ref)
    load_halo(first_ref, second_ref, halo_v)

    def body(x, carry):
        def row_of(slot, dx, dy):
            return halo_v[0 if dy == -1 else 1, slot, pl.ds(x + dx, 1), :]

        plane_step(
            x,
            lambda i, dx: post_ref[i, x + dx],
            lambda i, dx, dy: row_of(halo_slot(0, i, dy), dx, dy),
            lambda i, dx: adj_plane(adjf_ref, adjg_ref, i, x + dx),
            lambda i, dx, dy: row_of(halo_slot(1, i, dy), dx, dy),
            lambda dx: fluid_ref[x + dx],
            lambda dx, dy: row_of(MASK, dx, dy),
            fluid_ref[x],
            bcell_ref[x],
            profile_ref[x],
            magnet_ref[x],
            near_v,
            new_v,
            out_v,
            sums_ref,
            count,
            lambda: start_all(stores(x)[:2]),
            lambda: start_all(stores(x)[2:]),
        )
        return carry

    lax.fori_loop(1, sx - 1, body, 0)
    for x in range(1, sx - 1):
        wait_all(stores(x))


def inner_call(post, adjf, adjg, fluid, bcell, first, second, profile, magnet, count):
    sx, sy, sz = profile.shape
    full = pltpu.VMEM((NP, sx, sy, sz), jnp.float32)
    flow = jax.ShapeDtypeStruct((NF, sx, sy, sz), jnp.float32)
    field = jax.ShapeDtypeStruct((NG, sx, sy, sz), jnp.float32)
    return pl.pallas_call(
        inner_kernel,
        in_specs=[VMEM] * 9,
        out_specs=[ANY, ANY, ANY, ANY, VMEM],
        out_shape=[flow, field, flow, field, pltpu.VMEM((count, 8, 128), jnp.float32)],
        scratch_shapes=[
            full,
            full,
            pltpu.VMEM((2, SLOTS, sx, sz), jnp.float32),
            pltpu.VMEM((18, sy, sz), jnp.float32),
            pltpu.SemaphoreType.DMA((4, sx)),
        ],
        compiler_params=pltpu.CompilerParams(vmem_limit_bytes=INNER_VMEM),
        cost_estimate=pl.CostEstimate(
            flops=700 * sx * sy * sz, bytes_accessed=16 * NP * sx * sy * sz, transcendentals=0
        ),
        name="inner",
    )(post, adjf, adjg, fluid, bcell, first, second, profile, magnet)


def outer_kernel(
    scale, second_ref, fromleft_ref, fromright_ref, first_ref, post_ref, adjf_ref, adjg_ref,
    fluid_ref, bcell_ref,
    cornerleft_ref, cornerright_ref, profile_ref, magnet_ref,
    partial_ref, newf_in, newg_in, outf_in, outg_in,
    newf_ref, newg_ref, outf_ref, outg_ref, share_ref,
    new_v, out_v, halo_v, near_v, sums_v, store_sem,
):
    del newf_in, newg_in, outf_in, outg_in
    sx = fluid_ref.shape[0]
    count = sums_v.shape[0]
    sums_v[...] = partial_ref[...]
    keep_low, keep_high = load_halo(first_ref, second_ref, halo_v)
    stores = []
    for n, (x, away) in enumerate(((0, -1), (sx - 1, 1))):
        these = plane_stores(
            n, x, new_v, out_v, newf_ref, newg_ref, outf_ref, outg_ref, store_sem
        )
        stores += these
        face_ref, corner_ref = (
            (fromleft_ref, cornerleft_ref) if away == -1 else (fromright_ref, cornerright_ref)
        )

        def get(kind, i, dx, x=x, away=away, face_ref=face_ref):
            if dx == away:
                return face_ref[face_slot(kind, i, dx)]
            if kind == 1:
                return adj_plane(adjf_ref, adjg_ref, i, x + dx)
            return post_ref[i, x + dx]

        def row(kind, i, dx, dy, x=x, away=away, corner_ref=corner_ref):
            side = 0 if dy == -1 else 1
            if dx == away:
                line = corner_ref[2 * kind + side : 2 * kind + side + 1, :]
                if kind == 2:
                    line = line * (keep_low if side == 0 else keep_high)
                return line
            slot = MASK if kind == 2 else halo_slot(kind, i, dy)
            return halo_v[side, slot, x + dx : x + dx + 1, :]

        def mask(dx, x=x, away=away, face_ref=face_ref):
            return face_ref[MASK] if dx == away else fluid_ref[x + dx]

        plane_step(
            n,
            lambda i, dx, get=get: get(0, i, dx),
            lambda i, dx, dy, row=row: row(0, i, dx, dy),
            lambda i, dx, get=get: get(1, i, dx),
            lambda i, dx, dy, row=row: row(1, i, dx, dy),
            mask,
            lambda dx, dy, row=row: row(2, 0, dx, dy),
            fluid_ref[x],
            bcell_ref[x],
            profile_ref[x],
            magnet_ref[x],
            near_v,
            new_v,
            out_v,
            sums_v,
            count,
            lambda these=these: start_all(these[:2]),
            lambda these=these: start_all(these[2:]),
        )
    rows = jnp.concatenate(
        [jnp.sum(sums_v[m], axis=0, keepdims=True) for m in range(count)], axis=0
    )
    share_ref[...] = lax.dot_general(
        jnp.ones((share_ref.shape[0], 128), jnp.float32),
        rows * scale,
        (((1,), (1,)), ((), ())),
        precision=lax.Precision.HIGHEST,
        preferred_element_type=jnp.float32,
    )
    wait_all(stores)


def outer_call(
    post, adjf, adjg, fluid, bcell, first, second, fromleft, fromright, cornerleft, cornerright,
    profile, magnet, partial, newf, newg, outf, outg, scale,
):
    sx, sy, sz = profile.shape
    count = partial.shape[0]
    flow = jax.ShapeDtypeStruct(newf.shape, jnp.float32)
    field = jax.ShapeDtypeStruct(newg.shape, jnp.float32)
    return pl.pallas_call(
        functools.partial(outer_kernel, scale),
        in_specs=[VMEM] * 14 + [ANY] * 4,
        out_specs=[ANY] * 4 + [VMEM],
        out_shape=[
            flow,
            field,
            flow,
            field,
            jax.ShapeDtypeStruct((lax.axis_size(("gx", "gy")), count), jnp.float32),
        ],
        input_output_aliases={14: 0, 15: 1, 16: 2, 17: 3},
        scratch_shapes=[
            pltpu.VMEM((NP, 2, sy, sz), jnp.float32),
            pltpu.VMEM((NP, 2, sy, sz), jnp.float32),
            pltpu.VMEM((2, SLOTS, sx, sz), jnp.float32),
            pltpu.VMEM((18, sy, sz), jnp.float32),
            pltpu.VMEM((count, 8, 128), jnp.float32),
            pltpu.SemaphoreType.DMA((4, 2)),
        ],
        compiler_params=pltpu.CompilerParams(vmem_limit_bytes=OUTER_VMEM),
        name="outer",
    )(
        second, fromleft, fromright, first, post, adjf, adjg, fluid, bcell, cornerleft,
        cornerright, profile, magnet, partial, newf, newg, outf, outg,
    )


def ring(count, step):
    return [(i, (i + step) % count) for i in range(count)]


def on_device(flow, field, adj_flow_in, adj_field_in, profile, strengths, wall, magnet):
    across, around = lax.axis_size("gy"), lax.axis_size("gx")
    count = strengths.shape[0]
    table = strengths.reshape(1, count)
    arrays = (flow, field, adj_flow_in, adj_field_in, profile, table, wall, magnet)
    mine1, mine2, right, left = rim_call(*arrays)
    inside = [(i, i ^ 1) for i in range(across)]
    between = [(i, (((i + 1) ^ 1) - 1) % across) for i in range(across)]
    second = lax.ppermute(mine2, "gy", between)
    first = lax.ppermute(mine1, "gy", inside)
    fromleft = lax.ppermute(right, "gx", ring(around, 1))
    fromright = lax.ppermute(left, "gx", ring(around, -1))
    post, fluid, bcell, profile, magnet = collide_call(flow, field, profile, table, wall, magnet)
    corner_r, corner_l = corner_call(first, second, bcell)
    cornerleft = lax.ppermute(corner_r, "gx", ring(around, 1))
    cornerright = lax.ppermute(corner_l, "gx", ring(around, -1))
    newf, newg, outf, outg, partial = inner_call(
        post, adj_flow_in, adj_field_in, fluid, bcell, first, second, profile, magnet, count
    )
    cells = flow.shape[1] * around * flow.shape[2] * across * flow.shape[3]
    newf, newg, outf, outg, share = outer_call(
        post, adj_flow_in, adj_field_in, fluid, bcell, first, second, fromleft, fromright, cornerleft, cornerright,
        profile, magnet, partial, newf, newg, outf, outg, 1.0 / math.sqrt(cells / count),
    )
    totals = jnp.sum(lax.all_to_all(share, ("gx", "gy"), 0, 0, tiled=True), axis=0)
    return (newf, newg, outf, outg, totals)


def solution(mesh):
    stack = P(None, "gx", "gy", None)
    cell = P("gx", "gy", None)
    return jax.shard_map(
        on_device,
        mesh=mesh,
        in_specs=(stack, stack, stack, stack, cell, P(), cell, cell),
        out_specs=(stack, stack, stack, stack, P()),
        check_vma=False,
    )
```
